128 devices in a mesh: wide: 16 (over z, x), narrow: 8 (over y, core).
Axes of the slice: x: 4, y: 4, z: 4, core: 2. Of those that a mesh axis runs over, the one named last changes fastest.
Arguments:
- inputs: bfloat16 [4, 256, 16384], P(None, 'wide', 'narrow'), may hold values from -600 to 600
- norm_gain: bfloat16 [16384], P('narrow'), may hold values from 0.099609375 to 1.8984375
- w_query: bfloat16 [16384, 8192], P('narrow', 'wide'), may hold values from -0.0234375 to 0.0234375
- w_keyval: bfloat16 [16384, 1024], P('narrow', 'wide'), may hold values from -0.0234375 to 0.0234375
- w_out: bfloat16 [8192, 16384], P('wide', 'narrow'), may hold values from -0.0625 to 0.0625
- key_cache: bfloat16 [256, 4096, 512], P(('wide', 'narrow')), may hold values from -1700 to 1700
- value_cache: bfloat16 [256, 4096, 512], P(('wide', 'narrow')), may hold values from -48 to 48
- lengths: int32 [256], P(('wide', 'narrow')), may hold values from 1024 to 4092, as said below
- positions: int32 [256], P(('wide', 'narrow')), may hold values from 1024 to 8187, as said below
Outputs:
- attended: bfloat16 [4, 256, 16384], P(None, 'wide', 'narrow')
- new_keys: bfloat16 [4, 256, 512], P(None, ('wide', 'narrow'))
- new_values: bfloat16 [4, 256, 512], P(None, ('wide', 'narrow'))
The draws below stay inside these ranges and needn't reach their ends.
Inputs may be any that keep to these rules, and one draw needn't show every extreme that they name: A row's cache holds its first lengths slots. `positions`: a row's later new tokens follow its first one position by position.
All inputs are finite; a program needn't handle non-finite values.
Results may differ from the reference program's by a relative error of at most 0.007.
The reference program's roundings to bfloat16 on the way count: a program that leaves them out, or rounds other values in their place, can miss the bound.
Values may be sent and summed in bfloat16 or wider, within the bound.
A program may use at most 128 MiB of HBM per device.

```python
import jax
import jax.numpy as jnp
from jax import lax

D = 16384
HQ = 64
KVH = 4
HD = 128
S = 4096
STEPS = 4
B = 256


def ragged_parts(key):
    drawn = jax.random.randint(jax.random.fold_in(key, 11), (B,), S // 4, S - STEPS + 1)
    first_row = jax.random.randint(jax.random.fold_in(key, 12), (), 0, B)
    other_row = (first_row + 1 + jax.random.randint(jax.random.fold_in(key, 13), (), 0, B - 1)) % B
    return (drawn.at[first_row].set(S - STEPS).at[other_row].set(S // 4), first_row, other_row)


def draw_lengths(key, part):
    return ragged_parts(key)[0]


def draw_positions(key, part):
    length_rows, first_row, other_row = ragged_parts(key)
    offsets = jax.random.randint(jax.random.fold_in(key, 14), (B,), 0, S)
    offsets = offsets.at[first_row].set(S - 1).at[other_row].set(0)
    return length_rows + offsets


def query_matrix(key):
    scaled = jnp.clip(jax.random.normal(jax.random.fold_in(key, 21), (D, HQ * HD)), -3.0, 3.0)
    return scaled * D ** (-0.5)


def draw_w_query(key, part):
    return query_matrix(key).astype(jnp.bfloat16)


def draw_w_keyval(key, part):
    query_part = query_matrix(key)
    group_size = HQ // KVH
    chosen = jax.random.randint(jax.random.fold_in(key, 22), (KVH,), 0, group_size) + jnp.arange(KVH, dtype=jnp.int32) * group_size
    aligned = query_part.reshape(D, HQ, HD)[:, chosen, :].reshape(D, KVH * HD)
    key_noise = 0.5 * jnp.clip(jax.random.normal(jax.random.fold_in(key, 23), (D, KVH * HD)), -3.0, 3.0) * D ** (-0.5)
    limit = 3.0 * D ** (-0.5)
    key_part = jnp.clip(aligned + key_noise, -limit, limit)
    value_part = jnp.clip(jax.random.normal(jax.random.fold_in(key, 24), (D, KVH * HD)), -3.0, 3.0) * D ** (-0.5)
    return jnp.concatenate([key_part, value_part], axis=1).astype(jnp.bfloat16)


def draw_inputs(key, part):
    row_scale = jnp.power(10.0, jax.random.uniform(jax.random.fold_in(key, 1), (STEPS, B, 1)))
    col_scale = jnp.power(10.0, 0.5 * jnp.arange(D, dtype=jnp.float32) / D + 0.5 * jax.random.uniform(jax.random.fold_in(key, 2), (D,)))
    noise = jnp.clip(jax.random.normal(jax.random.fold_in(key, 3), (STEPS, B, D)), -6.0, 6.0)
    return (noise * row_scale * col_scale).astype(jnp.bfloat16)


def draw_key_cache(key, part):
    drawn = 1.5 * jnp.clip(jax.random.normal(jax.random.fold_in(key, 5), (B, S, KVH * HD)), -6.0, 6.0)
    return drawn.astype(jnp.bfloat16)


def block_levels(own_key, shape, cuts, least, largest):
    gain, own = 1.0, jax.random.fold_in(own_key, 6)
    for axis_at, parts in cuts:
        heights = jnp.exp(jax.random.uniform(jax.random.fold_in(own, axis_at), (parts,), jnp.float32, least / len(cuts), largest / len(cuts)))
        gain = gain * jnp.repeat(heights, shape[axis_at] // parts).reshape([-1 if axis == axis_at else 1 for axis in range(len(shape))])
    return gain


def centred(own_key, dims, deviation, bound, cuts=(), kind=jnp.bfloat16):
    level = block_levels(own_key, dims, cuts, -0.22, 0.18) if cuts else 1.0
    result = jax.random.normal(own_key, dims, jnp.float32) * deviation * level
    return jnp.minimum(jnp.maximum(result, -bound), bound).astype(kind)


def setup_inputs(seed: int = 0) -> dict:
    keys = jax.random.split(jax.random.key(seed), 10)
    inputs = draw_inputs(jax.random.fold_in(keys[9], 71), 0)
    norm_gain = jnp.clip(1.0 + 0.18 * jax.random.normal(keys[1], (D,), jnp.float32), 0.099609375, 1.8984375).astype(jnp.bfloat16)
    w_query = draw_w_query(jax.random.fold_in(keys[9], 71), 0)
    w_keyval = draw_w_keyval(jax.random.fold_in(keys[9], 71), 0)
    w_out = centred(keys[4], (HQ * HD, D), (HQ * HD) ** -0.5, 0.0625, ((0, 16), (1, 8)))
    key_cache = draw_key_cache(jax.random.fold_in(keys[9], 71), 0)
    value_cache = centred(keys[6], (B, S, KVH * HD), 8.0, 48.0, ((0, 128),))
    lengths = draw_lengths(jax.random.fold_in(keys[9], 71), 0)
    positions = draw_positions(jax.random.fold_in(keys[9], 71), 0)
    return {"inputs": inputs, "norm_gain": norm_gain, "w_query": w_query, "w_keyval": w_keyval, "w_out": w_out, "key_cache": key_cache, "value_cache": value_cache, "lengths": lengths, "positions": positions}


def rotate(values, rotary_pos):
    half_dim = values.shape[-1] // 2
    inverse_freq = jnp.exp(-jnp.log(jnp.float32(500000.0)) * jnp.arange(half_dim, dtype=jnp.float32) * 2.0 / (2 * half_dim))
    angles = rotary_pos.astype(jnp.float32)[..., None] * inverse_freq
    cosine = jnp.cos(angles)[..., None, :]
    sine = jnp.sin(angles)[..., None, :]
    first_half = values[..., :half_dim]
    second_half = values[..., half_dim:]
    return jnp.concatenate([first_half * cosine - second_half * sine, second_half * cosine + first_half * sine], axis=-1)

def attend_row(operands):
    query_row, cache_keys, cache_values, length, fresh_keys, fresh_values = operands
    fresh_count = fresh_keys.shape[0]
    factor = 1.0 / jnp.sqrt(jnp.float32(HD))
    grouped = query_row.astype(jnp.float32).reshape(KVH, HQ // KVH, HD)
    keys_f = cache_keys.astype(jnp.float32).reshape(S, KVH, HD)
    cache_scores = jnp.einsum('gqd,sgd->gqs', grouped, keys_f) * factor
    visible = jnp.arange(S, dtype=jnp.int32) < length
    cache_scores = jnp.where(visible, cache_scores, -jnp.inf)
    fresh_f = fresh_keys.astype(jnp.float32).reshape(fresh_count, KVH, HD)
    fresh_scores = jnp.einsum('gqd,mgd->gqm', grouped, fresh_f) * factor
    highest = jnp.maximum(lax.optimization_barrier(jnp.max(cache_scores, -1)), lax.optimization_barrier(jnp.max(fresh_scores, -1)))[..., None]
    cache_exp = jnp.exp(cache_scores - highest)
    fresh_exp = jnp.exp(fresh_scores - highest)
    normaliser = lax.optimization_barrier(jnp.sum(cache_exp, -1, keepdims=True)) + lax.optimization_barrier(jnp.sum(fresh_exp, -1, keepdims=True))
    cache_weights = (cache_exp / normaliser).astype(jnp.bfloat16)
    fresh_weights = (fresh_exp / normaliser).astype(jnp.bfloat16)
    output = jnp.einsum('gqs,sgd->gqd', cache_weights.astype(jnp.float32), cache_values.astype(jnp.float32).reshape(S, KVH, HD))
    output = output + jnp.einsum('gqm,mgd->gqd', fresh_weights.astype(jnp.float32), fresh_values.astype(jnp.float32).reshape(fresh_count, KVH, HD))
    return output.astype(jnp.bfloat16).reshape(HQ * HD)

def reference(inputs, norm_gain, w_query, w_keyval, w_out, key_cache, value_cache, lengths, positions):
    key_list = []
    value_list = []
    step_outputs = []
    for step_index in range(STEPS):
        row_values = inputs[step_index].astype(jnp.float32)
        mean_square = lax.optimization_barrier(jnp.mean(row_values * row_values, axis=-1, keepdims=True))
        normed = (row_values * lax.rsqrt(mean_square + 1e-05) * norm_gain.astype(jnp.float32)).astype(jnp.bfloat16)
        query = jnp.dot(normed, w_query, preferred_element_type=jnp.float32).astype(jnp.bfloat16)
        keyval = jnp.dot(normed, w_keyval, preferred_element_type=jnp.float32).astype(jnp.bfloat16)
        rotary_pos = positions + step_index
        rot_query = rotate(query.astype(jnp.float32).reshape(B, HQ, HD), rotary_pos).astype(jnp.bfloat16).reshape(B, HQ * HD)
        rot_keys = rotate(keyval[:, :KVH * HD].astype(jnp.float32).reshape(B, KVH, HD), rotary_pos).astype(jnp.bfloat16).reshape(B, KVH * HD)
        key_list.append(rot_keys)
        value_list.append(keyval[:, KVH * HD:])
        fresh_keys = jnp.stack(key_list, axis=1)
        fresh_values = jnp.stack(value_list, axis=1)
        attention_out = lax.map(attend_row, (rot_query, key_cache, value_cache, lengths, fresh_keys, fresh_values))
        step_outputs.append(jnp.dot(attention_out, w_out, preferred_element_type=jnp.float32).astype(jnp.bfloat16))
    return (jnp.stack(step_outputs), jnp.stack(key_list), jnp.stack(value_list))
```

```python
import functools

import jax
import jax.numpy as jnp
from jax import lax
from jax.experimental import pallas as pl
from jax.experimental.pallas import tpu as pltpu
from jax.sharding import PartitionSpec as P

D = 16384
HQ = 64
KVH = 4
HD = 128
STEPS = 4
F32 = jnp.float32
BF16 = jnp.bfloat16
MESH = pl.DeviceIdType.MESH


def m4(v):
    return lax.rem(v + 8, 4)


def place():
    w = lax.axis_index("wide")
    n = lax.axis_index("narrow")
    return w, n, w // 4, lax.rem(w, 4), n // 2, lax.rem(n, 2)


def rcopy(src, dst, ssem, rsem, target):
    return pltpu.make_async_remote_copy(
        src_ref=src,
        dst_ref=dst,
        send_sem=ssem,
        recv_sem=rsem,
        device_id=target,
        device_id_type=MESH,
    )


def greet(w, n):
    barrier = pltpu.get_barrier_semaphore()
    for i in range(1, 8):
        pl.semaphore_signal(
            barrier, inc=1, device_id=(w, lax.rem(n + i, 8)), device_id_type=MESH
        )
    for i in range(1, 16):
        pl.semaphore_signal(
            barrier, inc=1, device_id=(lax.rem(w + i, 16), n), device_id_type=MESH
        )
    pl.semaphore_wait(barrier, 22)


class Copies:
    def __init__(self, ssem, rsem):
        self.ssem, self.rsem, self.sent = ssem, rsem, []

    def send(self, k, src, dst, target):
        c = rcopy(src, dst, self.ssem.at[k], self.rsem.at[k], target)
        c.start()
        self.sent.append(c)

    def take(self, k, dst, target):
        rcopy(dst, dst, self.ssem.at[k], self.rsem.at[k], target).wait_recv()

    def drain(self):
        for c in self.sent:
            c.wait_send()


def gather_half(cp, k0, buf, row0, p1, p2, index, to1, to2):
    full, lo, hi = pl.ds(row0, 32), pl.ds(row0, 16), pl.ds(row0 + 16, 16)

    def at(a, b, rows):
        return buf.at[index(m4(a), m4(b)), rows]

    def send(k, a, b, rows, target):
        r = at(a, b, rows)
        cp.send(k0 + k, r, r, target)

    def take(k, a, b, rows):
        cp.take(k0 + k, at(a, b, rows), to1(1))

    def spread(j, a):
        send(4 + 4 * j, a, p2, full, to2(1))
        send(5 + 4 * j, a, p2, full, to2(-1))

    def onward(j, a):
        take(4 + 4 * j, a, p2 - 1, full)
        send(6 + 4 * j, a, p2 - 1, lo, to2(1))
        take(5 + 4 * j, a, p2 + 1, full)
        send(7 + 4 * j, a, p2 + 1, hi, to2(-1))

    def last(j, a):
        take(6 + 4 * j, a, p2 + 2, lo)
        take(7 + 4 * j, a, p2 + 2, hi)

    def s0():
        send(0, p1, p2, full, to1(1))
        send(1, p1, p2, full, to1(-1))

    def s1():
        spread(0, p1)

    def s2():
        take(0, p1 - 1, p2, full)
        send(2, p1 - 1, p2, lo, to1(1))
        take(1, p1 + 1, p2, full)
        send(3, p1 + 1, p2, hi, to1(-1))
        spread(1, p1 - 1)
        spread(2, p1 + 1)

    def s3():
        onward(0, p1)

    def s4():
        take(2, p1 + 2, p2, lo)
        take(3, p1 + 2, p2, hi)
        spread(3, p1 + 2)

    def s5():
        onward(1, p1 - 1)
        onward(2, p1 + 1)

    def s6():
        last(0, p1)
        onward(3, p1 + 2)

    def s7():
        last(1, p1 - 1)
        last(2, p1 + 1)
        last(3, p1 + 2)

    return [s0, s1, s2, s3, s4, s5, s6, s7]


def project_kernel(
    x_ref, gain_ref, wq_hbm, wkv_hbm, out_ref,
    xs, sq, sqr, buf, wq, wkv, part, pair, ring_o, ring_n, qsend, qrecv,
    wsem, sq_s, sq_r, ag_s, ag_r, rs_s, rs_r, aa_s, aa_r,
):
    w, n, z, x, y, c = place()
    load_q = pltpu.make_async_copy(wq_hbm, wq, wsem.at[0])
    load_kv = pltpu.make_async_copy(wkv_hbm, wkv, wsem.at[1])
    load_q.start()
    load_kv.start()
    acc = jnp.zeros((64, 128), F32)
    for j in range(16):
        cols = slice(j * 128, j * 128 + 128)
        for t in range(4):
            xs[j, pl.ds(t, 16, stride=4), :] = x_ref[t, :, cols].astype(F32)
        acc = acc + xs[j] * xs[j]
    row = jnp.sum(acc, axis=-1, keepdims=True)
    diag = lax.broadcasted_iota(jnp.int32, (64, 128), 0) == lax.broadcasted_iota(
        jnp.int32, (64, 128), 1
    )
    flat = jnp.sum(jnp.where(diag, row, 0.0), axis=0, keepdims=True)
    sq[...] = jnp.broadcast_to(flat, (8, 128))
    greet(w, n)

    sqc = Copies(sq_s, sq_r)
    for i in range(1, 8):
        peer = lax.rem(n + i, 8)
        sqc.send(i - 1, sq, sqr.at[i - 1], (w, peer))
    for i in range(1, 8):
        sqc.take(i - 1, sqr.at[i - 1], (w, n))
    total = sq[...]
    for i in range(7):
        total = total + sqr[i]
    column = jnp.sum(
        jnp.where(diag, jnp.broadcast_to(total[0:1], (64, 128)), 0.0), axis=-1, keepdims=True
    )
    inv = lax.rsqrt(column / D + 1e-05)
    for j in range(16):
        cols = slice(j * 128, j * 128 + 128)
        buf[w, :, cols] = (xs[j] * inv * gain_ref[:, cols].astype(F32)).astype(BF16)

    ag = Copies(ag_s, ag_r)
    first = gather_half(
        ag, 0, buf, 0, x, z, lambda a, b: b * 4 + a,
        lambda d: (z * 4 + m4(x + d), n), lambda d: (m4(z + d) * 4 + x, n),
    )
    second = gather_half(
        ag, 20, buf, 32, z, x, lambda a, b: a * 4 + b,
        lambda d: (m4(z + d) * 4 + x, n), lambda d: (z * 4 + m4(x + d), n),
    )
    for a, b in zip(first, second):
        a()
        b()
    load_q.wait()
    load_kv.wait()

    rs = Copies(rs_s, rs_r)
    other = (w, y * 2 + (1 - c))
    up, down = (w, m4(y + 1) * 2 + c), (w, m4(y - 1) * 2 + c)
    order = (m4(y + 2), m4(y + 1), m4(y - 1), y)

    def project(yy):
        rows = pl.ds(pl.multiple_of(yy * 16, 16), 16)
        lhs = buf[:, rows, :].reshape(256, 2048)
        q = jnp.dot(lhs, wq[...], preferred_element_type=F32).reshape(16, 2, 8, 512)
        kv = jnp.dot(lhs, wkv[...], preferred_element_type=F32).reshape(16, 2, 8, 64)
        for cc in range(2):
            part[cc, yy, :, :, 0:512] = q[:, cc]
            part[cc, yy, :, :, 512:576] = kv[:, cc]

    def step(i, carry):
        yy = m4(y + jnp.where(i == 0, 2, jnp.where(i == 1, 1, jnp.where(i == 2, 3, 0))))
        project(yy)
        rcopy(part.at[1 - c, yy], pair.at[yy], rs_s.at[i], rs_r.at[i], other).start()
        return carry

    lax.fori_loop(0, 4, step, 0)

    def merge(i):
        yy = order[i]
        rcopy(part.at[1 - c, yy], pair.at[yy], rs_s.at[i], rs_r.at[i], other).wait_recv()
        part[c, yy] = part[c, yy] + pair[yy]

    lo, hi = pl.ds(0, 8), pl.ds(8, 8)
    merge(0)
    rs.send(4, part.at[c, order[0], lo], ring_o.at[0], up)
    rs.send(5, part.at[c, order[0], hi], ring_o.at[1], down)
    merge(1)
    rs.send(6, part.at[c, order[1], hi], ring_n.at[0, hi], up)
    merge(2)
    rs.send(7, part.at[c, order[2], lo], ring_n.at[1, lo], down)
    rs.take(4, ring_o.at[0], up)
    part[c, order[1], 0:8] = part[c, order[1], 0:8] + ring_o[0]
    rs.send(8, part.at[c, order[1], lo], ring_n.at[0, lo], up)
    rs.take(5, ring_o.at[1], up)
    part[c, order[2], 8:16] = part[c, order[2], 8:16] + ring_o[1]
    rs.send(9, part.at[c, order[2], hi], ring_n.at[1, hi], down)
    merge(3)
    rs.take(6, ring_n.at[0, hi], up)
    rs.take(7, ring_n.at[1, lo], up)
    rs.take(8, ring_n.at[0, lo], up)
    rs.take(9, ring_n.at[1, hi], up)
    qsend[...] = (part[c, y] + ring_n[0] + ring_n[1]).astype(BF16)

    aa = Copies(aa_s, aa_r)
    for i in range(1, 16):
        peer = lax.rem(w + i, 16)
        aa.send(i - 1, qsend.at[peer], qrecv.at[w], (peer, n))
    qrecv[w] = qsend[w]
    for i in range(1, 16):
        aa.take(i - 1, qrecv.at[lax.rem(w - i + 16, 16)], (w, n))
    out_ref[...] = qrecv[...]
    sqc.drain()
    ag.drain()
    for i in range(4):
        rcopy(
            part.at[1 - c, order[i]], pair.at[order[i]], rs_s.at[i], rs_r.at[i], other
        ).wait_send()
    rs.drain()
    aa.drain()


def project(inputs, norm_gain, w_query, w_keyval):
    dma = pltpu.SemaphoreType.DMA
    vm = pl.BlockSpec(memory_space=pltpu.VMEM)
    return pl.pallas_call(
        project_kernel,
        out_shape=jax.ShapeDtypeStruct((16, 8, 576), BF16),
        in_specs=[vm, vm, pl.BlockSpec(memory_space=pl.ANY), pl.BlockSpec(memory_space=pl.ANY)],
        out_specs=vm,
        scratch_shapes=[
            pltpu.VMEM((16, 64, 128), F32),
            pltpu.VMEM((8, 128), F32),
            pltpu.VMEM((7, 8, 128), F32),
            pltpu.VMEM((16, 64, 2048), BF16),
            pltpu.VMEM((2048, 512), BF16),
            pltpu.VMEM((2048, 64), BF16),
            pltpu.VMEM((2, 4, 16, 8, 576), F32),
            pltpu.VMEM((4, 16, 8, 576), F32),
            pltpu.VMEM((2, 8, 8, 576), F32),
            pltpu.VMEM((2, 16, 8, 576), F32),
            pltpu.VMEM((16, 8, 576), BF16),
            pltpu.VMEM((16, 8, 576), BF16),
            dma((2,)), dma((7,)), dma((7,)), dma((40,)), dma((40,)), dma((10,)), dma((10,)),
            dma((15,)), dma((15,)),
        ],
        compiler_params=pltpu.CompilerParams(
            collective_id=0, has_side_effects=True, vmem_limit_bytes=48 << 20
        ),
        name="project",
    )(inputs, norm_gain.reshape(1, 2048), w_query, w_keyval)


def attend_kernel(len_ref, qkv, cos_ref, sin_ref, k_ref, v_ref, att, nk, nv,
                  qs, kf, vf, sc, os):
    i = pl.program_id(0)
    r, gp = i // 2, lax.rem(i, 2)
    low = lax.broadcasted_iota(jnp.int32, (1, 8, 128), 1) < 4

    @pl.when(i == 0)
    def _():
        cos, sin = cos_ref[...], sin_ref[...]

        def turn(a):
            return (a * cos + pltpu.roll(a, 64, a.ndim - 1) * sin).astype(BF16)

        qs[...] = jnp.zeros_like(qs)
        kf[...] = jnp.zeros_like(kf)
        vf[...] = jnp.zeros_like(vf)
        for p in range(2):
            a = turn(qkv[:, :, p * 256 : p * 256 + 128].astype(F32)).astype(F32)
            b = turn(qkv[:, :, p * 256 + 128 : p * 256 + 256].astype(F32)).astype(F32)
            for rr, tile in (
                (0, jnp.where(low, a, pltpu.roll(b, 4, 1))),
                (1, jnp.where(low, pltpu.roll(a, 4, 1), b)),
            ):
                for g in range(4):
                    gi = g % 2
                    qs[rr, g // 2, gi * 64 + p * 32 : gi * 64 + p * 32 + 32,
                       gi * 128 : gi * 128 + 128] = (
                        tile[4 * g : 4 * g + 4].reshape(32, 128).astype(BF16)
                    )
        for g in range(4):
            key = jnp.concatenate(
                [qkv[2 * g, :, 512:576].astype(F32), qkv[2 * g + 1, :, 512:576].astype(F32)], -1
            )
            val = jnp.concatenate(
                [qkv[2 * g + 8, :, 512:576].astype(F32), qkv[2 * g + 9, :, 512:576].astype(F32)], -1
            )
            kf[0:8, g * 128 : g * 128 + 128] = turn(key)
            vf[0:8, g * 128 : g * 128 + 128] = val.astype(BF16)
        nk[...] = kf[0:8, :]
        nv[...] = vf[0:8, :]

    factor = 1.0 / jnp.sqrt(F32(HD))
    q = qs[r, gp]
    cols = pl.ds(pl.multiple_of(gp * 256, 256), 256)
    length = len_ref[r]
    nt = (((1,), (1,)), ((), ()))

    fs = lax.dot_general(q, kf[:, cols], nt, preferred_element_type=F32) * factor
    lane = lax.broadcasted_iota(jnp.int32, (128, 128), 1)
    step = lax.rem(lax.broadcasted_iota(jnp.int32, (128, 128), 0), 4)
    ok = (lane // 4 == r) & (lane - 4 * r <= step)
    fs = jnp.where(ok, fs, -jnp.inf)

    chunk = 512
    count = 4096 // chunk

    def score(j, top):
        at = pl.ds(pl.multiple_of(j * chunk, chunk), chunk)
        s = lax.dot_general(q, k_ref[0, at, :], nt, preferred_element_type=F32) * factor
        pos = lax.broadcasted_iota(jnp.int32, (128, chunk), 1) + j * chunk
        s = jnp.where(pos < length, s, -jnp.inf)
        sc[:, at] = s
        for u in range(chunk // 128):
            top = jnp.maximum(top, s[:, u * 128 : u * 128 + 128])
        return top

    top = lax.fori_loop(0, count, score, fs)
    top = jnp.max(top, axis=-1, keepdims=True)
    fe = jnp.exp(fs - top)

    def expo(j, acc):
        at = pl.ds(pl.multiple_of(j * chunk, chunk), chunk)
        e = jnp.exp(sc[:, at] - top)
        sc[:, at] = e
        for u in range(chunk // 128):
            acc = acc + e[:, u * 128 : u * 128 + 128]
        return acc

    acc = lax.fori_loop(0, count, expo, fe)
    scale = 1.0 / jnp.sum(acc, axis=-1, keepdims=True)

    def value(j, out):
        at = pl.ds(pl.multiple_of(j * chunk, chunk), chunk)
        p = (sc[:, at] * scale).astype(BF16)
        return out + jnp.dot(p, v_ref[0, at, :], preferred_element_type=F32)

    out = jnp.dot((fe * scale).astype(BF16), vf[:, cols], preferred_element_type=F32)
    out = lax.fori_loop(0, count, value, out)
    os[r, gp, 0] = out[0:64, 0:128]
    os[r, gp, 1] = out[64:128, 128:256]

    @pl.when(i == 3)
    def _():
        for g in range(4):
            for p in range(2):
                rows = slice(p * 32, p * 32 + 32)
                a = os[0, g // 2, g % 2, rows].reshape(4, 8, 128)
                b = os[1, g // 2, g % 2, rows].reshape(4, 8, 128)
                att[4 * g : 4 * g + 4, :, p * 256 : p * 256 + 128] = jnp.where(
                    low, a, pltpu.roll(b, 4, 1)
                ).astype(BF16)
                att[4 * g : 4 * g + 4, :, p * 256 + 128 : p * 256 + 256] = jnp.where(
                    low, pltpu.roll(a, 4, 1), b
                ).astype(BF16)


def attend(qkv, key_cache, value_cache, lengths, positions):
    half = HD // 2
    freq = jnp.exp(
        -jnp.log(F32(500000.0)) * jnp.arange(half, dtype=F32) * 2.0 / (2 * half)
    )
    pos = positions[:, None] + jnp.arange(STEPS, dtype=jnp.int32)[None, :]
    ang = (pos.astype(F32)[..., None] * freq).reshape(8, half)
    cos, sin = jnp.cos(ang), jnp.sin(ang)
    cos2 = jnp.concatenate([cos, cos], -1)
    sin2 = jnp.concatenate([-sin, sin], -1)

    def whole(shape):
        return pl.BlockSpec(shape, lambda i, ln: (0,) * len(shape))

    cache = pl.BlockSpec((1, 4096, 256), lambda i, ln: (i // 2, 0, lax.rem(i, 2)))
    return pl.pallas_call(
        attend_kernel,
        out_shape=(
            jax.ShapeDtypeStruct((16, 8, 512), BF16),
            jax.ShapeDtypeStruct((8, 512), BF16),
            jax.ShapeDtypeStruct((8, 512), BF16),
        ),
        grid_spec=pltpu.PrefetchScalarGridSpec(
            num_scalar_prefetch=1,
            grid=(4,),
            in_specs=[whole((16, 8, 576)), whole((8, 128)), whole((8, 128)), cache, cache],
            out_specs=(whole((16, 8, 512)), whole((8, 512)), whole((8, 512))),
            scratch_shapes=[
                pltpu.VMEM((2, 2, 128, 256), BF16),
                pltpu.VMEM((128, 512), BF16),
                pltpu.VMEM((128, 512), BF16),
                pltpu.VMEM((128, 4096), F32),
                pltpu.VMEM((2, 2, 2, 64, 128), F32),
            ],
        ),
        compiler_params=pltpu.CompilerParams(vmem_limit_bytes=32 << 20),
        name="attend",
    )(lengths, qkv, cos2, sin2, key_cache, value_cache)


def output_kernel(
    att, wo_hbm, out_ref,
    wo, g, gm, prod, so, sn, ro, rn, so2, sn2, ro2, rn2, res,
    wsem, aa_s, aa_r, ag_s, ag_r, st_s, st_r, st2_s, st2_r,
):
    w, n, z, x, y, c = place()
    load = pltpu.make_async_copy(wo_hbm, wo, wsem)
    load.start()
    greet(w, n)

    aa = Copies(aa_s, aa_r)
    for i in range(1, 16):
        peer = lax.rem(w + i, 16)
        aa.send(i - 1, att.at[peer], g.at[n, w], (peer, n))
    g[n, w] = att[w]
    for i in range(1, 16):
        aa.take(i - 1, g.at[n, lax.rem(w - i + 16, 16)], (w, n))

    ag = Copies(ag_s, ag_r)
    other = (w, y * 2 + (1 - c))
    up, down = (w, m4(y + 1) * 2 + c), (w, m4(y - 1) * 2 + c)
    above, below, far = m4(y + 1) * 2 + c, m4(y - 1) * 2 + c, m4(y + 2) * 2 + c
    lo, hi = pl.ds(0, 8), pl.ds(8, 8)
    ag.send(0, g.at[n], g.at[n], up)
    ag.send(1, g.at[n], g.at[n], down)
    ag.send(2, g.at[n], g.at[n], other)
    ag.take(0, g.at[below], up)
    ag.send(3, g.at[below, lo], g.at[below, lo], up)
    ag.send(4, g.at[below], g.at[below], other)
    ag.take(1, g.at[above], up)
    ag.send(5, g.at[above, hi], g.at[above, hi], down)
    ag.send(6, g.at[above], g.at[above], other)
    ag.take(3, g.at[far, lo], up)
    ag.take(5, g.at[far, hi], up)
    ag.send(7, g.at[far], g.at[far], other)
    ag.take(2, g.at[y * 2 + 1 - c], up)
    ag.take(4, g.at[m4(y - 1) * 2 + 1 - c], up)
    ag.take(6, g.at[m4(y + 1) * 2 + 1 - c], up)
    ag.take(7, g.at[m4(y + 2) * 2 + 1 - c], up)

    def regroup(i, carry):
        gm[i] = g[:, i].astype(F32).reshape(64, 512).astype(BF16)
        return carry

    lax.fori_loop(0, 16, regroup, 0)
    load.wait()

    def multiply(i, carry):
        rows = pl.ds(pl.multiple_of((i // 4) * 4, 4), 4)
        cols = pl.ds(pl.multiple_of(lax.rem(i, 4) * 512, 512), 512)
        v = jnp.dot(gm[rows].reshape(256, 512), wo[:, cols], preferred_element_type=F32)
        prod[rows, :, cols] = v.reshape(4, 64, 512)
        return carry

    lax.fori_loop(0, 16, multiply, 0)

    st = Copies(st_s, st_r)
    st2 = Copies(st2_s, st2_r)
    top, bot = pl.ds(0, 32), pl.ds(32, 32)
    halves = (
        (0, x, z, lambda a, b: m4(b) * 4 + m4(a),
         lambda d: (z * 4 + m4(x + d), n), lambda d: (m4(z + d) * 4 + x, n)),
        (1, z, x, lambda a, b: m4(a) * 4 + m4(b),
         lambda d: (m4(z + d) * 4 + x, n), lambda d: (z * 4 + m4(x + d), n)),
    )
    for h, p1, p2, index, to1, to2 in halves:
        cols = pl.ds(h * 1024, 1024)
        for q in range(4):
            so[h, 0, q] = prod[index(p1 + 2, q), top, cols].astype(BF16)
            so[h, 1, q] = prod[index(p1 + 2, q), bot, cols].astype(BF16)
        st.send(h * 6 + 0, so.at[h, 0], ro.at[h, 0], to1(1))
        st.send(h * 6 + 1, so.at[h, 1], ro.at[h, 1], to1(-1))
    for h, p1, p2, index, to1, to2 in halves:
        cols = pl.ds(h * 1024, 1024)
        for q in range(4):
            sn[h, 0, q, bot] = prod[index(p1 + 1, q), bot, cols].astype(BF16)
            sn[h, 1, q, top] = prod[index(p1 - 1, q), top, cols].astype(BF16)
        st.send(h * 6 + 2, sn.at[h, 0, :, bot], rn.at[h, 0, :, bot], to1(1))
        st.send(h * 6 + 3, sn.at[h, 1, :, top], rn.at[h, 1, :, top], to1(-1))
    for h, p1, p2, index, to1, to2 in halves:
        cols = pl.ds(h * 1024, 1024)
        st.take(h * 6 + 0, ro.at[h, 0], to1(1))
        for q in range(4):
            sn[h, 0, q, top] = (
                prod[index(p1 + 1, q), top, cols] + ro[h, 0, q].astype(F32)
            ).astype(BF16)
        st.send(h * 6 + 4, sn.at[h, 0, :, top], rn.at[h, 0, :, top], to1(1))
        st.take(h * 6 + 1, ro.at[h, 1], to1(1))
        for q in range(4):
            sn[h, 1, q, bot] = (
                prod[index(p1 - 1, q), bot, cols] + ro[h, 1, q].astype(F32)
            ).astype(BF16)
        st.send(h * 6 + 5, sn.at[h, 1, :, bot], rn.at[h, 1, :, bot], to1(-1))
    for h, p1, p2, index, to1, to2 in halves:
        cols = pl.ds(h * 1024, 1024)
        st.take(h * 6 + 2, rn.at[h, 0, :, bot], to1(1))
        st.take(h * 6 + 3, rn.at[h, 1, :, top], to1(1))
        st.take(h * 6 + 4, rn.at[h, 0, :, top], to1(1))
        st.take(h * 6 + 5, rn.at[h, 1, :, bot], to1(1))

        def add(b):
            i = index(p1, b)
            b = m4(b)
            prod[i, :, cols] = (
                prod[i, :, cols] + rn[h, 0, b].astype(F32) + rn[h, 1, b].astype(F32)
            )
            return i

        i = add(p2 + 2)
        so2[h, 0] = prod[i, top, cols].astype(BF16)
        so2[h, 1] = prod[i, bot, cols].astype(BF16)
        st2.send(h * 6 + 0, so2.at[h, 0], ro2.at[h, 0], to2(1))
        st2.send(h * 6 + 1, so2.at[h, 1], ro2.at[h, 1], to2(-1))
        i = add(p2 + 1)
        sn2[h, 0, bot] = prod[i, bot, cols].astype(BF16)
        st2.send(h * 6 + 2, sn2.at[h, 0, bot], rn2.at[h, 0, bot], to2(1))
        i = add(p2 - 1)
        sn2[h, 1, top] = prod[i, top, cols].astype(BF16)
        st2.send(h * 6 + 3, sn2.at[h, 1, top], rn2.at[h, 1, top], to2(-1))
        add(p2)
    for h, p1, p2, index, to1, to2 in halves:
        cols = pl.ds(h * 1024, 1024)
        st2.take(h * 6 + 0, ro2.at[h, 0], to1(1))
        sn2[h, 0, top] = (
            prod[index(p1, p2 + 1), top, cols] + ro2[h, 0].astype(F32)
        ).astype(BF16)
        st2.send(h * 6 + 4, sn2.at[h, 0, top], rn2.at[h, 0, top], to2(1))
        st2.take(h * 6 + 1, ro2.at[h, 1], to1(1))
        sn2[h, 1, bot] = (
            prod[index(p1, p2 - 1), bot, cols] + ro2[h, 1].astype(F32)
        ).astype(BF16)
        st2.send(h * 6 + 5, sn2.at[h, 1, bot], rn2.at[h, 1, bot], to2(-1))
    for h, p1, p2, index, to1, to2 in halves:
        cols = pl.ds(h * 1024, 1024)
        st2.take(h * 6 + 2, rn2.at[h, 0, bot], to1(1))
        st2.take(h * 6 + 3, rn2.at[h, 1, top], to1(1))
        st2.take(h * 6 + 4, rn2.at[h, 0, top], to1(1))
        st2.take(h * 6 + 5, rn2.at[h, 1, bot], to1(1))
        for j in range(8):
            sub = slice(j * 128, j * 128 + 128)
            res[h * 8 + j] = (
                prod[w, :, pl.ds(h * 1024 + j * 128, 128)]
                + rn2[h, 0, :, sub].astype(F32)
                + rn2[h, 1, :, sub].astype(F32)
            )
    for j in range(16):
        for t in range(4):
            out_ref[t, :, j * 128 : j * 128 + 128] = res[j, pl.ds(t, 16, stride=4), :].astype(BF16)
    aa.drain()
    ag.drain()
    st.drain()
    st2.drain()


def output(att, w_out):
    dma = pltpu.SemaphoreType.DMA
    vm = pl.BlockSpec(memory_space=pltpu.VMEM)
    return pl.pallas_call(
        output_kernel,
        out_shape=jax.ShapeDtypeStruct((4, 16, 2048), BF16),
        in_specs=[vm, pl.BlockSpec(memory_space=pl.ANY)],
        out_specs=vm,
        scratch_shapes=[
            pltpu.VMEM((512, 2048), BF16),
            pltpu.VMEM((8, 16, 8, 512), BF16),
            pltpu.VMEM((16, 64, 512), BF16),
            pltpu.VMEM((16, 64, 2048), F32),
            pltpu.VMEM((2, 2, 4, 32, 1024), BF16),
            pltpu.VMEM((2, 2, 4, 64, 1024), BF16),
            pltpu.VMEM((2, 2, 4, 32, 1024), BF16),
            pltpu.VMEM((2, 2, 4, 64, 1024), BF16),
            pltpu.VMEM((2, 2, 32, 1024), BF16),
            pltpu.VMEM((2, 2, 64, 1024), BF16),
            pltpu.VMEM((2, 2, 32, 1024), BF16),
            pltpu.VMEM((2, 2, 64, 1024), BF16),
            pltpu.VMEM((16, 64, 128), F32),
            dma, dma((15,)), dma((15,)), dma((8,)), dma((8,)),
            dma((12,)), dma((12,)), dma((12,)), dma((12,)),
        ],
        compiler_params=pltpu.CompilerParams(
            collective_id=1, has_side_effects=True, vmem_limit_bytes=48 << 20
        ),
        name="output",
    )(att, w_out)


def local(inputs, norm_gain, w_query, w_keyval, w_out, key_cache, value_cache, lengths, positions):
    qkv = project(inputs, norm_gain, w_query, w_keyval)
    att, nk, nv = attend(qkv, key_cache, value_cache, lengths, positions)
    attended = output(att, w_out)

    def by_step(a):
        return a.reshape(2, STEPS, KVH * HD).transpose(1, 0, 2)

    return attended, by_step(nk), by_step(nv)


def solution(mesh):
    return jax.shard_map(
        local,
        mesh=mesh,
        in_specs=(
            P(None, "wide", "narrow"),
            P("narrow"),
            P("narrow", "wide"),
            P("narrow", "wide"),
            P("wide", "narrow"),
            P(("wide", "narrow"), None, None),
            P(("wide", "narrow"), None, None),
            P(("wide", "narrow")),
            P(("wide", "narrow")),
        ),
        out_specs=(
            P(None, "wide", "narrow"),
            P(None, ("wide", "narrow"), None),
            P(None, ("wide", "narrow"), None),
        ),
        check_vma=False,
    )
```

```python
import jax
import jax.numpy as jnp
from jax import lax
from jax.experimental import pallas as pl
from jax.experimental.pallas import tpu as pltpu
from jax.sharding import PartitionSpec as P

D = 16384
HQ = 64
KVH = 4
HD = 128
STEPS = 4
F32 = jnp.float32
BF16 = jnp.bfloat16
MESH = pl.DeviceIdType.MESH
NT = (((1,), (1,)), ((), ()))
CHUNK = 2048

SLOTS = (
    ((0, 0), (-1, 0), (1, 0), (2, 0)),
    ((-1, -1), (-1, 1), (1, -1), (1, 1)),
    ((0, -1), (0, 1), (2, -1), (2, 1)),
    ((0, 2), (-1, 2), (1, 2), (2, 2)),
)
WHERE = {(a % 4, b % 4): (g, s) for g, row in enumerate(SLOTS) for s, (a, b) in enumerate(row)}
OFFSETS = (2, 1, -1, 0)


def m4(v):
    return lax.rem(v + 8, 4)


def rcopy(src, dst, ssem, rsem, target):
    return pltpu.make_async_remote_copy(
        src_ref=src,
        dst_ref=dst,
        send_sem=ssem,
        recv_sem=rsem,
        device_id=target,
        device_id_type=MESH,
    )


class Copies:
    def __init__(self, ssem, rsem):
        self.ssem, self.rsem, self.sent = ssem, rsem, []

    def send(self, k, src, dst, target):
        c = rcopy(src, dst, self.ssem.at[k], self.rsem.at[k], target)
        c.start()
        self.sent.append(c)

    def take(self, k, dst, target):
        rcopy(dst, dst, self.ssem.at[k], self.rsem.at[k], target).wait_recv()

    def drain(self):
        for c in self.sent:
            c.wait_send()


def gather_half(cp, k0, buf, h, to1, to2):
    full, lo, hi = pl.ds(0, 32), pl.ds(0, 16), pl.ds(16, 16)

    def at(a, b, rows):
        g, s = WHERE[(a % 4, b % 4)]
        return buf.at[g, h, s, rows]

    def send1(k, a, b, rows, d):
        cp.send(k0 + k, at(a, b, rows), at(a - d, b, rows), to1(d))

    def send2(k, a, b, rows, d):
        cp.send(k0 + k, at(a, b, rows), at(a, b - d, rows), to2(d))

    def take(k, a, b, rows):
        cp.take(k0 + k, at(a, b, rows), to1(1))

    def spread(j, a):
        send2(4 + 4 * j, a, 0, full, 1)
        send2(5 + 4 * j, a, 0, full, -1)

    def onward(j, a):
        take(4 + 4 * j, a, -1, full)
        send2(6 + 4 * j, a, -1, lo, 1)
        take(5 + 4 * j, a, 1, full)
        send2(7 + 4 * j, a, 1, hi, -1)

    def last(j, a):
        take(6 + 4 * j, a, 2, lo)
        take(7 + 4 * j, a, 2, hi)

    def s0():
        send1(0, 0, 0, full, 1)
        send1(1, 0, 0, full, -1)

    def s1():
        spread(0, 0)

    def s2():
        take(0, -1, 0, full)
        send1(2, -1, 0, lo, 1)
        take(1, 1, 0, full)
        send1(3, 1, 0, hi, -1)
        spread(1, -1)
        spread(2, 1)

    def s3():
        onward(0, 0)

    def s4():
        take(2, 2, 0, lo)
        take(3, 2, 0, hi)
        spread(3, 2)

    def s5():
        onward(1, -1)
        onward(2, 1)

    def s6():
        last(0, 0)
        onward(3, 2)

    def s7():
        last(1, -1)
        last(2, 1)
        last(3, 2)

    return [s0, s1, s2, s3, s4, s5, s6, s7]


def layer_kernel(
    len_ref, x_hbm, gain_hbm, wq_hbm, wkv_hbm, wo_hbm, k_hbm, v_hbm, cos_ref, sin_ref,
    out_ref, nk, nv,
    xv, gain, wq, wkv, wo, kb, vb,
    xs, sq, sqr, buf, part, pair, ring_o, ring_n, qsend, qrecv,
    qs, kf, vf, sc, os, att, g, gm,
    so, sn, ro, rn, kp, km, so2, sn2, ro2, rn2, res,
    ld, sq_s, sq_r, ag_s, ag_r, ex_s, ex_r, rs_s, rs_r, aa_s, aa_r,
    ao_s, ao_r, gn_s, gn_r, st_s, st_r, st2_s, st2_r,
):
    w = lax.axis_index("wide")
    n = lax.axis_index("narrow")
    z, x, y, c = w // 4, lax.rem(w, 4), n // 2, lax.rem(n, 2)

    def along_x(d):
        return (z * 4 + m4(x + d), n)

    def along_z(d):
        return (m4(z + d) * 4 + x, n)

    other = (w, y * 2 + (1 - c))
    up, down = (w, m4(y + 1) * 2 + c), (w, m4(y - 1) * 2 + c)

    barrier = pltpu.get_barrier_semaphore()
    for i in range(1, 8):
        pl.semaphore_signal(
            barrier, inc=1, device_id=(w, lax.rem(n + i, 8)), device_id_type=MESH
        )
    for d in (1, -1):
        pl.semaphore_signal(barrier, inc=1, device_id=along_x(d), device_id_type=MESH)
        pl.semaphore_signal(barrier, inc=1, device_id=along_z(d), device_id_type=MESH)

    pairs = [(x_hbm, xv), (gain_hbm, gain), (wq_hbm, wq), (wkv_hbm, wkv), (wo_hbm, wo)]
    pairs += [(k_hbm, kb), (v_hbm, vb)]
    loads = [pltpu.make_async_copy(s, d, ld.at[i]) for i, (s, d) in enumerate(pairs)]
    for load in loads[:5]:
        load.start()
    loads[0].wait()
    acc = jnp.zeros((64, 128), F32)
    for j in range(16):
        cols = slice(j * 128, j * 128 + 128)
        for t in range(4):
            xs[j, pl.ds(t, 16, stride=4), :] = xv[t, :, cols].astype(F32)
        acc = acc + xs[j] * xs[j]
    row = jnp.sum(acc, axis=-1, keepdims=True)
    diag = lax.broadcasted_iota(jnp.int32, (64, 128), 0) == lax.broadcasted_iota(
        jnp.int32, (64, 128), 1
    )
    flat = jnp.sum(jnp.where(diag, row, 0.0), axis=0, keepdims=True)
    sq[...] = jnp.broadcast_to(flat, (8, 128))
    pl.semaphore_wait(barrier, 11)

    sqc = Copies(sq_s, sq_r)
    for i in range(1, 8):
        sqc.send(i - 1, sq, sqr.at[i - 1], (w, lax.rem(n + i, 8)))
    loads[5].start()
    loads[6].start()
    for i in range(1, 8):
        sqc.take(i - 1, sqr.at[i - 1], other)
    total = sq[...]
    for i in range(7):
        total = total + sqr[i]
    column = jnp.sum(
        jnp.where(diag, jnp.broadcast_to(total[0:1], (64, 128)), 0.0), axis=-1, keepdims=True
    )
    inv = lax.rsqrt(column / D + 1e-05)
    loads[1].wait()
    for j in range(16):
        cols = slice(j * 128, j * 128 + 128)
        own = (xs[j] * inv * gain[:, cols].astype(F32)).astype(BF16)
        buf[0, 0, 0, :, cols] = own[0:32]
        buf[0, 1, 0, :, cols] = own[32:64]

    ag = Copies(ag_s, ag_r)
    first = gather_half(ag, 0, buf, 0, along_x, along_z)
    second = gather_half(ag, 20, buf, 1, along_z, along_x)

    def gather(*steps):
        for i in steps:
            first[i]()
            second[i]()

    ex, rs, aa = Copies(ex_s, ex_r), Copies(rs_s, rs_r), Copies(aa_s, aa_r)
    far, above, below = m4(y + 2), m4(y + 1), m4(y - 1)

    def multiply(i):
        lhs = buf[i].reshape(256, 2048)
        q = jnp.dot(lhs, wq[...], preferred_element_type=F32)
        kv = lax.dot_general(lhs, wkv[...], NT, preferred_element_type=F32)
        for h in range(2):
            qh = q[h * 128 : h * 128 + 128].reshape(4, 2, 2, 8, 512)
            kvh = kv[h * 128 : h * 128 + 128].reshape(4, 2, 2, 8, 64)
            for yy in range(2):
                for cc in range(2):
                    part[cc, h * 2 + yy, 4 * i : 4 * i + 4, :, 0:512] = qh[:, yy, cc]
                    part[cc, h * 2 + yy, 4 * i : 4 * i + 4, :, 512:576] = kvh[:, yy, cc]
        at = pl.ds(4 * i, 4)
        ex.send(i, part.at[1 - c, :, at], pair.at[:, at], other)

    def ring1(i):
        at, lo, hi = pl.ds(4 * i, 4), pl.ds(4 * i, 2), pl.ds(4 * i + 2, 2)
        ex.take(i, pair.at[:, at], other)
        part[c, :, at] = part[c, :, at] + pair[:, at]
        rs.send(6 * i + 0, part.at[c, far, lo], ring_o.at[0, i], up)
        rs.send(6 * i + 1, part.at[c, far, hi], ring_o.at[1, i], down)
        rs.send(6 * i + 2, part.at[c, above, hi], ring_n.at[0, hi], up)
        rs.send(6 * i + 3, part.at[c, below, lo], ring_n.at[1, lo], down)

    def ring2(i):
        lo, hi = pl.ds(4 * i, 2), pl.ds(4 * i + 2, 2)
        rs.take(6 * i + 0, ring_o.at[0, i], up)
        part[c, above, lo] = part[c, above, lo] + ring_o[0, i]
        rs.send(6 * i + 4, part.at[c, above, lo], ring_n.at[0, lo], up)
        rs.take(6 * i + 1, ring_o.at[1, i], up)
        part[c, below, hi] = part[c, below, hi] + ring_o[1, i]
        rs.send(6 * i + 5, part.at[c, below, hi], ring_n.at[1, hi], down)

    def finish(i):
        at, lo, hi = pl.ds(4 * i, 4), pl.ds(4 * i, 2), pl.ds(4 * i + 2, 2)
        rs.take(6 * i + 2, ring_n.at[0, hi], up)
        rs.take(6 * i + 3, ring_n.at[1, lo], up)
        rs.take(6 * i + 4, ring_n.at[0, lo], up)
        rs.take(6 * i + 5, ring_n.at[1, hi], up)
        qsend[at] = (part[c, y, at] + ring_n[0, at] + ring_n[1, at]).astype(BF16)
        for s, (a, b) in enumerate(SLOTS[i]):
            if (a, b) == (0, 0):
                qrecv[w] = qsend[0]
                continue
            dz, dx = jnp.where(y < 2, b, a), jnp.where(y < 2, a, b)
            k = 4 * i + s
            aa.send(k, qsend.at[k], qrecv.at[w], (m4(z + dz) * 4 + m4(x + dx), n))

    gather(0, 1, 2, 3, 4)
    loads[2].wait()
    loads[3].wait()
    multiply(0)
    gather(5)
    multiply(1)
    ring1(0)
    gather(6)
    multiply(2)
    ring1(1)
    ring2(0)
    gather(7)
    multiply(3)
    finish(0)
    ring1(2)
    ring2(1)
    ring1(3)
    ring2(2)
    finish(1)
    ring2(3)
    finish(2)
    finish(3)
    for i in range(4):
        for s, (a, b) in enumerate(SLOTS[i]):
            if (a, b) != (0, 0):
                dz, dx = jnp.where(y < 2, b, a), jnp.where(y < 2, a, b)
                source = m4(z - dz) * 4 + m4(x - dx)
                aa.take(4 * i + s, qrecv.at[source], other)

    low = lax.broadcasted_iota(jnp.int32, (1, 8, 128), 1) < 4
    cos, sin = cos_ref[...], sin_ref[...]

    def turn(a):
        return (a * cos + pltpu.roll(a, 64, a.ndim - 1) * sin).astype(BF16)

    qs[...] = jnp.zeros_like(qs)
    kf[...] = jnp.zeros_like(kf)
    vf[...] = jnp.zeros_like(vf)
    for p in range(2):
        a = turn(qrecv[:, :, p * 256 : p * 256 + 128].astype(F32)).astype(F32)
        b = turn(qrecv[:, :, p * 256 + 128 : p * 256 + 256].astype(F32)).astype(F32)
        for rr, tile in (
            (0, jnp.where(low, a, pltpu.roll(b, 4, 1))),
            (1, jnp.where(low, pltpu.roll(a, 4, 1), b)),
        ):
            for h in range(4):
                gi = h % 2
                qs[rr, h // 2, gi * 64 + p * 32 : gi * 64 + p * 32 + 32,
                   gi * 128 : gi * 128 + 128] = (
                    tile[4 * h : 4 * h + 4].reshape(32, 128).astype(BF16)
                )
    for h in range(4):
        key = jnp.concatenate(
            [qrecv[2 * h, :, 512:576].astype(F32), qrecv[2 * h + 1, :, 512:576].astype(F32)], -1
        )
        val = jnp.concatenate(
            [qrecv[2 * h + 8, :, 512:576].astype(F32), qrecv[2 * h + 9, :, 512:576].astype(F32)], -1
        )
        kf[0:8, h * 128 : h * 128 + 128] = turn(key)
        vf[0:8, h * 128 : h * 128 + 128] = val.astype(BF16)
    nk[...] = kf[0:8, :]
    nv[...] = vf[0:8, :]
    loads[5].wait()
    loads[6].wait()

    factor = 1.0 / jnp.sqrt(F32(HD))
    lane = lax.broadcasted_iota(jnp.int32, (128, 128), 1)
    step = lax.rem(lax.broadcasted_iota(jnp.int32, (128, 128), 0), 4)
    place = lax.broadcasted_iota(jnp.int32, (128, CHUNK), 1)

    def attend(i, carry):
        r, gp = lax.rem(i, 2), i // 2
        q = qs[r, gp]
        cols = pl.ds(pl.multiple_of(gp * 256, 256), 256)
        length = len_ref[r]
        fs = lax.dot_general(q, kf[:, cols], NT, preferred_element_type=F32) * factor
        fs = jnp.where((lane // 4 == r) & (lane - 4 * r <= step), fs, -jnp.inf)

        def score(j, top):
            at = pl.ds(pl.multiple_of(j * CHUNK, CHUNK), CHUNK)
            s = lax.dot_general(q, kb[r, at, cols], NT, preferred_element_type=F32) * factor
            s = jnp.where(place < length - j * CHUNK, s, -jnp.inf)
            sc[:, at] = s
            for u in range(CHUNK // 128):
                top = jnp.maximum(top, s[:, u * 128 : u * 128 + 128])
            return top

        top = lax.fori_loop(0, 4096 // CHUNK, score, fs)
        top = jnp.max(top, axis=-1, keepdims=True)
        fe = jnp.exp(fs - top)

        def expo(j, acc):
            at = pl.ds(pl.multiple_of(j * CHUNK, CHUNK), CHUNK)
            e = jnp.exp(sc[:, at] - top)
            sc[:, at] = e
            for u in range(CHUNK // 128):
                acc = acc + e[:, u * 128 : u * 128 + 128]
            return acc

        acc = lax.fori_loop(0, 4096 // CHUNK, expo, fe)
        scale = 1.0 / jnp.sum(acc, axis=-1, keepdims=True)

        def value(j, out):
            at = pl.ds(pl.multiple_of(j * CHUNK, CHUNK), CHUNK)
            p = (sc[:, at] * scale).astype(BF16)
            return out + jnp.dot(p, vb[r, at, cols], preferred_element_type=F32)

        out = jnp.dot((fe * scale).astype(BF16), vf[:, cols], preferred_element_type=F32)
        out = lax.fori_loop(0, 4096 // CHUNK, value, out)
        os[r, gp, 0] = out[0:64, 0:128]
        os[r, gp, 1] = out[64:128, 128:256]
        return carry

    lax.fori_loop(0, 4, attend, 0)
    for h in range(4):
        for p in range(2):
            rows = slice(p * 32, p * 32 + 32)
            a = os[0, h // 2, h % 2, rows].reshape(4, 8, 128)
            b = os[1, h // 2, h % 2, rows].reshape(4, 8, 128)
            att[4 * h : 4 * h + 4, :, p * 256 : p * 256 + 128] = jnp.where(
                low, a, pltpu.roll(b, 4, 1)
            ).astype(BF16)
            att[4 * h : 4 * h + 4, :, p * 256 + 128 : p * 256 + 256] = jnp.where(
                low, pltpu.roll(a, 4, 1), b
            ).astype(BF16)

    ao = Copies(ao_s, ao_r)
    for i in range(1, 16):
        peer = lax.rem(w + i, 16)
        ao.send(i - 1, att.at[peer], g.at[n, w], (peer, n))
    g[n, w] = att[w]
    for i in range(1, 16):
        ao.take(i - 1, g.at[n, lax.rem(w - i + 16, 16)], other)

    gn = Copies(gn_s, gn_r)
    na, nb, nf = above * 2 + c, below * 2 + c, far * 2 + c
    lo, hi = pl.ds(0, 8), pl.ds(8, 8)
    gn.send(0, g.at[n], g.at[n], up)
    gn.send(1, g.at[n], g.at[n], down)
    gn.send(2, g.at[n], g.at[n], other)
    gn.take(0, g.at[nb], up)
    gn.send(3, g.at[nb, lo], g.at[nb, lo], up)
    gn.send(4, g.at[nb], g.at[nb], other)
    gn.take(1, g.at[na], up)
    gn.send(5, g.at[na, hi], g.at[na, hi], down)
    gn.send(6, g.at[na], g.at[na], other)
    gn.take(3, g.at[nf, lo], up)
    gn.take(5, g.at[nf, hi], up)
    gn.send(7, g.at[nf], g.at[nf], other)
    gn.take(2, g.at[y * 2 + 1 - c], up)
    gn.take(4, g.at[below * 2 + 1 - c], up)
    gn.take(6, g.at[above * 2 + 1 - c], up)
    gn.take(7, g.at[far * 2 + 1 - c], up)

    def regroup(i, carry):
        gm[i] = g[:, i].astype(F32).reshape(64, 512).astype(BF16)
        return carry

    lax.fori_loop(0, 16, regroup, 0)
    loads[4].wait()

    st, st2 = Copies(st_s, st_r), Copies(st2_s, st2_r)
    halves = (
        (0, lambda a, b: m4(z + b) * 4 + m4(x + a), along_x, along_z),
        (1, lambda a, b: m4(z + a) * 4 + m4(x + b), along_z, along_x),
    )
    top, bot = pl.ds(0, 32), pl.ds(32, 32)

    def product(h, index, a):
        lhs = jnp.concatenate([gm[index(a, b)] for b in OFFSETS], axis=0)
        cols = slice(h * 1024, h * 1024 + 1024)
        v = jnp.dot(lhs, wo[:, cols], preferred_element_type=F32)
        return v.reshape(4, 64, 1024)

    for h, index, to1, to2 in halves:
        v = product(h, index, 2)
        so[h, 0] = v[:, 0:32].astype(BF16)
        so[h, 1] = v[:, 32:64].astype(BF16)
        for q in range(4):
            st.send(h * 24 + q, so.at[h, 0, q], ro.at[h, 0, q], to1(1))
            st.send(h * 24 + 4 + q, so.at[h, 1, q], ro.at[h, 1, q], to1(-1))
    for h, index, to1, to2 in halves:
        v = product(h, index, 1)
        sn[h, 0, :, 32:64] = v[:, 32:64].astype(BF16)
        kp[h, 0] = v[:, 0:32]
        for q in range(4):
            st.send(h * 24 + 8 + q, sn.at[h, 0, q, bot], rn.at[h, 0, q, bot], to1(1))
        v = product(h, index, -1)
        sn[h, 1, :, 0:32] = v[:, 0:32].astype(BF16)
        kp[h, 1] = v[:, 32:64]
        for q in range(4):
            st.send(h * 24 + 12 + q, sn.at[h, 1, q, top], rn.at[h, 1, q, top], to1(-1))
    for h, index, to1, to2 in halves:
        km[h] = product(h, index, 0)
    for q in range(4):
        for h, index, to1, to2 in halves:
            st.take(h * 24 + q, ro.at[h, 0, q], to1(1))
            sn[h, 0, q, 0:32] = (kp[h, 0, q] + ro[h, 0, q].astype(F32)).astype(BF16)
            st.send(h * 24 + 16 + q, sn.at[h, 0, q, top], rn.at[h, 0, q, top], to1(1))
            st.take(h * 24 + 4 + q, ro.at[h, 1, q], to1(1))
            sn[h, 1, q, 32:64] = (kp[h, 1, q] + ro[h, 1, q].astype(F32)).astype(BF16)
            st.send(h * 24 + 20 + q, sn.at[h, 1, q, bot], rn.at[h, 1, q, bot], to1(-1))
    for q in range(4):
        for h, index, to1, to2 in halves:
            st.take(h * 24 + 8 + q, rn.at[h, 0, q, bot], to1(1))
            st.take(h * 24 + 12 + q, rn.at[h, 1, q, top], to1(1))
            st.take(h * 24 + 16 + q, rn.at[h, 0, q, top], to1(1))
            st.take(h * 24 + 20 + q, rn.at[h, 1, q, bot], to1(1))
            v = km[h, q] + rn[h, 0, q].astype(F32) + rn[h, 1, q].astype(F32)
            if q == 0:
                so2[h] = v.reshape(2, 32, 1024).astype(BF16)
                st2.send(h * 6 + 0, so2.at[h, 0], ro2.at[h, 0], to2(1))
                st2.send(h * 6 + 1, so2.at[h, 1], ro2.at[h, 1], to2(-1))
            elif q == 1:
                sn2[h, 0, 32:64] = v[32:64].astype(BF16)
                km[h, q] = v
                st2.send(h * 6 + 2, sn2.at[h, 0, bot], rn2.at[h, 0, bot], to2(1))
            elif q == 2:
                sn2[h, 1, 0:32] = v[0:32].astype(BF16)
                km[h, q] = v
                st2.send(h * 6 + 3, sn2.at[h, 1, top], rn2.at[h, 1, top], to2(-1))
            else:
                km[h, q] = v
        if q == 2:
            for h, index, to1, to2 in halves:
                st2.take(h * 6 + 0, ro2.at[h, 0], to1(1))
                sn2[h, 0, 0:32] = (km[h, 1, 0:32] + ro2[h, 0].astype(F32)).astype(BF16)
                st2.send(h * 6 + 4, sn2.at[h, 0, top], rn2.at[h, 0, top], to2(1))
                st2.take(h * 6 + 1, ro2.at[h, 1], to1(1))
                sn2[h, 1, 32:64] = (km[h, 2, 32:64] + ro2[h, 1].astype(F32)).astype(BF16)
                st2.send(h * 6 + 5, sn2.at[h, 1, bot], rn2.at[h, 1, bot], to2(-1))
    for h, index, to1, to2 in halves:
        st2.take(h * 6 + 2, rn2.at[h, 0, bot], to1(1))
        st2.take(h * 6 + 3, rn2.at[h, 1, top], to1(1))
        st2.take(h * 6 + 4, rn2.at[h, 0, top], to1(1))
        st2.take(h * 6 + 5, rn2.at[h, 1, bot], to1(1))
        for j in range(8):
            sub = slice(j * 128, j * 128 + 128)
            res[h * 8 + j] = (
                km[h, 3, :, sub] + rn2[h, 0, :, sub].astype(F32) + rn2[h, 1, :, sub].astype(F32)
            )
    for j in range(16):
        for t in range(4):
            out_ref[t, :, j * 128 : j * 128 + 128] = res[j, pl.ds(t, 16, stride=4), :].astype(BF16)
    for group in (sqc, ag, ex, rs, aa, ao, gn, st, st2):
        group.drain()


def local(inputs, norm_gain, w_query, w_keyval, w_out, key_cache, value_cache, lengths, positions):
    half = HD // 2
    freq = jnp.exp(-jnp.log(F32(500000.0)) * jnp.arange(half, dtype=F32) * 2.0 / (2 * half))
    pos = positions[:, None] + jnp.arange(STEPS, dtype=jnp.int32)[None, :]
    ang = (pos.astype(F32)[..., None] * freq).reshape(8, half)
    cos, sin = jnp.cos(ang), jnp.sin(ang)
    cos2 = jnp.concatenate([cos, cos], -1)
    sin2 = jnp.concatenate([-sin, sin], -1)

    dma = pltpu.SemaphoreType.DMA
    vm = pl.BlockSpec(memory_space=pltpu.VMEM)
    hbm = pl.BlockSpec(memory_space=pl.ANY)

    def b16(*shape):
        return pltpu.VMEM(shape, BF16)

    def f32(*shape):
        return pltpu.VMEM(shape, F32)

    attended, nk, nv = pl.pallas_call(
        layer_kernel,
        out_shape=(
            jax.ShapeDtypeStruct((4, 16, 2048), BF16),
            jax.ShapeDtypeStruct((8, 512), BF16),
            jax.ShapeDtypeStruct((8, 512), BF16),
        ),
        in_specs=[pl.BlockSpec(memory_space=pltpu.SMEM)] + [hbm] * 7 + [vm, vm],
        out_specs=(vm, vm, vm),
        scratch_shapes=[
            b16(4, 16, 2048), b16(1, 2048), b16(2048, 512), b16(64, 2048), b16(512, 2048),
            b16(2, 4096, 512), b16(2, 4096, 512),
            f32(16, 64, 128), f32(8, 128), f32(7, 8, 128), b16(4, 2, 4, 32, 2048),
            f32(2, 4, 16, 8, 576), f32(4, 16, 8, 576), f32(2, 4, 2, 8, 576),
            f32(2, 16, 8, 576), b16(16, 8, 576), b16(16, 8, 576),
            b16(2, 2, 128, 256), b16(128, 512), b16(128, 512), f32(128, 4096),
            f32(2, 2, 2, 64, 128), b16(16, 8, 512), b16(8, 16, 8, 512), b16(16, 64, 512),
            b16(2, 2, 4, 32, 1024), b16(2, 2, 4, 64, 1024),
            b16(2, 2, 4, 32, 1024), b16(2, 2, 4, 64, 1024),
            f32(2, 2, 4, 32, 1024), f32(2, 4, 64, 1024),
            b16(2, 2, 32, 1024), b16(2, 2, 64, 1024), b16(2, 2, 32, 1024), b16(2, 2, 64, 1024),
            f32(16, 64, 128),
            dma((7,)), dma((7,)), dma((7,)), dma((40,)), dma((40,)), dma((4,)), dma((4,)),
            dma((24,)), dma((24,)), dma((16,)), dma((16,)), dma((15,)), dma((15,)),
            dma((8,)), dma((8,)), dma((48,)), dma((48,)), dma((12,)), dma((12,)),
        ],
        compiler_params=pltpu.CompilerParams(
            collective_id=0, has_side_effects=True, vmem_limit_bytes=60 << 20
        ),
        name="layer",
    )(
        lengths, inputs, norm_gain.reshape(1, 2048), w_query, w_keyval.T, w_out,
        key_cache, value_cache, cos2, sin2,
    )

    def by_step(a):
        return a.reshape(2, STEPS, KVH * HD).transpose(1, 0, 2)

    return attended, by_step(nk), by_step(nv)


def solution(mesh):
    return jax.shard_map(
        local,
        mesh=mesh,
        in_specs=(
            P(None, "wide", "narrow"),
            P("narrow"),
            P("narrow", "wide"),
            P("narrow", "wide"),
            P("wide", "narrow"),
            P(("wide", "narrow"), None, None),
            P(("wide", "narrow"), None, None),
            P(("wide", "narrow")),
            P(("wide", "narrow")),
        ),
        out_specs=(
            P(None, "wide", "narrow"),
            P(None, ("wide", "narrow"), None),
            P(None, ("wide", "narrow"), None),
        ),
        check_vma=False,
    )
```

```python
import jax
import jax.numpy as jnp
import numpy as np
from jax import lax
from jax.experimental import pallas as pl
from jax.experimental.pallas import tpu as pltpu
from jax.sharding import PartitionSpec as P

D = 16384
HQ = 64
KVH = 4
HD = 128
STEPS = 4
F32 = jnp.float32
BF16 = jnp.bfloat16
MESH = pl.DeviceIdType.MESH
NT = (((1,), (1,)), ((), ()))
CHUNK = 2048

SLOTS = (
    ((0, 0), (-1, 0), (1, 0), (2, 0)),
    ((-1, -1), (-1, 1), (1, -1), (1, 1)),
    ((0, -1), (0, 1), (2, -1), (2, 1)),
    ((0, 2), (-1, 2), (1, 2), (2, 2)),
)
WHERE = {(a % 4, b % 4): (g, s) for g, row in enumerate(SLOTS) for s, (a, b) in enumerate(row)}
OFFSETS = (2, 1, -1, 0)
FREQ = np.exp(
    -np.log(np.float32(500000.0)) * np.arange(64, dtype=np.float32) * np.float32(2.0) / np.float32(128)
)


def m4(v):
    return lax.rem(v + 8, 4)


def rcopy(src, dst, ssem, rsem, target):
    return pltpu.make_async_remote_copy(
        src_ref=src,
        dst_ref=dst,
        send_sem=ssem,
        recv_sem=rsem,
        device_id=target,
        device_id_type=MESH,
    )


class Copies:
    def __init__(self, ssem, rsem):
        self.ssem, self.rsem, self.sent = ssem, rsem, []

    def send(self, k, src, dst, target):
        c = rcopy(src, dst, self.ssem.at[k], self.rsem.at[k], target)
        c.start()
        self.sent.append(c)

    def take(self, k, dst, target):
        rcopy(dst, dst, self.ssem.at[k], self.rsem.at[k], target).wait_recv()

    def drain(self):
        for c in self.sent:
            c.wait_send()


def gather_half(cp, k0, buf, r, h, to1, to2):
    full, lo, hi = pl.ds(0, 2048), pl.ds(0, 1024), pl.ds(1024, 1024)

    def at(a, b, cols):
        g, s = WHERE[(a % 4, b % 4)]
        return buf.at[r, g, h, s, :, cols]

    def send1(k, a, b, cols, d):
        cp.send(k0 + k, at(a, b, cols), at(a - d, b, cols), to1(d))

    def send2(k, a, b, cols, d):
        cp.send(k0 + k, at(a, b, cols), at(a, b - d, cols), to2(d))

    def take(k, a, b, cols):
        cp.take(k0 + k, at(a, b, cols), to1(1))

    def spread(j, a):
        send2(4 + 4 * j, a, 0, full, 1)
        send2(5 + 4 * j, a, 0, full, -1)

    def onward(j, a):
        take(4 + 4 * j, a, -1, full)
        send2(6 + 4 * j, a, -1, lo, 1)
        take(5 + 4 * j, a, 1, full)
        send2(7 + 4 * j, a, 1, hi, -1)

    def last(j, a):
        take(6 + 4 * j, a, 2, lo)
        take(7 + 4 * j, a, 2, hi)

    def s0():
        send1(0, 0, 0, full, 1)
        send1(1, 0, 0, full, -1)

    def s1():
        spread(0, 0)

    def s2():
        take(0, -1, 0, full)
        send1(2, -1, 0, lo, 1)
        take(1, 1, 0, full)
        send1(3, 1, 0, hi, -1)
        spread(1, -1)
        spread(2, 1)

    def s3():
        onward(0, 0)

    def s4():
        take(2, 2, 0, lo)
        take(3, 2, 0, hi)
        spread(3, 2)

    def s5():
        onward(1, -1)
        onward(2, 1)

    def s6():
        last(0, 0)
        onward(3, 2)

    def s7():
        last(1, -1)
        last(2, 1)
        last(3, 2)

    return [s0, s1, s2, s3, s4, s5, s6, s7]


def zip_rows(a, b):
    low = lax.broadcasted_iota(jnp.int32, (1,) * (a.ndim - 2) + (8, a.shape[-1]), a.ndim - 2) < 4
    axis = a.ndim - 2
    return (
        jnp.where(low, a, pltpu.roll(b, 4, axis)),
        jnp.where(low, pltpu.roll(a, 4, axis), b),
    )


def layer_kernel(
    len_ref, pos_ref, x_hbm, gain_hbm, wq_hbm, wkv_hbm, wo_hbm, k_hbm, v_hbm,
    out_ref, nk, nv,
    xv, gain, wq, wkv, wo, kb, vb,
    xs, sq, sqr, buf, part, pair, ring_o, ring_n, qsend, qrecv, qx,
    qs, kf, vf, kvout, sc, att, g, gm,
    so, sn, ro, rn, kp, km, so2, sn2, ro2, rn2, res, rows16,
    ld, sq_s, sq_r, ag_s, ag_r, ex_s, ex_r, rs_s, rs_r, aa_s, aa_r,
    ao_s, ao_r, gn_s, gn_r, st_s, st_r, st2_s, st2_r,
):
    w = lax.axis_index("wide")
    n = lax.axis_index("narrow")
    z, x, y, c = w // 4, lax.rem(w, 4), n // 2, lax.rem(n, 2)

    def along_x(d):
        return (z * 4 + m4(x + d), n)

    def along_z(d):
        return (m4(z + d) * 4 + x, n)

    other = (w, y * 2 + (1 - c))
    up, down = (w, m4(y + 1) * 2 + c), (w, m4(y - 1) * 2 + c)
    far, above, below = m4(y + 2), m4(y + 1), m4(y - 1)

    barrier = pltpu.get_barrier_semaphore()
    for i in range(1, 8):
        pl.semaphore_signal(
            barrier, inc=1, device_id=(w, lax.rem(n + i, 8)), device_id_type=MESH
        )
    for d in (1, -1):
        pl.semaphore_signal(barrier, inc=1, device_id=along_x(d), device_id_type=MESH)
        pl.semaphore_signal(barrier, inc=1, device_id=along_z(d), device_id_type=MESH)

    pairs = [(x_hbm, xv), (gain_hbm, gain), (wq_hbm, wq), (wkv_hbm, wkv), (wo_hbm, wo)]
    pairs += [(k_hbm, kb), (v_hbm, vb)]
    loads = [pltpu.make_async_copy(s, d, ld.at[i]) for i, (s, d) in enumerate(pairs)]
    for load in loads[:5]:
        load.start()
    qs[...] = jnp.zeros_like(qs)
    kf[...] = jnp.zeros_like(kf)
    vf[...] = jnp.zeros_like(vf)
    loads[0].wait()
    acc = jnp.zeros((64, 128), F32)
    for j in range(16):
        cols = slice(j * 128, j * 128 + 128)
        for t in range(4):
            xs[j, pl.ds(t, 16, stride=4), :] = xv[t, :, cols].astype(F32)
        acc = acc + xs[j] * xs[j]
    row = jnp.sum(acc, axis=-1, keepdims=True)
    diag = lax.broadcasted_iota(jnp.int32, (64, 128), 0) == lax.broadcasted_iota(
        jnp.int32, (64, 128), 1
    )
    flat = jnp.sum(jnp.where(diag, row, 0.0), axis=0, keepdims=True)
    sq[...] = jnp.broadcast_to(flat, (8, 128))
    pl.semaphore_wait(barrier, 11)

    sqc = Copies(sq_s, sq_r)
    for i in range(1, 8):
        sqc.send(i - 1, sq, sqr.at[i - 1], (w, lax.rem(n + i, 8)))
    loads[5].start()
    loads[6].start()

    spot = lax.rem(lax.broadcasted_iota(jnp.int32, (8, 128), 1), 64)
    freq = jnp.zeros((8, 128), F32)
    for i in range(64):
        freq = jnp.where(spot == i, F32(FREQ[i]), freq)
    later = lax.rem(lax.broadcasted_iota(jnp.int32, (8, 128), 0), 4)
    left = lax.broadcasted_iota(jnp.int32, (8, 128), 1) < 64
    turns = []
    for r in range(2):
        angle = (later + pos_ref[r]).astype(F32) * freq
        sine = jnp.sin(angle)
        turns.append((jnp.cos(angle), jnp.where(left, -sine, sine)))

    for i in range(1, 8):
        sqc.take(i - 1, sqr.at[i - 1], other)
    total = sq[...]
    for i in range(7):
        total = total + sqr[i]
    column = jnp.sum(
        jnp.where(diag, jnp.broadcast_to(total[0:1], (64, 128)), 0.0), axis=-1, keepdims=True
    )
    inv = lax.rsqrt(column / D + 1e-05)
    loads[1].wait()
    for j in range(16):
        cols = slice(j * 128, j * 128 + 128)
        own = (xs[j] * inv * gain[cols].astype(F32).reshape(1, 128)).reshape(4, 2, 8, 128)
        for r, v in enumerate(zip_rows(own[:, 0], own[:, 1])):
            v = v.reshape(32, 128).astype(BF16)
            buf[r, 0, 0, 0, :, cols] = v[0:16]
            buf[r, 0, 1, 0, :, cols] = v[16:32]

    ag = Copies(ag_s, ag_r)
    ways = [
        [
            gather_half(ag, r * 40, buf, r, 0, along_x, along_z),
            gather_half(ag, r * 40 + 20, buf, r, 1, along_z, along_x),
        ]
        for r in range(2)
    ]

    def gather(r, *steps):
        for i in steps:
            ways[r][0][i]()
            ways[r][1][i]()

    ex, rs, aa = Copies(ex_s, ex_r), Copies(rs_s, rs_r), Copies(aa_s, aa_r)

    def multiply(r, m):
        lhs = buf[r, 2 * m : 2 * m + 2].reshape(256, 2048)
        q = jnp.dot(lhs, wq[...], preferred_element_type=F32)
        kv = lax.dot_general(lhs, wkv[...], NT, preferred_element_type=F32)
        for cols, v in ((slice(0, 512), q), (slice(512, 576), kv)):
            v = v.reshape(2, 2, 2, 2, 2, 8, v.shape[-1])
            for h in range(2):
                for yy in range(2):
                    a = v[:, h, :, 0, yy].reshape(4, 8, v.shape[-1])
                    b = v[:, h, :, 1, yy].reshape(4, 8, v.shape[-1])
                    for cc, tile in enumerate(zip_rows(a, b)):
                        part[r, cc, h * 2 + yy, 4 * m : 4 * m + 4, :, cols] = tile
        at = pl.ds(4 * m, 4)
        ex.send(2 * r + m, part.at[r, 1 - c, :, at], pair.at[r, :, at], other)

    def ring1(r, m):
        k = 6 * (2 * r + m)
        at, lo, hi = pl.ds(4 * m, 4), pl.ds(4 * m, 2), pl.ds(4 * m + 2, 2)
        ex.take(2 * r + m, pair.at[r, :, at], other)
        part[r, c, :, at] = part[r, c, :, at] + pair[r, :, at]
        rs.send(k + 0, part.at[r, c, far, lo], ring_o.at[r, 0, m], up)
        rs.send(k + 1, part.at[r, c, far, hi], ring_o.at[r, 1, m], down)
        rs.send(k + 2, part.at[r, c, above, hi], ring_n.at[r, 0, hi], up)
        rs.send(k + 3, part.at[r, c, below, lo], ring_n.at[r, 1, lo], down)

    def ring2(r, m):
        k = 6 * (2 * r + m)
        lo, hi = pl.ds(4 * m, 2), pl.ds(4 * m + 2, 2)
        rs.take(k + 0, ring_o.at[r, 0, m], up)
        part[r, c, above, lo] = part[r, c, above, lo] + ring_o[r, 0, m]
        rs.send(k + 4, part.at[r, c, above, lo], ring_n.at[r, 0, lo], up)
        rs.take(k + 1, ring_o.at[r, 1, m], up)
        part[r, c, below, hi] = part[r, c, below, hi] + ring_o[r, 1, m]
        rs.send(k + 5, part.at[r, c, below, hi], ring_n.at[r, 1, hi], down)

    def shift(a, b):
        return jnp.where(y < 2, b, a), jnp.where(y < 2, a, b)

    def finish(r, m):
        k = 6 * (2 * r + m)
        at, lo, hi = pl.ds(4 * m, 4), pl.ds(4 * m, 2), pl.ds(4 * m + 2, 2)
        rs.take(k + 2, ring_n.at[r, 0, hi], up)
        rs.take(k + 3, ring_n.at[r, 1, lo], up)
        rs.take(k + 4, ring_n.at[r, 0, lo], up)
        rs.take(k + 5, ring_n.at[r, 1, hi], up)
        qsend[r, at] = (part[r, c, y, at] + ring_n[r, 0, at] + ring_n[r, 1, at]).astype(BF16)
        for i in (2 * m, 2 * m + 1):
            for s, (a, b) in enumerate(SLOTS[i]):
                k = 4 * i + s
                if k == 0:
                    qrecv[r, 0] = qsend[r, 0]
                    continue
                dz, dx = shift(a, b)
                target = (m4(z + dz) * 4 + m4(x + dx), n)
                aa.send(16 * r + k, qsend.at[r, k // 2], qrecv.at[r, k], target)

    def receive(r):
        for i in range(4):
            for s, (a, b) in enumerate(SLOTS[i]):
                k = 4 * i + s
                if k:
                    aa.take(16 * r + k, qrecv.at[r, k], other)
                dz, dx = shift(a, b)
                tile = qrecv[r, k].astype(F32)
                if s % 2:
                    tile = pltpu.roll(tile, 4, 0)
                qx[m4(z - dz) * 4 + m4(x - dx)] = tile
        cos, sin = turns[r]

        def turn(v):
            return (v * cos + pltpu.roll(v, 64, v.ndim - 1) * sin).astype(BF16)

        low = lax.broadcasted_iota(jnp.int32, (1, 8, 128), 1) < 4
        for p in range(2):
            a = turn(qx[:, :, p * 256 : p * 256 + 128]).astype(F32)
            b = turn(qx[:, :, p * 256 + 128 : p * 256 + 256]).astype(F32)
            tile = jnp.where(low, a, pltpu.roll(b, 4, 1))
            for h in range(4):
                gi = h % 2
                qs[h // 2, gi * 64 + p * 32 : gi * 64 + p * 32 + 32,
                   gi * 128 : gi * 128 + 128] = (
                    tile[4 * h : 4 * h + 4].reshape(32, 128).astype(BF16)
                )
        for h in range(4):
            cols = slice(h * 128, h * 128 + 128)
            key = jnp.concatenate([qx[2 * h, :, 512:576], qx[2 * h + 1, :, 512:576]], -1)
            val = jnp.concatenate([qx[2 * h + 8, :, 512:576], qx[2 * h + 9, :, 512:576]], -1)
            key = turn(key)
            kf[0:8, cols] = key
            vf[0:8, cols] = val.astype(BF16)
            kvout[r, 0, :, cols] = key.astype(F32)
            kvout[r, 1, :, cols] = val

    factor = 1.0 / jnp.sqrt(F32(HD))

    def attend(r, gp):
        lane = lax.broadcasted_iota(jnp.int32, (128, 128), 1)
        step = lax.rem(lax.broadcasted_iota(jnp.int32, (128, 128), 0), 4)
        place = lax.broadcasted_iota(jnp.int32, (128, CHUNK), 1)
        q = qs[gp]
        cols = pl.ds(gp * 256, 256)
        length = len_ref[r]
        fs = lax.dot_general(q, kf[:, cols], NT, preferred_element_type=F32) * factor
        fs = jnp.where(lane <= step, fs, -jnp.inf)

        def score(j, top):
            at = pl.ds(pl.multiple_of(j * CHUNK, CHUNK), CHUNK)
            s = lax.dot_general(q, kb[r, at, cols], NT, preferred_element_type=F32) * factor
            s = jnp.where(place < length - j * CHUNK, s, -jnp.inf)
            sc[:, at] = s
            for u in range(CHUNK // 128):
                top = jnp.maximum(top, s[:, u * 128 : u * 128 + 128])
            return top

        top = lax.fori_loop(0, 4096 // CHUNK, score, fs)
        top = jnp.max(top, axis=-1, keepdims=True)
        fe = jnp.exp(fs - top)

        def expo(j, acc):
            at = pl.ds(pl.multiple_of(j * CHUNK, CHUNK), CHUNK)
            e = jnp.exp(sc[:, at] - top)
            sc[:, at] = e
            for u in range(CHUNK // 128):
                acc = acc + e[:, u * 128 : u * 128 + 128]
            return acc

        acc = lax.fori_loop(0, 4096 // CHUNK, expo, fe)
        scale = 1.0 / jnp.sum(acc, axis=-1, keepdims=True)

        def value(j, out):
            at = pl.ds(pl.multiple_of(j * CHUNK, CHUNK), CHUNK)
            p = (sc[:, at] * scale).astype(BF16)
            return out + jnp.dot(p, vb[r, at, cols], preferred_element_type=F32)

        out = jnp.dot((fe * scale).astype(BF16), vf[:, cols], preferred_element_type=F32)
        out = lax.fori_loop(0, 4096 // CHUNK, value, out)
        for gi in range(2):
            v = out[gi * 64 : gi * 64 + 64, gi * 128 : gi * 128 + 128].reshape(2, 4, 8, 128)
            h = 2 * gp + gi
            att[r, 4 * h : 4 * h + 4, :, 0:128] = v[0].astype(BF16)
            att[r, 4 * h : 4 * h + 4, :, 128:256] = v[1].astype(BF16)

    ao, gn = Copies(ao_s, ao_r), Copies(gn_s, gn_r)
    na, nb, nf = above * 2 + c, below * 2 + c, far * 2 + c
    lo8, hi8 = pl.ds(0, 8), pl.ds(8, 8)

    def spread_heads(r):
        for i in range(1, 16):
            peer = lax.rem(w + i, 16)
            ao.send(15 * r + i - 1, att.at[r, peer], g.at[r, n, w], (peer, n))
        g[r, n, w] = att[r, w]

    def narrow1(r):
        k = 8 * r
        for i in range(1, 16):
            ao.take(15 * r + i - 1, g.at[r, n, lax.rem(w - i + 16, 16)], other)
        gn.send(k + 0, g.at[r, n], g.at[r, n], up)
        gn.send(k + 1, g.at[r, n], g.at[r, n], down)
        gn.send(k + 2, g.at[r, n], g.at[r, n], other)

    def narrow2(r):
        k = 8 * r
        gn.take(k + 0, g.at[r, nb], up)
        gn.send(k + 3, g.at[r, nb, lo8], g.at[r, nb, lo8], up)
        gn.send(k + 4, g.at[r, nb], g.at[r, nb], other)
        gn.take(k + 1, g.at[r, na], up)
        gn.send(k + 5, g.at[r, na, hi8], g.at[r, na, hi8], down)
        gn.send(k + 6, g.at[r, na], g.at[r, na], other)

    def narrow3(r):
        k = 8 * r
        gn.take(k + 3, g.at[r, nf, lo8], up)
        gn.take(k + 5, g.at[r, nf, hi8], up)
        gn.send(k + 7, g.at[r, nf], g.at[r, nf], other)
        gn.take(k + 2, g.at[r, y * 2 + 1 - c], up)
        gn.take(k + 4, g.at[r, below * 2 + 1 - c], up)
        gn.take(k + 6, g.at[r, above * 2 + 1 - c], up)
        gn.take(k + 7, g.at[r, far * 2 + 1 - c], up)

        def regroup(i, carry):
            v = g[r, :, i].astype(F32).reshape(4, 2, 8, 256)
            for hl, tile in enumerate(zip_rows(v[:, 0], v[:, 1])):
                tile = tile.reshape(32, 256).astype(BF16)
                for p in range(2):
                    at = p * 256 + hl * 128
                    gm[i, :, at : at + 128] = tile[:, p * 128 : p * 128 + 128]
            return carry

        lax.fori_loop(0, 16, regroup, 0)

    st, st2 = Copies(st_s, st_r), Copies(st2_s, st2_r)
    halves = (
        (0, lambda a, b: m4(z + b) * 4 + m4(x + a), along_x, along_z),
        (1, lambda a, b: m4(z + a) * 4 + m4(x + b), along_z, along_x),
    )
    top16, bot16 = pl.ds(0, 16), pl.ds(16, 16)
    two = (pl.ds(0, 2), pl.ds(2, 2))

    def product(h, index, a):
        lhs = jnp.concatenate([gm[index(a, b)] for b in OFFSETS], axis=0)
        cols = slice(h * 1024, h * 1024 + 1024)
        v = jnp.dot(lhs, wo[:, cols], preferred_element_type=F32)
        return v.reshape(4, 32, 1024)

    def products(r):
        for h, index, to1, to2 in halves:
            k = 24 * r + 12 * h
            v = product(h, index, 2)
            so[r, h, 0] = v[:, 0:16].astype(BF16)
            so[r, h, 1] = v[:, 16:32].astype(BF16)
            for u, q in enumerate(two):
                st.send(k + u, so.at[r, h, 0, q], ro.at[r, h, 0, q], to1(1))
                st.send(k + 2 + u, so.at[r, h, 1, q], ro.at[r, h, 1, q], to1(-1))
        for h, index, to1, to2 in halves:
            k = 24 * r + 12 * h
            v = product(h, index, 1)
            sn[r, h, 0, :, 16:32] = v[:, 16:32].astype(BF16)
            kp[r, h, 0] = v[:, 0:16]
            for u, q in enumerate(two):
                st.send(
                    k + 4 + u, sn.at[r, h, 0, q, bot16], rn.at[r, h, 0, q, bot16], to1(1)
                )
            v = product(h, index, -1)
            sn[r, h, 1, :, 0:16] = v[:, 0:16].astype(BF16)
            kp[r, h, 1] = v[:, 16:32]
            for u, q in enumerate(two):
                st.send(
                    k + 6 + u, sn.at[r, h, 1, q, top16], rn.at[r, h, 1, q, top16], to1(-1)
                )
        for h, index, to1, to2 in halves:
            km[r, h] = product(h, index, 0)

    def relay(r):
        for u, q in enumerate(two):
            qq = slice(2 * u, 2 * u + 2)
            for h, index, to1, to2 in halves:
                k = 24 * r + 12 * h
                st.take(k + u, ro.at[r, h, 0, q], to1(1))
                sn[r, h, 0, qq, 0:16] = (
                    kp[r, h, 0, qq] + ro[r, h, 0, qq].astype(F32)
                ).astype(BF16)
                st.send(k + 8 + u, sn.at[r, h, 0, q, top16], rn.at[r, h, 0, q, top16], to1(1))
                st.take(k + 2 + u, ro.at[r, h, 1, q], to1(1))
                sn[r, h, 1, qq, 16:32] = (
                    kp[r, h, 1, qq] + ro[r, h, 1, qq].astype(F32)
                ).astype(BF16)
                st.send(k + 10 + u, sn.at[r, h, 1, q, bot16], rn.at[r, h, 1, q, bot16], to1(-1))

    def second(r):
        for u, q in enumerate(two):
            for h, index, to1, to2 in halves:
                k, k2 = 24 * r + 12 * h, 12 * r + 6 * h
                st.take(k + 4 + u, rn.at[r, h, 0, q, bot16], to1(1))
                st.take(k + 6 + u, rn.at[r, h, 1, q, top16], to1(1))
                st.take(k + 8 + u, rn.at[r, h, 0, q, top16], to1(1))
                st.take(k + 10 + u, rn.at[r, h, 1, q, bot16], to1(1))
                for i in (2 * u, 2 * u + 1):
                    v = km[r, h, i] + rn[r, h, 0, i].astype(F32) + rn[r, h, 1, i].astype(F32)
                    if i == 0:
                        so2[r, h] = v.reshape(2, 16, 1024).astype(BF16)
                        st2.send(k2 + 0, so2.at[r, h, 0], ro2.at[r, h, 0], to2(1))
                        st2.send(k2 + 1, so2.at[r, h, 1], ro2.at[r, h, 1], to2(-1))
                        continue
                    km[r, h, i] = v
                    if i == 1:
                        sn2[r, h, 0, 16:32] = v[16:32].astype(BF16)
                        st2.send(k2 + 2, sn2.at[r, h, 0, bot16], rn2.at[r, h, 0, bot16], to2(1))
                    elif i == 2:
                        sn2[r, h, 1, 0:16] = v[0:16].astype(BF16)
                        st2.send(k2 + 3, sn2.at[r, h, 1, top16], rn2.at[r, h, 1, top16], to2(-1))
        for h, index, to1, to2 in halves:
            k2 = 12 * r + 6 * h
            st2.take(k2 + 0, ro2.at[r, h, 0], to1(1))
            sn2[r, h, 0, 0:16] = (km[r, h, 1, 0:16] + ro2[r, h, 0].astype(F32)).astype(BF16)
            st2.send(k2 + 4, sn2.at[r, h, 0, top16], rn2.at[r, h, 0, top16], to2(1))
            st2.take(k2 + 1, ro2.at[r, h, 1], to1(1))
            sn2[r, h, 1, 16:32] = (km[r, h, 2, 16:32] + ro2[r, h, 1].astype(F32)).astype(BF16)
            st2.send(k2 + 5, sn2.at[r, h, 1, bot16], rn2.at[r, h, 1, bot16], to2(-1))

    def total_rows(r):
        for h, index, to1, to2 in halves:
            k2 = 12 * r + 6 * h
            st2.take(k2 + 2, rn2.at[r, h, 0, bot16], to1(1))
            st2.take(k2 + 3, rn2.at[r, h, 1, top16], to1(1))
            st2.take(k2 + 4, rn2.at[r, h, 0, top16], to1(1))
            st2.take(k2 + 5, rn2.at[r, h, 1, bot16], to1(1))
            for j in range(8):
                sub = slice(j * 128, j * 128 + 128)
                res[h * 8 + j] = (
                    km[r, h, 3, :, sub]
                    + rn2[r, h, 0, :, sub].astype(F32)
                    + rn2[r, h, 1, :, sub].astype(F32)
                )
        for j in range(16):
            for t in range(4):
                rows16[j, t, pl.ds(r, 8, stride=2), :] = res[j, pl.ds(t, 8, stride=4), :]

    gather(0, 0, 1, 2, 3, 4, 5)
    loads[2].wait()
    loads[3].wait()
    multiply(0, 0)
    gather(1, 0, 1)
    gather(0, 6)
    ring1(0, 0)
    gather(0, 7)
    multiply(0, 1)
    gather(1, 2, 3)
    ring2(0, 0)
    ring1(0, 1)
    gather(1, 4, 5)
    finish(0, 0)
    ring2(0, 1)
    multiply(1, 0)
    gather(1, 6)
    finish(0, 1)
    ring1(1, 0)
    gather(1, 7)
    multiply(1, 1)
    ring2(1, 0)
    receive(0)
    ring1(1, 1)
    loads[5].wait()
    loads[6].wait()
    attend(0, 0)
    finish(1, 0)
    ring2(1, 1)
    attend(0, 1)
    spread_heads(0)
    finish(1, 1)
    narrow1(0)
    receive(1)
    attend(1, 0)
    narrow2(0)
    attend(1, 1)
    spread_heads(1)
    loads[4].wait()
    narrow3(0)
    products(0)
    narrow1(1)
    relay(0)
    narrow2(1)
    narrow3(1)
    products(1)
    second(0)
    relay(1)
    total_rows(0)
    second(1)
    total_rows(1)
    for j in range(16):
        for t in range(4):
            out_ref[t, :, j * 128 : j * 128 + 128] = rows16[j, t].astype(BF16)
    nk[...] = zip_rows(kvout[0, 0], kvout[1, 0])[0].astype(BF16)
    nv[...] = zip_rows(kvout[0, 1], kvout[1, 1])[0].astype(BF16)
    for group in (sqc, ag, ex, rs, aa, ao, gn, st, st2):
        group.drain()


def local(inputs, norm_gain, w_query, w_keyval, w_out, key_cache, value_cache, lengths, positions):
    dma = pltpu.SemaphoreType.DMA
    vm = pl.BlockSpec(memory_space=pltpu.VMEM)
    sm = pl.BlockSpec(memory_space=pltpu.SMEM)
    hbm = pl.BlockSpec(memory_space=pl.ANY)

    def b16(*shape):
        return pltpu.VMEM(shape, BF16)

    def f32(*shape):
        return pltpu.VMEM(shape, F32)

    attended, nk, nv = pl.pallas_call(
        layer_kernel,
        out_shape=(
            jax.ShapeDtypeStruct((4, 16, 2048), BF16),
            jax.ShapeDtypeStruct((8, 512), BF16),
            jax.ShapeDtypeStruct((8, 512), BF16),
        ),
        in_specs=[sm, sm] + [hbm] * 7,
        out_specs=(vm, vm, vm),
        scratch_shapes=[
            b16(4, 16, 2048), b16(2048), b16(2048, 512), b16(64, 2048), b16(512, 2048),
            b16(2, 4096, 512), b16(2, 4096, 512),
            f32(16, 64, 128), f32(8, 128), f32(7, 8, 128), b16(2, 4, 2, 4, 16, 2048),
            f32(2, 2, 4, 8, 8, 576), f32(2, 4, 8, 8, 576), f32(2, 2, 2, 2, 8, 576),
            f32(2, 2, 8, 8, 576), b16(2, 8, 8, 576), b16(2, 16, 8, 576), f32(16, 8, 576),
            b16(2, 128, 256), b16(128, 512), b16(128, 512), f32(2, 2, 8, 512), f32(128, 4096),
            b16(2, 16, 8, 256), b16(2, 8, 16, 8, 256), b16(16, 32, 512),
            b16(2, 2, 2, 4, 16, 1024), b16(2, 2, 2, 4, 32, 1024),
            b16(2, 2, 2, 4, 16, 1024), b16(2, 2, 2, 4, 32, 1024),
            f32(2, 2, 2, 4, 16, 1024), f32(2, 2, 4, 32, 1024),
            b16(2, 2, 2, 16, 1024), b16(2, 2, 2, 32, 1024),
            b16(2, 2, 2, 16, 1024), b16(2, 2, 2, 32, 1024),
            f32(16, 32, 128), f32(16, 4, 16, 128),
            dma((7,)), dma((7,)), dma((7,)), dma((80,)), dma((80,)), dma((4,)), dma((4,)),
            dma((24,)), dma((24,)), dma((32,)), dma((32,)), dma((30,)), dma((30,)),
            dma((16,)), dma((16,)), dma((48,)), dma((48,)), dma((24,)), dma((24,)),
        ],
        compiler_params=pltpu.CompilerParams(
            collective_id=0, has_side_effects=True, vmem_limit_bytes=60 << 20
        ),
        name="layer",
    )(
        lengths, positions, inputs, norm_gain, w_query, w_keyval.T, w_out,
        key_cache, value_cache,
    )

    def by_step(a):
        return a.reshape(2, STEPS, KVH * HD).transpose(1, 0, 2)

    return attended, by_step(nk), by_step(nv)


def solution(mesh):
    return jax.shard_map(
        local,
        mesh=mesh,
        in_specs=(
            P(None, "wide", "narrow"),
            P("narrow"),
            P("narrow", "wide"),
            P("narrow", "wide"),
            P("wide", "narrow"),
            P(("wide", "narrow"), None, None),
            P(("wide", "narrow"), None, None),
            P(("wide", "narrow")),
            P(("wide", "narrow")),
        ),
        out_specs=(
            P(None, "wide", "narrow"),
            P(None, ("wide", "narrow"), None),
            P(None, ("wide", "narrow"), None),
        ),
        check_vma=False,
    )
```

```python
import jax
import jax.numpy as jnp
import numpy as np
from jax import lax
from jax.experimental import pallas as pl
from jax.experimental.pallas import tpu as pltpu
from jax.sharding import PartitionSpec as P

D = 16384
HQ = 64
KVH = 4
HD = 128
STEPS = 4
F32 = jnp.float32
BF16 = jnp.bfloat16
MESH = pl.DeviceIdType.MESH
NT = (((1,), (1,)), ((), ()))
CHUNK = 2048

SLOTS = (
    ((0, 0), (-1, 0), (1, 0), (2, 0)),
    ((-1, -1), (-1, 1), (1, -1), (1, 1)),
    ((0, -1), (0, 1), (2, -1), (2, 1)),
    ((0, 2), (-1, 2), (1, 2), (2, 2)),
)
WHERE = {(a % 4, b % 4): (g, s) for g, row in enumerate(SLOTS) for s, (a, b) in enumerate(row)}
OFFSETS = (2, 1, -1, 0)
FREQ = np.exp(
    -np.log(np.float32(500000.0)) * np.arange(64, dtype=np.float32) * np.float32(2.0) / np.float32(128)
)


def m4(v):
    return lax.rem(v + 8, 4)


def rcopy(src, dst, ssem, rsem, target):
    return pltpu.make_async_remote_copy(
        src_ref=src,
        dst_ref=dst,
        send_sem=ssem,
        recv_sem=rsem,
        device_id=target,
        device_id_type=MESH,
    )


class Copies:
    def __init__(self, ssem, rsem):
        self.ssem, self.rsem, self.sent = ssem, rsem, []

    def send(self, k, src, dst, target):
        c = rcopy(src, dst, self.ssem.at[k], self.rsem.at[k], target)
        c.start()
        self.sent.append(c)

    def take(self, k, dst, target):
        rcopy(dst, dst, self.ssem.at[k], self.rsem.at[k], target).wait_recv()

    def drain(self):
        for c in self.sent:
            c.wait_send()


def gather_half(cp, k0, buf, r, h, to1, to2):
    full, lo, hi = pl.ds(0, 2048), pl.ds(0, 1024), pl.ds(1024, 1024)

    def at(a, b, cols):
        g, s = WHERE[(a % 4, b % 4)]
        return buf.at[r, g, h, s, :, cols]

    def send1(k, a, b, cols, d):
        cp.send(k0 + k, at(a, b, cols), at(a - d, b, cols), to1(d))

    def send2(k, a, b, cols, d):
        cp.send(k0 + k, at(a, b, cols), at(a, b - d, cols), to2(d))

    def take(k, a, b, cols):
        cp.take(k0 + k, at(a, b, cols), to1(1))

    def spread(j, a):
        send2(4 + 4 * j, a, 0, full, 1)
        send2(5 + 4 * j, a, 0, full, -1)

    def onward(j, a):
        take(4 + 4 * j, a, -1, full)
        send2(6 + 4 * j, a, -1, lo, 1)
        take(5 + 4 * j, a, 1, full)
        send2(7 + 4 * j, a, 1, hi, -1)

    def last(j, a):
        take(6 + 4 * j, a, 2, lo)
        take(7 + 4 * j, a, 2, hi)

    def s0():
        send1(0, 0, 0, full, 1)
        send1(1, 0, 0, full, -1)

    def s1():
        spread(0, 0)

    def s2():
        take(0, -1, 0, full)
        send1(2, -1, 0, lo, 1)
        take(1, 1, 0, full)
        send1(3, 1, 0, hi, -1)
        spread(1, -1)
        spread(2, 1)

    def s3():
        onward(0, 0)

    def s4():
        take(2, 2, 0, lo)
        take(3, 2, 0, hi)
        spread(3, 2)

    def s5():
        onward(1, -1)
        onward(2, 1)

    def s6():
        last(0, 0)
        onward(3, 2)

    def s7():
        last(1, -1)
        last(2, 1)
        last(3, 2)

    return [s0, s1, s2, s3, s4, s5, s6, s7]


def zip_rows(a, b):
    low = lax.broadcasted_iota(jnp.int32, (1,) * (a.ndim - 2) + (8, a.shape[-1]), a.ndim - 2) < 4
    axis = a.ndim - 2
    return (
        jnp.where(low, a, pltpu.roll(b, 4, axis)),
        jnp.where(low, pltpu.roll(a, 4, axis), b),
    )


def layer_kernel(
    len_ref, pos_ref, x_hbm, gain_hbm, wq_hbm, wkv_hbm, wo_hbm, k_hbm, v_hbm,
    out_hbm, nk_hbm, nv_hbm,
    out_ref, nk, nv, xv, gain, wq, wkv, wo, kb, vb,
    xs, sq, sqr, buf, part, pair, ring_o, ring_n, qsend, qrecv, qx,
    qs, kf, vf, kvout, sc, att, g, gm,
    so, sn, ro, rn, kp, km, so2, sn2, ro2, rn2, res, rows16,
    ld, sq_s, sq_r, ag_s, ag_r, ex_s, ex_r, rs_s, rs_r, aa_s, aa_r,
    ao_s, ao_r, gn_s, gn_r, st_s, st_r, st2_s, st2_r,
):
    w = lax.axis_index("wide")
    n = lax.axis_index("narrow")
    z, x, y, c = w // 4, lax.rem(w, 4), n // 2, lax.rem(n, 2)

    def along_x(d):
        return (z * 4 + m4(x + d), n)

    def along_z(d):
        return (m4(z + d) * 4 + x, n)

    other = (w, y * 2 + (1 - c))
    up, down = (w, m4(y + 1) * 2 + c), (w, m4(y - 1) * 2 + c)
    up2, down2 = (w, m4(y + 1) * 2 + 1 - c), (w, m4(y - 1) * 2 + 1 - c)
    far, above, below = m4(y + 2), m4(y + 1), m4(y - 1)

    barrier = pltpu.get_barrier_semaphore()
    for i in range(1, 8):
        pl.semaphore_signal(
            barrier, inc=1, device_id=(w, lax.rem(n + i, 8)), device_id_type=MESH
        )
    for d in (1, -1):
        pl.semaphore_signal(barrier, inc=1, device_id=along_x(d), device_id_type=MESH)
        pl.semaphore_signal(barrier, inc=1, device_id=along_z(d), device_id_type=MESH)

    pairs = [(x_hbm, xv), (gain_hbm, gain), (wq_hbm, wq), (wkv_hbm, wkv), (wo_hbm, wo)]
    pairs += [(k_hbm, kb), (v_hbm, vb)]
    loads = [pltpu.make_async_copy(s, d, ld.at[i]) for i, (s, d) in enumerate(pairs)]
    for load in loads[:5]:
        load.start()
    qs[...] = jnp.zeros_like(qs)
    kf[...] = jnp.zeros_like(kf)
    vf[...] = jnp.zeros_like(vf)
    loads[0].wait()
    acc = jnp.zeros((64, 128), F32)
    for j in range(16):
        cols = slice(j * 128, j * 128 + 128)
        for t in range(4):
            xs[j, pl.ds(t, 16, stride=4), :] = xv[t, :, cols].astype(F32)
        acc = acc + xs[j] * xs[j]
    row = jnp.sum(acc, axis=-1, keepdims=True)
    diag = lax.broadcasted_iota(jnp.int32, (64, 128), 0) == lax.broadcasted_iota(
        jnp.int32, (64, 128), 1
    )
    flat = jnp.sum(jnp.where(diag, row, 0.0), axis=0, keepdims=True)
    sq[...] = jnp.broadcast_to(flat, (8, 128))
    pl.semaphore_wait(barrier, 11)

    sqc = Copies(sq_s, sq_r)
    for i in range(1, 8):
        sqc.send(i - 1, sq, sqr.at[i - 1], (w, lax.rem(n + i, 8)))
    loads[5].start()
    loads[6].start()

    spot = lax.rem(lax.broadcasted_iota(jnp.int32, (8, 128), 1), 64)
    freq = jnp.zeros((8, 128), F32)
    for i in range(64):
        freq = jnp.where(spot == i, F32(FREQ[i]), freq)
    later = lax.rem(lax.broadcasted_iota(jnp.int32, (8, 128), 0), 4)
    left = lax.broadcasted_iota(jnp.int32, (8, 128), 1) < 64
    turns = []
    for r in range(2):
        angle = (later + pos_ref[r]).astype(F32) * freq
        sine = jnp.sin(angle)
        turns.append((jnp.cos(angle), jnp.where(left, -sine, sine)))

    for i in range(1, 8):
        sqc.take(i - 1, sqr.at[i - 1], other)
    total = sq[...]
    for i in range(7):
        total = total + sqr[i]
    column = jnp.sum(
        jnp.where(diag, jnp.broadcast_to(total[0:1], (64, 128)), 0.0), axis=-1, keepdims=True
    )
    inv = lax.rsqrt(column / D + 1e-05)
    loads[1].wait()
    for j in range(16):
        cols = slice(j * 128, j * 128 + 128)
        own = (xs[j] * inv * gain[cols].astype(F32).reshape(1, 128)).reshape(4, 2, 8, 128)
        for r, v in enumerate(zip_rows(own[:, 0], own[:, 1])):
            v = v.reshape(32, 128).astype(BF16)
            buf[r, 0, 0, 0, :, cols] = v[0:16]
            buf[r, 0, 1, 0, :, cols] = v[16:32]

    ag = Copies(ag_s, ag_r)
    ways = [
        [
            gather_half(ag, r * 40, buf, r, 0, along_x, along_z),
            gather_half(ag, r * 40 + 20, buf, r, 1, along_z, along_x),
        ]
        for r in range(2)
    ]

    def gather(r, *steps):
        for i in steps:
            ways[r][0][i]()
            ways[r][1][i]()

    ex, rs, aa = Copies(ex_s, ex_r), Copies(rs_s, rs_r), Copies(aa_s, aa_r)

    def multiply(r, m):
        lhs = buf[r, 2 * m : 2 * m + 2].reshape(256, 2048)
        q = jnp.dot(lhs, wq[...], preferred_element_type=F32)
        kv = lax.dot_general(lhs, wkv[...], NT, preferred_element_type=F32)
        for cols, v in ((slice(0, 512), q), (slice(512, 576), kv)):
            v = v.reshape(2, 2, 2, 2, 2, 8, v.shape[-1])
            for h in range(2):
                for yy in range(2):
                    a = v[:, h, :, 0, yy].reshape(4, 8, v.shape[-1])
                    b = v[:, h, :, 1, yy].reshape(4, 8, v.shape[-1])
                    for cc, tile in enumerate(zip_rows(a, b)):
                        part[r, cc, h * 2 + yy, 4 * m : 4 * m + 4, :, cols] = tile
        at = pl.ds(4 * m, 4)
        ex.send(2 * r + m, part.at[r, 1 - c, :, at], pair.at[r, :, at], other)

    def ring1(r, m):
        k = 6 * (2 * r + m)
        at, lo, hi = pl.ds(4 * m, 4), pl.ds(4 * m, 2), pl.ds(4 * m + 2, 2)
        ex.take(2 * r + m, pair.at[r, :, at], other)
        part[r, c, :, at] = part[r, c, :, at] + pair[r, :, at]
        rs.send(k + 0, part.at[r, c, far, lo], ring_o.at[r, 0, m], up)
        rs.send(k + 1, part.at[r, c, far, hi], ring_o.at[r, 1, m], down)
        rs.send(k + 2, part.at[r, c, above, hi], ring_n.at[r, 0, hi], up)
        rs.send(k + 3, part.at[r, c, below, lo], ring_n.at[r, 1, lo], down)

    def ring2(r, m):
        k = 6 * (2 * r + m)
        lo, hi = pl.ds(4 * m, 2), pl.ds(4 * m + 2, 2)
        rs.take(k + 0, ring_o.at[r, 0, m], up)
        part[r, c, above, lo] = part[r, c, above, lo] + ring_o[r, 0, m]
        rs.send(k + 4, part.at[r, c, above, lo], ring_n.at[r, 0, lo], up)
        rs.take(k + 1, ring_o.at[r, 1, m], up)
        part[r, c, below, hi] = part[r, c, below, hi] + ring_o[r, 1, m]
        rs.send(k + 5, part.at[r, c, below, hi], ring_n.at[r, 1, hi], down)

    def shift(a, b):
        return jnp.where(y < 2, b, a), jnp.where(y < 2, a, b)

    def finish(r, m):
        k = 6 * (2 * r + m)
        at, lo, hi = pl.ds(4 * m, 4), pl.ds(4 * m, 2), pl.ds(4 * m + 2, 2)
        rs.take(k + 2, ring_n.at[r, 0, hi], up)
        rs.take(k + 3, ring_n.at[r, 1, lo], up)
        rs.take(k + 4, ring_n.at[r, 0, lo], up)
        rs.take(k + 5, ring_n.at[r, 1, hi], up)
        qsend[r, at] = (part[r, c, y, at] + ring_n[r, 0, at] + ring_n[r, 1, at]).astype(BF16)
        for i in (2 * m, 2 * m + 1):
            for s, (a, b) in enumerate(SLOTS[i]):
                k = 4 * i + s
                if k == 0:
                    qrecv[r, 0] = qsend[r, 0]
                    continue
                dz, dx = shift(a, b)
                target = (m4(z + dz) * 4 + m4(x + dx), n)
                aa.send(16 * r + k, qsend.at[r, k // 2], qrecv.at[r, k], target)

    def receive(r):
        for i in range(4):
            for s, (a, b) in enumerate(SLOTS[i]):
                k = 4 * i + s
                if k:
                    aa.take(16 * r + k, qrecv.at[r, k], other)
                dz, dx = shift(a, b)
                tile = qrecv[r, k].astype(F32)
                if s % 2:
                    tile = pltpu.roll(tile, 4, 0)
                qx[m4(z - dz) * 4 + m4(x - dx)] = tile
        cos, sin = turns[r]

        def turn(v):
            return (v * cos + pltpu.roll(v, 64, v.ndim - 1) * sin).astype(BF16)

        low = lax.broadcasted_iota(jnp.int32, (1, 8, 128), 1) < 4
        for p in range(2):
            a = turn(qx[:, :, p * 256 : p * 256 + 128]).astype(F32)
            b = turn(qx[:, :, p * 256 + 128 : p * 256 + 256]).astype(F32)
            tile = jnp.where(low, a, pltpu.roll(b, 4, 1))
            for h in range(4):
                gi = h % 2
                qs[h // 2, gi * 64 + p * 32 : gi * 64 + p * 32 + 32,
                   gi * 128 : gi * 128 + 128] = (
                    tile[4 * h : 4 * h + 4].reshape(32, 128).astype(BF16)
                )
        for h in range(4):
            cols = slice(h * 128, h * 128 + 128)
            key = jnp.concatenate([qx[2 * h, :, 512:576], qx[2 * h + 1, :, 512:576]], -1)
            val = jnp.concatenate([qx[2 * h + 8, :, 512:576], qx[2 * h + 9, :, 512:576]], -1)
            key = turn(key)
            kf[0:8, cols] = key
            vf[0:8, cols] = val.astype(BF16)
            kvout[0, h, pl.ds(r, 4, stride=2), :] = key.astype(F32)[0:4]
            kvout[1, h, pl.ds(r, 4, stride=2), :] = val[0:4]

    factor = 1.0 / jnp.sqrt(F32(HD))

    def attend(r, gp):
        lane = lax.broadcasted_iota(jnp.int32, (128, 128), 1)
        step = lax.rem(lax.broadcasted_iota(jnp.int32, (128, 128), 0), 4)
        place = lax.broadcasted_iota(jnp.int32, (128, CHUNK), 1)
        q = qs[gp]
        cols = pl.ds(gp * 256, 256)
        length = len_ref[r]
        fs = lax.dot_general(q, kf[:, cols], NT, preferred_element_type=F32) * factor
        fs = jnp.where(lane <= step, fs, -jnp.inf)

        def score(j, top):
            at = pl.ds(pl.multiple_of(j * CHUNK, CHUNK), CHUNK)
            s = lax.dot_general(q, kb[r, at, cols], NT, preferred_element_type=F32) * factor
            s = jnp.where(place < length - j * CHUNK, s, -jnp.inf)
            sc[:, at] = s
            for u in range(CHUNK // 128):
                top = jnp.maximum(top, s[:, u * 128 : u * 128 + 128])
            return top

        top = lax.fori_loop(0, 4096 // CHUNK, score, fs)
        top = jnp.max(top, axis=-1, keepdims=True)
        fe = jnp.exp(fs - top)

        def expo(j, acc):
            at = pl.ds(pl.multiple_of(j * CHUNK, CHUNK), CHUNK)
            e = jnp.exp(sc[:, at] - top)
            sc[:, at] = e
            for u in range(CHUNK // 128):
                acc = acc + e[:, u * 128 : u * 128 + 128]
            return acc

        acc = lax.fori_loop(0, 4096 // CHUNK, expo, fe)
        scale = 1.0 / jnp.sum(acc, axis=-1, keepdims=True)

        def value(j, out):
            at = pl.ds(pl.multiple_of(j * CHUNK, CHUNK), CHUNK)
            p = (sc[:, at] * scale).astype(BF16)
            return out + jnp.dot(p, vb[r, at, cols], preferred_element_type=F32)

        out = jnp.dot((fe * scale).astype(BF16), vf[:, cols], preferred_element_type=F32)
        out = lax.fori_loop(0, 4096 // CHUNK, value, out)
        for gi in range(2):
            v = out[gi * 64 : gi * 64 + 64, gi * 128 : gi * 128 + 128].reshape(2, 4, 8, 128)
            h = 2 * gp + gi
            att[r, 4 * h : 4 * h + 4, :, 0:128] = v[0].astype(BF16)
            att[r, 4 * h : 4 * h + 4, :, 128:256] = v[1].astype(BF16)

    ao, gn = Copies(ao_s, ao_r), Copies(gn_s, gn_r)
    na, nb, nf = above * 2 + c, below * 2 + c, far * 2 + c
    lo8, hi8 = pl.ds(0, 8), pl.ds(8, 8)

    def spread_heads(r):
        for i in range(1, 16):
            peer = lax.rem(w + i, 16)
            ao.send(15 * r + i - 1, att.at[r, peer], g.at[r, n, w], (peer, n))
        g[r, n, w] = att[r, w]

    def narrow1(r):
        k = 10 * r
        for i in range(1, 16):
            ao.take(15 * r + i - 1, g.at[r, n, lax.rem(w - i + 16, 16)], other)
        gn.send(k + 0, g.at[r, n], g.at[r, n], up)
        gn.send(k + 1, g.at[r, n], g.at[r, n], down)
        gn.send(k + 2, g.at[r, n], g.at[r, n], other)

    def narrow2(r):
        k = 10 * r
        gn.take(k + 0, g.at[r, nb], up)
        gn.send(k + 3, g.at[r, nb, lo8], g.at[r, nb, lo8], up)
        gn.send(k + 8, g.at[r, nb, lo8], g.at[r, nb, lo8], up2)
        gn.send(k + 4, g.at[r, nb], g.at[r, nb], other)
        gn.take(k + 1, g.at[r, na], up)
        gn.send(k + 5, g.at[r, na, hi8], g.at[r, na, hi8], down)
        gn.send(k + 9, g.at[r, na, hi8], g.at[r, na, hi8], down2)
        gn.send(k + 6, g.at[r, na], g.at[r, na], other)

    def narrow3(r):
        k = 10 * r
        gn.take(k + 3, g.at[r, nf, lo8], up)
        gn.take(k + 5, g.at[r, nf, hi8], up)
        gn.take(k + 2, g.at[r, y * 2 + 1 - c], up)
        gn.take(k + 4, g.at[r, below * 2 + 1 - c], up)
        gn.take(k + 6, g.at[r, above * 2 + 1 - c], up)
        gn.take(k + 8, g.at[r, far * 2 + 1 - c, lo8], up)
        gn.take(k + 9, g.at[r, far * 2 + 1 - c, hi8], up)

        def regroup(i, carry):
            v = g[r, :, i].astype(F32).reshape(4, 2, 8, 256)
            for hl, tile in enumerate(zip_rows(v[:, 0], v[:, 1])):
                tile = tile.reshape(32, 256).astype(BF16)
                for p in range(2):
                    at = p * 256 + hl * 128
                    gm[i, :, at : at + 128] = tile[:, p * 128 : p * 128 + 128]
            return carry

        lax.fori_loop(0, 16, regroup, 0)

    st, st2 = Copies(st_s, st_r), Copies(st2_s, st2_r)
    halves = (
        (0, lambda a, b: m4(z + b) * 4 + m4(x + a), along_x, along_z),
        (1, lambda a, b: m4(z + a) * 4 + m4(x + b), along_z, along_x),
    )
    top16, bot16 = pl.ds(0, 16), pl.ds(16, 16)
    two = (pl.ds(0, 2), pl.ds(2, 2))

    def product(h, index, a):
        lhs = jnp.concatenate([gm[index(a, b)] for b in OFFSETS], axis=0)
        cols = slice(h * 1024, h * 1024 + 1024)
        v = jnp.dot(lhs, wo[:, cols], preferred_element_type=F32)
        return v.reshape(4, 32, 1024)

    def products(r):
        for h, index, to1, to2 in halves:
            k = 24 * r + 12 * h
            v = product(h, index, 2)
            so[r, h, 0] = v[:, 0:16].astype(BF16)
            so[r, h, 1] = v[:, 16:32].astype(BF16)
            for u, q in enumerate(two):
                st.send(k + u, so.at[r, h, 0, q], ro.at[r, h, 0, q], to1(1))
                st.send(k + 2 + u, so.at[r, h, 1, q], ro.at[r, h, 1, q], to1(-1))
        for h, index, to1, to2 in halves:
            k = 24 * r + 12 * h
            v = product(h, index, 1)
            sn[r, h, 0, :, 16:32] = v[:, 16:32].astype(BF16)
            kp[r, h, 0] = v[:, 0:16]
            for u, q in enumerate(two):
                st.send(
                    k + 4 + u, sn.at[r, h, 0, q, bot16], rn.at[r, h, 0, q, bot16], to1(1)
                )
            v = product(h, index, -1)
            sn[r, h, 1, :, 0:16] = v[:, 0:16].astype(BF16)
            kp[r, h, 1] = v[:, 16:32]
            for u, q in enumerate(two):
                st.send(
                    k + 6 + u, sn.at[r, h, 1, q, top16], rn.at[r, h, 1, q, top16], to1(-1)
                )
        for h, index, to1, to2 in halves:
            km[r, h] = product(h, index, 0)

    def relay(r):
        for u, q in enumerate(two):
            qq = slice(2 * u, 2 * u + 2)
            for h, index, to1, to2 in halves:
                k = 24 * r + 12 * h
                st.take(k + u, ro.at[r, h, 0, q], to1(1))
                sn[r, h, 0, qq, 0:16] = (
                    kp[r, h, 0, qq] + ro[r, h, 0, qq].astype(F32)
                ).astype(BF16)
                st.send(k + 8 + u, sn.at[r, h, 0, q, top16], rn.at[r, h, 0, q, top16], to1(1))
                st.take(k + 2 + u, ro.at[r, h, 1, q], to1(1))
                sn[r, h, 1, qq, 16:32] = (
                    kp[r, h, 1, qq] + ro[r, h, 1, qq].astype(F32)
                ).astype(BF16)
                st.send(k + 10 + u, sn.at[r, h, 1, q, bot16], rn.at[r, h, 1, q, bot16], to1(-1))

    def second(r):
        for u, q in enumerate(two):
            for h, index, to1, to2 in halves:
                k, k2 = 24 * r + 12 * h, 12 * r + 6 * h
                st.take(k + 4 + u, rn.at[r, h, 0, q, bot16], to1(1))
                st.take(k + 6 + u, rn.at[r, h, 1, q, top16], to1(1))
                st.take(k + 8 + u, rn.at[r, h, 0, q, top16], to1(1))
                st.take(k + 10 + u, rn.at[r, h, 1, q, bot16], to1(1))
                for i in (2 * u, 2 * u + 1):
                    v = km[r, h, i] + rn[r, h, 0, i].astype(F32) + rn[r, h, 1, i].astype(F32)
                    if i == 0:
                        so2[r, h] = v.reshape(2, 16, 1024).astype(BF16)
                        st2.send(k2 + 0, so2.at[r, h, 0], ro2.at[r, h, 0], to2(1))
                        st2.send(k2 + 1, so2.at[r, h, 1], ro2.at[r, h, 1], to2(-1))
                        continue
                    km[r, h, i] = v
                    if i == 1:
                        sn2[r, h, 0, 16:32] = v[16:32].astype(BF16)
                        st2.send(k2 + 2, sn2.at[r, h, 0, bot16], rn2.at[r, h, 0, bot16], to2(1))
                    elif i == 2:
                        sn2[r, h, 1, 0:16] = v[0:16].astype(BF16)
                        st2.send(k2 + 3, sn2.at[r, h, 1, top16], rn2.at[r, h, 1, top16], to2(-1))

    def relay2(r):
        for h, index, to1, to2 in halves:
            k2 = 12 * r + 6 * h
            st2.take(k2 + 0, ro2.at[r, h, 0], to1(1))
            sn2[r, h, 0, 0:16] = (km[r, h, 1, 0:16] + ro2[r, h, 0].astype(F32)).astype(BF16)
            st2.send(k2 + 4, sn2.at[r, h, 0, top16], rn2.at[r, h, 0, top16], to2(1))
            st2.take(k2 + 1, ro2.at[r, h, 1], to1(1))
            sn2[r, h, 1, 16:32] = (km[r, h, 2, 16:32] + ro2[r, h, 1].astype(F32)).astype(BF16)
            st2.send(k2 + 5, sn2.at[r, h, 1, bot16], rn2.at[r, h, 1, bot16], to2(-1))

    def total_rows(r):
        for h, index, to1, to2 in halves:
            k2 = 12 * r + 6 * h
            st2.take(k2 + 2, rn2.at[r, h, 0, bot16], to1(1))
            st2.take(k2 + 3, rn2.at[r, h, 1, top16], to1(1))
            st2.take(k2 + 4, rn2.at[r, h, 0, top16], to1(1))
            st2.take(k2 + 5, rn2.at[r, h, 1, bot16], to1(1))
            for j in range(8):
                sub = slice(j * 128, j * 128 + 128)
                res[h * 8 + j] = (
                    km[r, h, 3, :, sub]
                    + rn2[r, h, 0, :, sub].astype(F32)
                    + rn2[r, h, 1, :, sub].astype(F32)
                )
            for j in range(h * 8, h * 8 + 8):
                for t in range(4):
                    rows16[j, t, pl.ds(r, 8, stride=2), :] = res[j, pl.ds(t, 8, stride=4), :]
            if r == 1:
                for j in range(h * 8, h * 8 + 8):
                    for t in range(4):
                        out_ref[t, :, j * 128 : j * 128 + 128] = rows16[j, t].astype(BF16)
                cols = pl.ds(h * 1024, 1024)
                store = pltpu.make_async_copy(
                    out_ref.at[:, :, cols], out_hbm.at[:, :, cols], ld.at[9 + h]
                )
                store.start()
                stores.append(store)

    def new_rows():
        for t in range(4):
            for h in range(4):
                cols = slice(h * 128, h * 128 + 128)
                nk[t, :, cols] = kvout[0, h, 2 * t : 2 * t + 2].astype(BF16)
                nv[t, :, cols] = kvout[1, h, 2 * t : 2 * t + 2].astype(BF16)
        for i, (source, target) in enumerate(((nk, nk_hbm), (nv, nv_hbm))):
            store = pltpu.make_async_copy(source, target, ld.at[7 + i])
            store.start()
            stores.append(store)

    stores = []

    gather(0, 0, 1, 2)
    gather(1, 0, 1)
    gather(0, 3, 4)
    gather(1, 2)
    gather(0, 5)
    loads[2].wait()
    loads[3].wait()
    multiply(0, 0)
    gather(1, 3)
    gather(0, 6)
    gather(1, 4)
    ring1(0, 0)
    gather(0, 7)
    multiply(0, 1)
    gather(1, 5)
    ring2(0, 0)
    multiply(1, 0)
    gather(1, 6)
    finish(0, 0)
    ring1(0, 1)
    gather(1, 7)
    multiply(1, 1)
    ring1(1, 0)
    ring2(0, 1)
    ring2(1, 0)
    finish(0, 1)
    ring1(1, 1)
    finish(1, 0)
    ring2(1, 1)
    receive(0)
    loads[5].wait()
    loads[6].wait()
    attend(0, 0)
    finish(1, 1)
    attend(0, 1)
    spread_heads(0)
    receive(1)
    attend(1, 0)
    narrow1(0)
    attend(1, 1)
    spread_heads(1)
    new_rows()
    narrow2(0)
    loads[4].wait()
    narrow3(0)
    products(0)
    narrow1(1)
    relay(0)
    narrow2(1)
    narrow3(1)
    second(0)
    products(1)
    relay(1)
    relay2(0)
    second(1)
    total_rows(0)
    relay2(1)
    total_rows(1)
    for store in stores:
        store.wait()
    for group in (sqc, ag, ex, rs, aa, ao, gn, st, st2):
        group.drain()


def local(inputs, norm_gain, w_query, w_keyval, w_out, key_cache, value_cache, lengths, positions):
    dma = pltpu.SemaphoreType.DMA
    sm = pl.BlockSpec(memory_space=pltpu.SMEM)
    hbm = pl.BlockSpec(memory_space=pltpu.HBM)

    def b16(*shape):
        return pltpu.VMEM(shape, BF16)

    def f32(*shape):
        return pltpu.VMEM(shape, F32)

    return pl.pallas_call(
        layer_kernel,
        out_shape=(
            jax.ShapeDtypeStruct((4, 16, 2048), BF16),
            jax.ShapeDtypeStruct((4, 2, 512), BF16),
            jax.ShapeDtypeStruct((4, 2, 512), BF16),
        ),
        in_specs=[sm, sm] + [hbm] * 7,
        out_specs=(hbm, hbm, hbm),
        scratch_shapes=[
            b16(4, 16, 2048), b16(4, 2, 512), b16(4, 2, 512),
            b16(4, 16, 2048), b16(2048), b16(2048, 512), b16(64, 2048), b16(512, 2048),
            b16(2, 4096, 512), b16(2, 4096, 512),
            f32(16, 64, 128), f32(8, 128), f32(7, 8, 128), b16(2, 4, 2, 4, 16, 2048),
            f32(2, 2, 4, 8, 8, 576), f32(2, 4, 8, 8, 576), f32(2, 2, 2, 2, 8, 576),
            f32(2, 2, 8, 8, 576), b16(2, 8, 8, 576), b16(2, 16, 8, 576), f32(16, 8, 576),
            b16(2, 128, 256), b16(128, 512), b16(128, 512), f32(2, 4, 8, 128), f32(128, 4096),
            b16(2, 16, 8, 256), b16(2, 8, 16, 8, 256), b16(16, 32, 512),
            b16(2, 2, 2, 4, 16, 1024), b16(2, 2, 2, 4, 32, 1024),
            b16(2, 2, 2, 4, 16, 1024), b16(2, 2, 2, 4, 32, 1024),
            f32(2, 2, 2, 4, 16, 1024), f32(2, 2, 4, 32, 1024),
            b16(2, 2, 2, 16, 1024), b16(2, 2, 2, 32, 1024),
            b16(2, 2, 2, 16, 1024), b16(2, 2, 2, 32, 1024),
            f32(16, 32, 128), f32(16, 4, 16, 128),
            dma((11,)), dma((7,)), dma((7,)), dma((80,)), dma((80,)), dma((4,)), dma((4,)),
            dma((24,)), dma((24,)), dma((32,)), dma((32,)), dma((30,)), dma((30,)),
            dma((20,)), dma((20,)), dma((48,)), dma((48,)), dma((24,)), dma((24,)),
        ],
        compiler_params=pltpu.CompilerParams(
            collective_id=0, has_side_effects=True, vmem_limit_bytes=60 << 20
        ),
        name="layer",
    )(
        lengths, positions, inputs, norm_gain, w_query, w_keyval.T, w_out,
        key_cache, value_cache,
    )


def solution(mesh):
    return jax.shard_map(
        local,
        mesh=mesh,
        in_specs=(
            P(None, "wide", "narrow"),
            P("narrow"),
            P("narrow", "wide"),
            P("narrow", "wide"),
            P("wide", "narrow"),
            P(("wide", "narrow"), None, None),
            P(("wide", "narrow"), None, None),
            P(("wide", "narrow")),
            P(("wide", "narrow")),
        ),
        out_specs=(
            P(None, "wide", "narrow"),
            P(None, ("wide", "narrow"), None),
            P(None, ("wide", "narrow"), None),
        ),
        check_vma=False,
    )
```

```python
import jax
import jax.numpy as jnp
import numpy as np
from jax import lax
from jax.experimental import pallas as pl
from jax.experimental.pallas import tpu as pltpu
from jax.sharding import PartitionSpec as P

D = 16384
HQ = 64
KVH = 4
HD = 128
STEPS = 4
F32 = jnp.float32
BF16 = jnp.bfloat16
MESH = pl.DeviceIdType.MESH
NT = (((1,), (1,)), ((), ()))
CHUNK = 2048

SLOTS = (
    ((0, 0), (-1, 0), (1, 0), (2, 0)),
    ((-1, -1), (-1, 1), (1, -1), (1, 1)),
    ((0, -1), (0, 1), (2, -1), (2, 1)),
    ((0, 2), (-1, 2), (1, 2), (2, 2)),
)
WHERE = {(a % 4, b % 4): (g, s) for g, row in enumerate(SLOTS) for s, (a, b) in enumerate(row)}
OFFSETS = (2, 1, -1, 0)
FREQ = np.exp(
    -np.log(np.float32(500000.0)) * np.arange(64, dtype=np.float32) * np.float32(2.0) / np.float32(128)
)


def m4(v):
    return lax.rem(v + 8, 4)


def rcopy(src, dst, ssem, rsem, target):
    return pltpu.make_async_remote_copy(
        src_ref=src,
        dst_ref=dst,
        send_sem=ssem,
        recv_sem=rsem,
        device_id=target,
        device_id_type=MESH,
    )


class Copies:
    def __init__(self, ssem, rsem):
        self.ssem, self.rsem, self.sent = ssem, rsem, []

    def send(self, k, src, dst, target):
        c = rcopy(src, dst, self.ssem, self.rsem.at[k], target)
        c.start()
        self.sent.append(c)

    def take(self, k, dst, target):
        rcopy(dst, dst, self.ssem, self.rsem.at[k], target).wait_recv()

    def drain(self):
        for c in self.sent:
            c.wait_send()


def gather_half(cp, k0, buf, r, h, to1, to2):
    full, lo, hi = pl.ds(0, 2048), pl.ds(0, 1024), pl.ds(1024, 1024)

    def at(a, b, cols):
        g, s = WHERE[(a % 4, b % 4)]
        return buf.at[r, g, h, s, :, cols]

    def send1(k, a, b, cols, d):
        cp.send(k0 + k, at(a, b, cols), at(a - d, b, cols), to1(d))

    def send2(k, a, b, cols, d):
        cp.send(k0 + k, at(a, b, cols), at(a, b - d, cols), to2(d))

    def take(k, a, b, cols):
        cp.take(k0 + k, at(a, b, cols), to1(1))

    def spread(j, a):
        send2(3 + 3 * j, a, 0, full, 1)
        send2(4 + 3 * j, a, 0, full, -1)

    def onward(j, a):
        take(3 + 3 * j, a, -1, full)
        send2(5 + 3 * j, a, -1, lo, 1)
        take(4 + 3 * j, a, 1, full)
        send2(5 + 3 * j, a, 1, hi, -1)

    def last(j, a):
        take(5 + 3 * j, a, 2, full)

    def s0():
        send1(0, 0, 0, full, 1)
        send1(1, 0, 0, full, -1)

    def s1():
        spread(0, 0)

    def s2():
        take(0, -1, 0, full)
        send1(2, -1, 0, lo, 1)
        take(1, 1, 0, full)
        send1(2, 1, 0, hi, -1)
        spread(1, -1)
        spread(2, 1)

    def s3():
        onward(0, 0)

    def s4():
        take(2, 2, 0, full)
        spread(3, 2)

    def s5():
        onward(1, -1)
        onward(2, 1)

    def s6():
        last(0, 0)
        onward(3, 2)

    def s7():
        last(1, -1)
        last(2, 1)
        last(3, 2)

    return [s0, s1, s2, s3, s4, s5, s6, s7]


def zip_rows(a, b):
    low = lax.broadcasted_iota(jnp.int32, (1,) * (a.ndim - 2) + (8, a.shape[-1]), a.ndim - 2) < 4
    axis = a.ndim - 2
    return (
        jnp.where(low, a, pltpu.roll(b, 4, axis)),
        jnp.where(low, pltpu.roll(a, 4, axis), b),
    )


def layer_kernel(
    len_ref, pos_ref, x_hbm, gain_hbm, wq_hbm, wkv_hbm, wo_hbm, k_hbm, v_hbm,
    out_hbm, nk_hbm, nv_hbm,
    out_ref, nk, nv, xv, gain, wq, wkv, wo, kb, vb,
    xs, sq, sqr, buf, part, pair, ring_o, ring_n, qsend, qrecv, qx,
    qs, kf, vf, kvout, sc, att, g, gm,
    so, sn, ro, rn, kp, km, so2, sn2, ro2, rn2, res, rows16,
    ld, sq_s, sq_r, ag_s, ag_r, ex_s, ex_r, rs_s, rs_r, aa_s, aa_r,
    ao_s, ao_r, gn_s, gn_r, st_s, st_r, st2_s, st2_r,
):
    w = lax.axis_index("wide")
    n = lax.axis_index("narrow")
    z, x, y, c = w // 4, lax.rem(w, 4), n // 2, lax.rem(n, 2)

    def along_x(d):
        return (z * 4 + m4(x + d), n)

    def along_z(d):
        return (m4(z + d) * 4 + x, n)

    other = (w, y * 2 + (1 - c))
    up, down = (w, m4(y + 1) * 2 + c), (w, m4(y - 1) * 2 + c)
    up2, down2 = (w, m4(y + 1) * 2 + 1 - c), (w, m4(y - 1) * 2 + 1 - c)
    far, above, below = m4(y + 2), m4(y + 1), m4(y - 1)

    barrier = pltpu.get_barrier_semaphore()
    for i in range(1, 8):
        pl.semaphore_signal(
            barrier, inc=1, device_id=(w, lax.rem(n + i, 8)), device_id_type=MESH
        )
    for d in (1, -1):
        pl.semaphore_signal(barrier, inc=1, device_id=along_x(d), device_id_type=MESH)
        pl.semaphore_signal(barrier, inc=1, device_id=along_z(d), device_id_type=MESH)

    pairs = [(x_hbm, xv), (gain_hbm, gain), (wq_hbm, wq), (wkv_hbm, wkv), (wo_hbm, wo)]
    pairs += [(k_hbm, kb), (v_hbm, vb)]
    loads = [pltpu.make_async_copy(s, d, ld.at[i]) for i, (s, d) in enumerate(pairs)]
    for load in loads[:5]:
        load.start()
    qs[...] = jnp.zeros_like(qs)
    kf[...] = jnp.zeros_like(kf)
    vf[...] = jnp.zeros_like(vf)
    loads[0].wait()
    acc = jnp.zeros((64, 128), F32)
    for j in range(16):
        cols = slice(j * 128, j * 128 + 128)
        for t in range(4):
            xs[j, pl.ds(t, 16, stride=4), :] = xv[t, :, cols].astype(F32)
        acc = acc + xs[j] * xs[j]
    row = jnp.sum(acc, axis=-1, keepdims=True)
    diag = lax.broadcasted_iota(jnp.int32, (64, 128), 0) == lax.broadcasted_iota(
        jnp.int32, (64, 128), 1
    )
    flat = jnp.sum(jnp.where(diag, row, 0.0), axis=0, keepdims=True)
    sq[...] = jnp.broadcast_to(flat, (8, 128))
    pl.semaphore_wait(barrier, 11)

    sqc = Copies(sq_s, sq_r)
    for i in range(1, 8):
        sqc.send(0, sq, sqr.at[i - 1], (w, lax.rem(n + i, 8)))
    loads[5].start()
    loads[6].start()

    spot = lax.rem(lax.broadcasted_iota(jnp.int32, (8, 128), 1), 64)
    freq = jnp.zeros((8, 128), F32)
    for i in range(64):
        freq = jnp.where(spot == i, F32(FREQ[i]), freq)
    later = lax.rem(lax.broadcasted_iota(jnp.int32, (8, 128), 0), 4)
    left = lax.broadcasted_iota(jnp.int32, (8, 128), 1) < 64
    turns = []
    for r in range(2):
        angle = (later + pos_ref[r]).astype(F32) * freq
        sine = jnp.sin(angle)
        turns.append((jnp.cos(angle), jnp.where(left, -sine, sine)))

    sqc.take(0, sqr, other)
    total = sq[...]
    for i in range(7):
        total = total + sqr[i]
    column = jnp.sum(
        jnp.where(diag, jnp.broadcast_to(total[0:1], (64, 128)), 0.0), axis=-1, keepdims=True
    )
    inv = lax.rsqrt(column / D + 1e-05)
    loads[1].wait()
    for j in range(16):
        cols = slice(j * 128, j * 128 + 128)
        own = (xs[j] * inv * gain[cols].astype(F32).reshape(1, 128)).reshape(4, 2, 8, 128)
        for r, v in enumerate(zip_rows(own[:, 0], own[:, 1])):
            v = v.reshape(32, 128).astype(BF16)
            buf[r, 0, 0, 0, :, cols] = v[0:16]
            buf[r, 0, 1, 0, :, cols] = v[16:32]

    ag = Copies(ag_s, ag_r)
    ways = [
        [
            gather_half(ag, r * 30, buf, r, 0, along_x, along_z),
            gather_half(ag, r * 30 + 15, buf, r, 1, along_z, along_x),
        ]
        for r in range(2)
    ]

    def gather(r, *steps):
        for i in steps:
            ways[r][0][i]()
            ways[r][1][i]()

    ex, rs, aa = Copies(ex_s, ex_r), Copies(rs_s, rs_r), Copies(aa_s, aa_r)

    def multiply(r, m):
        lhs = buf[r, 2 * m : 2 * m + 2].reshape(256, 2048)
        q = jnp.dot(lhs, wq[...], preferred_element_type=F32)
        kv = lax.dot_general(lhs, wkv[...], NT, preferred_element_type=F32)
        for cols, v in ((slice(0, 512), q), (slice(512, 576), kv)):
            v = v.reshape(2, 2, 2, 2, 2, 8, v.shape[-1])
            for h in range(2):
                for yy in range(2):
                    a = v[:, h, :, 0, yy].reshape(4, 8, v.shape[-1])
                    b = v[:, h, :, 1, yy].reshape(4, 8, v.shape[-1])
                    for cc, tile in enumerate(zip_rows(a, b)):
                        part[r, cc, h * 2 + yy, 4 * m : 4 * m + 4, :, cols] = tile
        at = pl.ds(4 * m, 4)
        ex.send(2 * r + m, part.at[r, 1 - c, :, at], pair.at[r, :, at], other)

    def ring1(r, m):
        k = 3 * (2 * r + m)
        at, lo, hi = pl.ds(4 * m, 4), pl.ds(4 * m, 2), pl.ds(4 * m + 2, 2)
        ex.take(2 * r + m, pair.at[r, :, at], other)
        part[r, c, :, at] = part[r, c, :, at] + pair[r, :, at]
        rs.send(k + 0, part.at[r, c, far, lo], ring_o.at[r, 0, m], up)
        rs.send(k + 1, part.at[r, c, far, hi], ring_o.at[r, 1, m], down)
        rs.send(k + 2, part.at[r, c, above, hi], ring_n.at[r, 0, hi], up)
        rs.send(k + 2, part.at[r, c, below, lo], ring_n.at[r, 1, lo], down)

    def ring2(r, m):
        k = 3 * (2 * r + m)
        lo, hi = pl.ds(4 * m, 2), pl.ds(4 * m + 2, 2)
        rs.take(k + 0, ring_o.at[r, 0, m], up)
        part[r, c, above, lo] = part[r, c, above, lo] + ring_o[r, 0, m]
        rs.send(k + 2, part.at[r, c, above, lo], ring_n.at[r, 0, lo], up)
        rs.take(k + 1, ring_o.at[r, 1, m], up)
        part[r, c, below, hi] = part[r, c, below, hi] + ring_o[r, 1, m]
        rs.send(k + 2, part.at[r, c, below, hi], ring_n.at[r, 1, hi], down)

    def shift(a, b):
        return jnp.where(y < 2, b, a), jnp.where(y < 2, a, b)

    def finish(r, m):
        k = 3 * (2 * r + m)
        at = pl.ds(4 * m, 4)
        rs.take(k + 2, ring_n.at[r, :, at], up)
        qsend[r, at] = (part[r, c, y, at] + ring_n[r, 0, at] + ring_n[r, 1, at]).astype(BF16)
        for i in (2 * m, 2 * m + 1):
            for s, (a, b) in enumerate(SLOTS[i]):
                k = 4 * i + s
                if k == 0:
                    qrecv[r, 0] = qsend[r, 0]
                    continue
                dz, dx = shift(a, b)
                target = (m4(z + dz) * 4 + m4(x + dx), n)
                aa.send(r, qsend.at[r, k // 2], qrecv.at[r, k], target)

    def receive(r):
        aa.take(r, qrecv.at[r, pl.ds(1, 15)], other)
        for i in range(4):
            for s, (a, b) in enumerate(SLOTS[i]):
                k = 4 * i + s
                dz, dx = shift(a, b)
                tile = qrecv[r, k].astype(F32)
                if s % 2:
                    tile = pltpu.roll(tile, 4, 0)
                qx[m4(z - dz) * 4 + m4(x - dx)] = tile
        cos, sin = turns[r]

        def turn(v):
            return (v * cos + pltpu.roll(v, 64, v.ndim - 1) * sin).astype(BF16)

        low = lax.broadcasted_iota(jnp.int32, (1, 8, 128), 1) < 4
        for p in range(2):
            a = turn(qx[:, :, p * 256 : p * 256 + 128]).astype(F32)
            b = turn(qx[:, :, p * 256 + 128 : p * 256 + 256]).astype(F32)
            tile = jnp.where(low, a, pltpu.roll(b, 4, 1))
            for h in range(4):
                gi = h % 2
                qs[h // 2, gi * 64 + p * 32 : gi * 64 + p * 32 + 32,
                   gi * 128 : gi * 128 + 128] = (
                    tile[4 * h : 4 * h + 4].reshape(32, 128).astype(BF16)
                )
        for h in range(4):
            cols = slice(h * 128, h * 128 + 128)
            key = jnp.concatenate([qx[2 * h, :, 512:576], qx[2 * h + 1, :, 512:576]], -1)
            val = jnp.concatenate([qx[2 * h + 8, :, 512:576], qx[2 * h + 9, :, 512:576]], -1)
            key = turn(key)
            kf[0:8, cols] = key
            vf[0:8, cols] = val.astype(BF16)
            kvout[0, h, pl.ds(r, 4, stride=2), :] = key.astype(F32)[0:4]
            kvout[1, h, pl.ds(r, 4, stride=2), :] = val[0:4]

    factor = 1.0 / jnp.sqrt(F32(HD))

    def attend(r, gp):
        lane = lax.broadcasted_iota(jnp.int32, (128, 128), 1)
        step = lax.rem(lax.broadcasted_iota(jnp.int32, (128, 128), 0), 4)
        place = lax.broadcasted_iota(jnp.int32, (128, CHUNK), 1)
        q = qs[gp]
        cols = pl.ds(gp * 256, 256)
        length = len_ref[r]
        fs = lax.dot_general(q, kf[:, cols], NT, preferred_element_type=F32) * factor
        fs = jnp.where(lane <= step, fs, -jnp.inf)

        def score(j, top):
            at = pl.ds(pl.multiple_of(j * CHUNK, CHUNK), CHUNK)
            s = lax.dot_general(q, kb[r, at, cols], NT, preferred_element_type=F32) * factor
            s = jnp.where(place < length - j * CHUNK, s, -jnp.inf)
            sc[:, at] = s
            for u in range(CHUNK // 128):
                top = jnp.maximum(top, s[:, u * 128 : u * 128 + 128])
            return top

        top = lax.fori_loop(0, 4096 // CHUNK, score, fs)
        top = jnp.max(top, axis=-1, keepdims=True)
        fe = jnp.exp(fs - top)

        def expo(j, acc):
            at = pl.ds(pl.multiple_of(j * CHUNK, CHUNK), CHUNK)
            e = jnp.exp(sc[:, at] - top)
            sc[:, at] = e
            for u in range(CHUNK // 128):
                acc = acc + e[:, u * 128 : u * 128 + 128]
            return acc

        acc = lax.fori_loop(0, 4096 // CHUNK, expo, fe)
        scale = 1.0 / jnp.sum(acc, axis=-1, keepdims=True)

        def value(j, out):
            at = pl.ds(pl.multiple_of(j * CHUNK, CHUNK), CHUNK)
            p = (sc[:, at] * scale).astype(BF16)
            return out + jnp.dot(p, vb[r, at, cols], preferred_element_type=F32)

        out = jnp.dot((fe * scale).astype(BF16), vf[:, cols], preferred_element_type=F32)
        out = lax.fori_loop(0, 4096 // CHUNK, value, out)
        for gi in range(2):
            v = out[gi * 64 : gi * 64 + 64, gi * 128 : gi * 128 + 128].reshape(2, 4, 8, 128)
            h = 2 * gp + gi
            att[r, 4 * h : 4 * h + 4, :, 0:128] = v[0].astype(BF16)
            att[r, 4 * h : 4 * h + 4, :, 128:256] = v[1].astype(BF16)

    ao, gn = Copies(ao_s, ao_r), Copies(gn_s, gn_r)
    na, nb, nf = above * 2 + c, below * 2 + c, far * 2 + c
    lo8, hi8 = pl.ds(0, 8), pl.ds(8, 8)

    def spread_heads(r):
        for i in range(1, 16):
            peer = lax.rem(w + i, 16)
            ao.send(r, att.at[r, peer], g.at[r, n, w], (peer, n))
        g[r, n, w] = att[r, w]

    def narrow1(r):
        k = 3 * r
        ao.take(r, g.at[r, n, pl.ds(0, 15)], other)
        gn.send(k + 0, g.at[r, n], g.at[r, n], up)
        gn.send(k + 1, g.at[r, n], g.at[r, n], down)
        gn.send(k + 2, g.at[r, n], g.at[r, n], other)

    def narrow2(r):
        k = 3 * r
        gn.take(k + 0, g.at[r, nb], up)
        gn.send(k + 2, g.at[r, nb, lo8], g.at[r, nb, lo8], up)
        gn.send(k + 2, g.at[r, nb, lo8], g.at[r, nb, lo8], up2)
        gn.send(k + 2, g.at[r, nb], g.at[r, nb], other)
        gn.take(k + 1, g.at[r, na], up)
        gn.send(k + 2, g.at[r, na, hi8], g.at[r, na, hi8], down)
        gn.send(k + 2, g.at[r, na, hi8], g.at[r, na, hi8], down2)
        gn.send(k + 2, g.at[r, na], g.at[r, na], other)

    def narrow3(r):
        k = 3 * r
        gn.take(k + 2, g.at[r, pl.ds(0, 5)], up)

        def regroup(i, carry):
            v = g[r, :, i].astype(F32).reshape(4, 2, 8, 256)
            for hl, tile in enumerate(zip_rows(v[:, 0], v[:, 1])):
                tile = tile.reshape(32, 256).astype(BF16)
                for p in range(2):
                    at = p * 256 + hl * 128
                    gm[i, :, at : at + 128] = tile[:, p * 128 : p * 128 + 128]
            return carry

        lax.fori_loop(0, 16, regroup, 0)

    st, st2 = Copies(st_s, st_r), Copies(st2_s, st2_r)
    halves = (
        (0, lambda a, b: m4(z + b) * 4 + m4(x + a), along_x, along_z),
        (1, lambda a, b: m4(z + a) * 4 + m4(x + b), along_z, along_x),
    )
    top16, bot16 = pl.ds(0, 16), pl.ds(16, 16)
    two = (pl.ds(0, 2), pl.ds(2, 2))

    def product(h, index, a):
        lhs = jnp.concatenate([gm[index(a, b)] for b in OFFSETS], axis=0)
        cols = slice(h * 1024, h * 1024 + 1024)
        v = jnp.dot(lhs, wo[:, cols], preferred_element_type=F32)
        return v.reshape(4, 32, 1024)

    def products(r):
        for h, index, to1, to2 in halves:
            k = 12 * r + 6 * h
            v = product(h, index, 2)
            so[r, h, 0] = v[:, 0:16].astype(BF16)
            so[r, h, 1] = v[:, 16:32].astype(BF16)
            for u, q in enumerate(two):
                st.send(k + u, so.at[r, h, 0, q], ro.at[r, h, 0, q], to1(1))
                st.send(k + 2 + u, so.at[r, h, 1, q], ro.at[r, h, 1, q], to1(-1))
        for h, index, to1, to2 in halves:
            k = 12 * r + 6 * h
            v = product(h, index, 1)
            sn[r, h, 0, :, 16:32] = v[:, 16:32].astype(BF16)
            kp[r, h, 0] = v[:, 0:16]
            for u, q in enumerate(two):
                st.send(
                    k + 4 + u, sn.at[r, h, 0, q, bot16], rn.at[r, h, 0, q, bot16], to1(1)
                )
            v = product(h, index, -1)
            sn[r, h, 1, :, 0:16] = v[:, 0:16].astype(BF16)
            kp[r, h, 1] = v[:, 16:32]
            for u, q in enumerate(two):
                st.send(
                    k + 4 + u, sn.at[r, h, 1, q, top16], rn.at[r, h, 1, q, top16], to1(-1)
                )
        for h, index, to1, to2 in halves:
            km[r, h] = product(h, index, 0)

    def relay(r):
        for u, q in enumerate(two):
            qq = slice(2 * u, 2 * u + 2)
            for h, index, to1, to2 in halves:
                k = 12 * r + 6 * h
                st.take(k + u, ro.at[r, h, 0, q], to1(1))
                sn[r, h, 0, qq, 0:16] = (
                    kp[r, h, 0, qq] + ro[r, h, 0, qq].astype(F32)
                ).astype(BF16)
                st.send(k + 4 + u, sn.at[r, h, 0, q, top16], rn.at[r, h, 0, q, top16], to1(1))
                st.take(k + 2 + u, ro.at[r, h, 1, q], to1(1))
                sn[r, h, 1, qq, 16:32] = (
                    kp[r, h, 1, qq] + ro[r, h, 1, qq].astype(F32)
                ).astype(BF16)
                st.send(k + 4 + u, sn.at[r, h, 1, q, bot16], rn.at[r, h, 1, q, bot16], to1(-1))

    def second(r):
        for u, q in enumerate(two):
            for h, index, to1, to2 in halves:
                k, k2 = 12 * r + 6 * h, 6 * r + 3 * h
                st.take(k + 4 + u, rn.at[r, h, :, q], to1(1))
                for i in (2 * u, 2 * u + 1):
                    v = km[r, h, i] + rn[r, h, 0, i].astype(F32) + rn[r, h, 1, i].astype(F32)
                    if i == 0:
                        so2[r, h] = v.reshape(2, 16, 1024).astype(BF16)
                        st2.send(k2 + 0, so2.at[r, h, 0], ro2.at[r, h, 0], to2(1))
                        st2.send(k2 + 1, so2.at[r, h, 1], ro2.at[r, h, 1], to2(-1))
                        continue
                    km[r, h, i] = v
                    if i == 1:
                        sn2[r, h, 0, 16:32] = v[16:32].astype(BF16)
                        st2.send(k2 + 2, sn2.at[r, h, 0, bot16], rn2.at[r, h, 0, bot16], to2(1))
                    elif i == 2:
                        sn2[r, h, 1, 0:16] = v[0:16].astype(BF16)
                        st2.send(k2 + 2, sn2.at[r, h, 1, top16], rn2.at[r, h, 1, top16], to2(-1))

    def relay2(r):
        for h, index, to1, to2 in halves:
            k2 = 6 * r + 3 * h
            st2.take(k2 + 0, ro2.at[r, h, 0], to1(1))
            sn2[r, h, 0, 0:16] = (km[r, h, 1, 0:16] + ro2[r, h, 0].astype(F32)).astype(BF16)
            st2.send(k2 + 2, sn2.at[r, h, 0, top16], rn2.at[r, h, 0, top16], to2(1))
            st2.take(k2 + 1, ro2.at[r, h, 1], to1(1))
            sn2[r, h, 1, 16:32] = (km[r, h, 2, 16:32] + ro2[r, h, 1].astype(F32)).astype(BF16)
            st2.send(k2 + 2, sn2.at[r, h, 1, bot16], rn2.at[r, h, 1, bot16], to2(-1))

    def total_rows(r):
        for h, index, to1, to2 in halves:
            k2 = 6 * r + 3 * h
            st2.take(k2 + 2, rn2.at[r, h], to1(1))
            for j in range(8):
                sub = slice(j * 128, j * 128 + 128)
                res[h * 8 + j] = (
                    km[r, h, 3, :, sub]
                    + rn2[r, h, 0, :, sub].astype(F32)
                    + rn2[r, h, 1, :, sub].astype(F32)
                )
            for j in range(h * 8, h * 8 + 8):
                for t in range(4):
                    rows16[j, t, pl.ds(r, 8, stride=2), :] = res[j, pl.ds(t, 8, stride=4), :]
            if r == 1:
                for j in range(h * 8, h * 8 + 8):
                    for t in range(4):
                        out_ref[t, :, j * 128 : j * 128 + 128] = rows16[j, t].astype(BF16)
                cols = pl.ds(h * 1024, 1024)
                store = pltpu.make_async_copy(
                    out_ref.at[:, :, cols], out_hbm.at[:, :, cols], ld.at[9 + h]
                )
                store.start()
                stores.append(store)

    def new_rows():
        for t in range(4):
            for h in range(4):
                cols = slice(h * 128, h * 128 + 128)
                nk[t, :, cols] = kvout[0, h, 2 * t : 2 * t + 2].astype(BF16)
                nv[t, :, cols] = kvout[1, h, 2 * t : 2 * t + 2].astype(BF16)
        for i, (source, target) in enumerate(((nk, nk_hbm), (nv, nv_hbm))):
            store = pltpu.make_async_copy(source, target, ld.at[7 + i])
            store.start()
            stores.append(store)

    stores = []

    gather(0, 0, 1, 2)
    gather(1, 0, 1)
    gather(0, 3, 4)
    gather(1, 2)
    gather(0, 5)
    loads[2].wait()
    loads[3].wait()
    multiply(0, 0)
    gather(1, 3)
    gather(0, 6)
    gather(1, 4)
    ring1(0, 0)
    gather(0, 7)
    multiply(0, 1)
    gather(1, 5)
    ring2(0, 0)
    multiply(1, 0)
    gather(1, 6)
    finish(0, 0)
    ring1(0, 1)
    gather(1, 7)
    multiply(1, 1)
    ring1(1, 0)
    ring2(0, 1)
    ring1(1, 1)
    ring2(1, 0)
    finish(0, 1)
    finish(1, 0)
    ring2(1, 1)
    receive(0)
    loads[5].wait()
    loads[6].wait()
    finish(1, 1)
    attend(0, 0)
    attend(0, 1)
    spread_heads(0)
    receive(1)
    attend(1, 0)
    attend(1, 1)
    spread_heads(1)
    narrow1(0)
    new_rows()
    loads[4].wait()
    narrow2(0)
    narrow1(1)
    narrow3(0)
    products(0)
    narrow2(1)
    relay(0)
    narrow3(1)
    second(0)
    products(1)
    relay(1)
    relay2(0)
    second(1)
    total_rows(0)
    relay2(1)
    total_rows(1)
    for store in stores:
        store.wait()
    for group in (sqc, ag, ex, rs, aa, ao, gn, st, st2):
        group.drain()


def local(inputs, norm_gain, w_query, w_keyval, w_out, key_cache, value_cache, lengths, positions):
    dma = pltpu.SemaphoreType.DMA
    sm = pl.BlockSpec(memory_space=pltpu.SMEM)
    hbm = pl.BlockSpec(memory_space=pltpu.HBM)

    def b16(*shape):
        return pltpu.VMEM(shape, BF16)

    def f32(*shape):
        return pltpu.VMEM(shape, F32)

    return pl.pallas_call(
        layer_kernel,
        out_shape=(
            jax.ShapeDtypeStruct((4, 16, 2048), BF16),
            jax.ShapeDtypeStruct((4, 2, 512), BF16),
            jax.ShapeDtypeStruct((4, 2, 512), BF16),
        ),
        in_specs=[sm, sm] + [hbm] * 7,
        out_specs=(hbm, hbm, hbm),
        scratch_shapes=[
            b16(4, 16, 2048), b16(4, 2, 512), b16(4, 2, 512),
            b16(4, 16, 2048), b16(2048), b16(2048, 512), b16(64, 2048), b16(512, 2048),
            b16(2, 4096, 512), b16(2, 4096, 512),
            f32(16, 64, 128), f32(8, 128), f32(7, 8, 128), b16(2, 4, 2, 4, 16, 2048),
            f32(2, 2, 4, 8, 8, 576), f32(2, 4, 8, 8, 576), f32(2, 2, 2, 2, 8, 576),
            f32(2, 2, 8, 8, 576), b16(2, 8, 8, 576), b16(2, 16, 8, 576), f32(16, 8, 576),
            b16(2, 128, 256), b16(128, 512), b16(128, 512), f32(2, 4, 8, 128), f32(128, 4096),
            b16(2, 16, 8, 256), b16(2, 8, 16, 8, 256), b16(16, 32, 512),
            b16(2, 2, 2, 4, 16, 1024), b16(2, 2, 2, 4, 32, 1024),
            b16(2, 2, 2, 4, 16, 1024), b16(2, 2, 2, 4, 32, 1024),
            f32(2, 2, 2, 4, 16, 1024), f32(2, 2, 4, 32, 1024),
            b16(2, 2, 2, 16, 1024), b16(2, 2, 2, 32, 1024),
            b16(2, 2, 2, 16, 1024), b16(2, 2, 2, 32, 1024),
            f32(16, 32, 128), f32(16, 4, 16, 128),
            dma((11,)), dma, dma((1,)), dma, dma((60,)), dma, dma((4,)), dma, dma((12,)), dma,
            dma((2,)), dma, dma((2,)), dma, dma((6,)), dma, dma((24,)), dma, dma((12,)),
        ],
        compiler_params=pltpu.CompilerParams(
            collective_id=0, has_side_effects=True, vmem_limit_bytes=60 << 20
        ),
        name="layer",
    )(
        lengths, positions, inputs, norm_gain, w_query, w_keyval.T, w_out,
        key_cache, value_cache,
    )


def solution(mesh):
    return jax.shard_map(
        local,
        mesh=mesh,
        in_specs=(
            P(None, "wide", "narrow"),
            P("narrow"),
            P("narrow", "wide"),
            P("narrow", "wide"),
            P("wide", "narrow"),
            P(("wide", "narrow"), None, None),
            P(("wide", "narrow"), None, None),
            P(("wide", "narrow")),
            P(("wide", "narrow")),
        ),
        out_specs=(
            P(None, "wide", "narrow"),
            P(None, ("wide", "narrow"), None),
            P(None, ("wide", "narrow"), None),
        ),
        check_vma=False,
    )
```

```python
import jax
import jax.numpy as jnp
import numpy as np
from jax import lax
from jax.experimental import pallas as pl
from jax.experimental.pallas import tpu as pltpu
from jax.sharding import PartitionSpec as P

D = 16384
HQ = 64
KVH = 4
HD = 128
STEPS = 4
F32 = jnp.float32
BF16 = jnp.bfloat16
MESH = pl.DeviceIdType.MESH
NT = (((1,), (1,)), ((), ()))
CHUNK = 2048

SLOTS = (
    ((0, 0), (-1, 0), (1, 0), (2, 0)),
    ((-1, -1), (-1, 1), (1, -1), (1, 1)),
    ((0, -1), (0, 1), (2, -1), (2, 1)),
    ((0, 2), (-1, 2), (1, 2), (2, 2)),
)
WHERE = {(a % 4, b % 4): (g, s) for g, row in enumerate(SLOTS) for s, (a, b) in enumerate(row)}
OFFSETS = (2, 1, -1, 0)
FREQ = np.exp(
    -np.log(np.float32(500000.0)) * np.arange(64, dtype=np.float32) * np.float32(2.0) / np.float32(128)
)


def m4(v):
    return lax.rem(v + 8, 4)


def rcopy(src, dst, ssem, rsem, target):
    return pltpu.make_async_remote_copy(
        src_ref=src,
        dst_ref=dst,
        send_sem=ssem,
        recv_sem=rsem,
        device_id=target,
        device_id_type=MESH,
    )


class Copies:
    def __init__(self, ssem, rsem):
        self.ssem, self.rsem, self.sent = ssem, rsem, []

    def send(self, k, src, dst, target):
        c = rcopy(src, dst, self.ssem, self.rsem.at[k], target)
        c.start()
        self.sent.append(c)

    def take(self, k, dst, target):
        rcopy(dst, dst, self.ssem, self.rsem.at[k], target).wait_recv()

    def drain(self):
        for c in self.sent:
            c.wait_send()


def gather_half(cp, k0, buf, r, h, to1, to2):
    full, lo, hi = pl.ds(0, 2048), pl.ds(0, 1024), pl.ds(1024, 1024)

    def at(a, b, cols):
        g, s = WHERE[(a % 4, b % 4)]
        return buf.at[r, g, h, s, :, cols]

    def send1(k, a, b, cols, d):
        cp.send(k0 + k, at(a, b, cols), at(a - d, b, cols), to1(d))

    def send2(k, a, b, cols, d):
        cp.send(k0 + k, at(a, b, cols), at(a, b - d, cols), to2(d))

    def take(k, a, b, cols):
        cp.take(k0 + k, at(a, b, cols), to1(1))

    def spread(j, a):
        send2(3 + 3 * j, a, 0, full, 1)
        send2(4 + 3 * j, a, 0, full, -1)

    def onward(j, a):
        take(3 + 3 * j, a, -1, full)
        send2(5 + 3 * j, a, -1, lo, 1)
        take(4 + 3 * j, a, 1, full)
        send2(5 + 3 * j, a, 1, hi, -1)

    def last(j, a):
        take(5 + 3 * j, a, 2, full)

    def s0():
        send1(0, 0, 0, full, 1)
        send1(1, 0, 0, full, -1)

    def s1():
        spread(0, 0)

    def s2():
        take(0, -1, 0, full)
        send1(2, -1, 0, lo, 1)
        take(1, 1, 0, full)
        send1(2, 1, 0, hi, -1)
        spread(1, -1)
        spread(2, 1)

    def s3():
        onward(0, 0)

    def s4():
        take(2, 2, 0, full)
        spread(3, 2)

    def s5():
        onward(1, -1)
        onward(2, 1)

    def s6():
        last(0, 0)
        onward(3, 2)

    def s7():
        last(1, -1)
        last(2, 1)
        last(3, 2)

    return [s0, s1, s2, s3, s4, s5, s6, s7]


def zip_rows(a, b):
    low = lax.broadcasted_iota(jnp.int32, (1,) * (a.ndim - 2) + (8, a.shape[-1]), a.ndim - 2) < 4
    axis = a.ndim - 2
    return (
        jnp.where(low, a, pltpu.roll(b, 4, axis)),
        jnp.where(low, pltpu.roll(a, 4, axis), b),
    )


def layer_kernel(
    len_ref, pos_ref, x_hbm, gain_hbm, wq_hbm, wkv_hbm, wo_hbm, k_hbm, v_hbm,
    out_hbm, nk_hbm, nv_hbm,
    out_ref, nk, nv, xv, gain, wq, wkv, wo, kb, vb,
    xs, sq, sqr, buf, part, pair, ring_o, ring_n, qsend, qrecv, qx,
    qs, kf, vf, kvout, sc, att, g, gm,
    so, sn, ro, rn, kp, km, so2, sn2, ro2, rn2, res, rows16,
    ld, sq_s, sq_r, ag_s, ag_r, ex_s, ex_r, rs_s, rs_r, aa_s, aa_r,
    ao_s, ao_r, gn_s, gn_r, st_s, st_r, st2_s, st2_r,
):
    w = lax.axis_index("wide")
    n = lax.axis_index("narrow")
    z, x, y, c = w // 4, lax.rem(w, 4), n // 2, lax.rem(n, 2)

    def along_x(d):
        return (z * 4 + m4(x + d), n)

    def along_z(d):
        return (m4(z + d) * 4 + x, n)

    other = (w, y * 2 + (1 - c))
    up, down = (w, m4(y + 1) * 2 + c), (w, m4(y - 1) * 2 + c)
    up2, down2 = (w, m4(y + 1) * 2 + 1 - c), (w, m4(y - 1) * 2 + 1 - c)
    far, above, below = m4(y + 2), m4(y + 1), m4(y - 1)

    barrier = pltpu.get_barrier_semaphore()
    for i in range(1, 8):
        pl.semaphore_signal(
            barrier, inc=1, device_id=(w, lax.rem(n + i, 8)), device_id_type=MESH
        )
    for d in (1, -1):
        pl.semaphore_signal(barrier, inc=1, device_id=along_x(d), device_id_type=MESH)
        pl.semaphore_signal(barrier, inc=1, device_id=along_z(d), device_id_type=MESH)

    pairs = [(x_hbm, xv), (gain_hbm, gain), (wq_hbm, wq), (wkv_hbm, wkv), (wo_hbm, wo)]
    pairs += [(k_hbm, kb), (v_hbm, vb)]
    loads = [pltpu.make_async_copy(s, d, ld.at[i]) for i, (s, d) in enumerate(pairs)]
    for load in loads[:5]:
        load.start()
    qs[...] = jnp.zeros_like(qs)
    kf[...] = jnp.zeros_like(kf)
    vf[...] = jnp.zeros_like(vf)
    loads[0].wait()
    acc = jnp.zeros((64, 128), F32)
    for j in range(16):
        cols = slice(j * 128, j * 128 + 128)
        for t in range(4):
            xs[j, pl.ds(t, 16, stride=4), :] = xv[t, :, cols].astype(F32)
        acc = acc + xs[j] * xs[j]
    row = jnp.sum(acc, axis=-1, keepdims=True)
    diag = lax.broadcasted_iota(jnp.int32, (64, 128), 0) == lax.broadcasted_iota(
        jnp.int32, (64, 128), 1
    )
    flat = jnp.sum(jnp.where(diag, row, 0.0), axis=0, keepdims=True)
    sq[...] = jnp.broadcast_to(flat, (8, 128))
    pl.semaphore_wait(barrier, 11)

    sqc = Copies(sq_s, sq_r)
    for i in range(1, 8):
        sqc.send(0, sq, sqr.at[i - 1], (w, lax.rem(n + i, 8)))
    loads[5].start()
    loads[6].start()

    spot = lax.rem(lax.broadcasted_iota(jnp.int32, (8, 128), 1), 64)
    freq = jnp.zeros((8, 128), F32)
    for i in range(64):
        freq = jnp.where(spot == i, F32(FREQ[i]), freq)
    later = lax.rem(lax.broadcasted_iota(jnp.int32, (8, 128), 0), 4)
    left = lax.broadcasted_iota(jnp.int32, (8, 128), 1) < 64
    turns = []
    for r in range(2):
        angle = (later + pos_ref[r]).astype(F32) * freq
        sine = jnp.sin(angle)
        turns.append((jnp.cos(angle), jnp.where(left, -sine, sine)))

    sqc.take(0, sqr, other)
    total = sq[...]
    for i in range(7):
        total = total + sqr[i]
    column = jnp.sum(
        jnp.where(diag, jnp.broadcast_to(total[0:1], (64, 128)), 0.0), axis=-1, keepdims=True
    )
    inv = lax.rsqrt(column / D + 1e-05)
    loads[1].wait()
    for j in range(16):
        cols = slice(j * 128, j * 128 + 128)
        own = (xs[j] * inv * gain[cols].astype(F32).reshape(1, 128)).reshape(4, 2, 8, 128)
        for r, v in enumerate(zip_rows(own[:, 0], own[:, 1])):
            v = v.reshape(32, 128).astype(BF16)
            buf[r, 0, 0, 0, :, cols] = v[0:16]
            buf[r, 0, 1, 0, :, cols] = v[16:32]

    ag = Copies(ag_s, ag_r)
    ways = [
        [
            gather_half(ag, r * 30, buf, r, 0, along_x, along_z),
            gather_half(ag, r * 30 + 15, buf, r, 1, along_z, along_x),
        ]
        for r in range(2)
    ]

    def gather(r, *steps):
        for i in steps:
            ways[r][0][i]()
            ways[r][1][i]()

    ex, rs, aa = Copies(ex_s, ex_r), Copies(rs_s, rs_r), Copies(aa_s, aa_r)

    def multiply(r, m):
        lhs = buf[r, 2 * m : 2 * m + 2].reshape(256, 2048)
        q = jnp.dot(lhs, wq[...], preferred_element_type=F32)
        kv = lax.dot_general(lhs, wkv[...], NT, preferred_element_type=F32)
        for cols, v in ((slice(0, 512), q), (slice(512, 576), kv)):
            v = v.reshape(2, 2, 2, 2, 2, 8, v.shape[-1])
            for h in range(2):
                for yy in range(2):
                    a = v[:, h, :, 0, yy].reshape(4, 8, v.shape[-1])
                    b = v[:, h, :, 1, yy].reshape(4, 8, v.shape[-1])
                    for cc, tile in enumerate(zip_rows(a, b)):
                        part[r, cc, h * 2 + yy, 4 * m : 4 * m + 4, :, cols] = tile
        at = pl.ds(4 * m, 4)
        ex.send(2 * r + m, part.at[r, 1 - c, :, at], pair.at[r, :, at], other)

    def ring1(r, m):
        k = 3 * (2 * r + m)
        at, lo, hi = pl.ds(4 * m, 4), pl.ds(4 * m, 2), pl.ds(4 * m + 2, 2)
        ex.take(2 * r + m, pair.at[r, :, at], other)
        part[r, c, :, at] = part[r, c, :, at] + pair[r, :, at]
        rs.send(k + 0, part.at[r, c, far, lo], ring_o.at[r, 0, m], up)
        rs.send(k + 1, part.at[r, c, far, hi], ring_o.at[r, 1, m], down)
        rs.send(k + 2, part.at[r, c, above, hi], ring_n.at[r, 0, hi], up)
        rs.send(k + 2, part.at[r, c, below, lo], ring_n.at[r, 1, lo], down)

    def ring2(r, m):
        k = 3 * (2 * r + m)
        lo, hi = pl.ds(4 * m, 2), pl.ds(4 * m + 2, 2)
        rs.take(k + 0, ring_o.at[r, 0, m], up)
        part[r, c, above, lo] = part[r, c, above, lo] + ring_o[r, 0, m]
        rs.send(k + 2, part.at[r, c, above, lo], ring_n.at[r, 0, lo], up)
        rs.take(k + 1, ring_o.at[r, 1, m], up)
        part[r, c, below, hi] = part[r, c, below, hi] + ring_o[r, 1, m]
        rs.send(k + 2, part.at[r, c, below, hi], ring_n.at[r, 1, hi], down)

    def shift(a, b):
        return jnp.where(y < 2, b, a), jnp.where(y < 2, a, b)

    def finish(r, m):
        k = 3 * (2 * r + m)
        at = pl.ds(4 * m, 4)
        rs.take(k + 2, ring_n.at[r, :, at], up)
        qsend[r, at] = (part[r, c, y, at] + ring_n[r, 0, at] + ring_n[r, 1, at]).astype(BF16)
        for i in (2 * m, 2 * m + 1):
            for s, (a, b) in enumerate(SLOTS[i]):
                k = 4 * i + s
                if k == 0:
                    qrecv[r, 0] = qsend[r, 0]
                    continue
                dz, dx = shift(a, b)
                target = (m4(z + dz) * 4 + m4(x + dx), n)
                aa.send(r, qsend.at[r, k // 2], qrecv.at[r, k], target)

    def receive(r):
        aa.take(r, qrecv.at[r, pl.ds(1, 15)], other)
        for i in range(4):
            for s, (a, b) in enumerate(SLOTS[i]):
                k = 4 * i + s
                dz, dx = shift(a, b)
                tile = qrecv[r, k].astype(F32)
                if s % 2:
                    tile = pltpu.roll(tile, 4, 0)
                qx[m4(z - dz) * 4 + m4(x - dx)] = tile
        cos, sin = turns[r]

        def turn(v):
            return (v * cos + pltpu.roll(v, 64, v.ndim - 1) * sin).astype(BF16)

        low = lax.broadcasted_iota(jnp.int32, (1, 8, 128), 1) < 4
        for p in range(2):
            a = turn(qx[:, :, p * 256 : p * 256 + 128]).astype(F32)
            b = turn(qx[:, :, p * 256 + 128 : p * 256 + 256]).astype(F32)
            tile = jnp.where(low, a, pltpu.roll(b, 4, 1))
            for h in range(4):
                gi = h % 2
                qs[h // 2, gi * 64 + p * 32 : gi * 64 + p * 32 + 32,
                   gi * 128 : gi * 128 + 128] = (
                    tile[4 * h : 4 * h + 4].reshape(32, 128).astype(BF16)
                )
        for h in range(4):
            cols = slice(h * 128, h * 128 + 128)
            key = jnp.concatenate([qx[2 * h, :, 512:576], qx[2 * h + 1, :, 512:576]], -1)
            val = jnp.concatenate([qx[2 * h + 8, :, 512:576], qx[2 * h + 9, :, 512:576]], -1)
            key = turn(key)
            kf[0:8, cols] = key
            vf[0:8, cols] = val.astype(BF16)
            kvout[0, h, pl.ds(r, 4, stride=2), :] = key.astype(F32)[0:4]
            kvout[1, h, pl.ds(r, 4, stride=2), :] = val[0:4]

    factor = 1.0 / jnp.sqrt(F32(HD))

    def attend(r, gp):
        lane = lax.broadcasted_iota(jnp.int32, (128, 128), 1)
        step = lax.rem(lax.broadcasted_iota(jnp.int32, (128, 128), 0), 4)
        place = lax.broadcasted_iota(jnp.int32, (128, CHUNK), 1)
        q = qs[gp]
        cols = pl.ds(gp * 256, 256)
        length = len_ref[r]
        fs = lax.dot_general(q, kf[:, cols], NT, preferred_element_type=F32) * factor
        fs = jnp.where(lane <= step, fs, -jnp.inf)

        def score(j, top):
            at = pl.ds(pl.multiple_of(j * CHUNK, CHUNK), CHUNK)
            s = lax.dot_general(q, kb[r, at, cols], NT, preferred_element_type=F32) * factor
            s = jnp.where(place < length - j * CHUNK, s, -jnp.inf)
            sc[:, at] = s
            for u in range(CHUNK // 128):
                top = jnp.maximum(top, s[:, u * 128 : u * 128 + 128])
            return top

        top = lax.fori_loop(0, 4096 // CHUNK, score, fs)
        top = jnp.max(top, axis=-1, keepdims=True)
        fe = jnp.exp(fs - top)

        def expo(j, acc):
            at = pl.ds(pl.multiple_of(j * CHUNK, CHUNK), CHUNK)
            e = jnp.exp(sc[:, at] - top)
            sc[:, at] = e
            for u in range(CHUNK // 128):
                acc = acc + e[:, u * 128 : u * 128 + 128]
            return acc

        acc = lax.fori_loop(0, 4096 // CHUNK, expo, fe)
        scale = 1.0 / jnp.sum(acc, axis=-1, keepdims=True)

        def value(j, out):
            at = pl.ds(pl.multiple_of(j * CHUNK, CHUNK), CHUNK)
            p = (sc[:, at] * scale).astype(BF16)
            return out + jnp.dot(p, vb[r, at, cols], preferred_element_type=F32)

        out = jnp.dot((fe * scale).astype(BF16), vf[:, cols], preferred_element_type=F32)
        out = lax.fori_loop(0, 4096 // CHUNK, value, out)
        for gi in range(2):
            v = out[gi * 64 : gi * 64 + 64, gi * 128 : gi * 128 + 128].reshape(2, 4, 8, 128)
            h = 2 * gp + gi
            att[r, 4 * h : 4 * h + 4, :, 0:128] = v[0].astype(BF16)
            att[r, 4 * h : 4 * h + 4, :, 128:256] = v[1].astype(BF16)

    ao, gn = Copies(ao_s, ao_r), Copies(gn_s, gn_r)
    na, nb, nf = above * 2 + c, below * 2 + c, far * 2 + c
    lo8, hi8 = pl.ds(0, 8), pl.ds(8, 8)

    def spread_heads(r):
        for i in range(1, 16):
            peer = lax.rem(w + i, 16)
            ao.send(r, att.at[r, peer], g.at[r, n, w], (peer, n))
        g[r, n, w] = att[r, w]

    def narrow1(r):
        k = 3 * r
        ao.take(r, g.at[r, n, pl.ds(0, 15)], other)
        gn.send(k + 0, g.at[r, n], g.at[r, n], up)
        gn.send(k + 1, g.at[r, n], g.at[r, n], down)
        gn.send(k + 2, g.at[r, n], g.at[r, n], other)

    def narrow2(r):
        k = 3 * r
        gn.take(k + 0, g.at[r, nb], up)
        gn.send(k + 2, g.at[r, nb, lo8], g.at[r, nb, lo8], up)
        gn.send(k + 2, g.at[r, nb, lo8], g.at[r, nb, lo8], up2)
        gn.send(k + 2, g.at[r, nb], g.at[r, nb], other)
        gn.take(k + 1, g.at[r, na], up)
        gn.send(k + 2, g.at[r, na, hi8], g.at[r, na, hi8], down)
        gn.send(k + 2, g.at[r, na, hi8], g.at[r, na, hi8], down2)
        gn.send(k + 2, g.at[r, na], g.at[r, na], other)

    def narrow3(r):
        k = 3 * r
        gn.take(k + 2, g.at[r, pl.ds(0, 5)], up)

        def regroup(i, carry):
            v = g[r, :, i].astype(F32).reshape(4, 2, 8, 256)
            for hl, tile in enumerate(zip_rows(v[:, 0], v[:, 1])):
                tile = tile.reshape(32, 256).astype(BF16)
                for p in range(2):
                    at = p * 256 + hl * 128
                    gm[i, :, at : at + 128] = tile[:, p * 128 : p * 128 + 128]
            return carry

        lax.fori_loop(0, 16, regroup, 0)

    st, st2 = Copies(st_s, st_r), Copies(st2_s, st2_r)
    halves = (
        (0, lambda a, b: m4(z + b) * 4 + m4(x + a), along_x, along_z),
        (1, lambda a, b: m4(z + a) * 4 + m4(x + b), along_z, along_x),
    )
    top16, bot16 = pl.ds(0, 16), pl.ds(16, 16)
    two = (pl.ds(0, 2), pl.ds(2, 2))

    def product(h, index, a):
        lhs = jnp.concatenate([gm[index(a, b)] for b in OFFSETS], axis=0)
        cols = slice(h * 1024, h * 1024 + 1024)
        v = jnp.dot(lhs, wo[:, cols], preferred_element_type=F32)
        return v.reshape(4, 32, 1024)

    def products(r):
        for h, index, to1, to2 in halves:
            k = 12 * r + 6 * h
            v = product(h, index, 2)
            so[r, h, 0] = v[:, 0:16].astype(BF16)
            so[r, h, 1] = v[:, 16:32].astype(BF16)
            for u, q in enumerate(two):
                st.send(k + u, so.at[r, h, 0, q], ro.at[r, h, 0, q], to1(1))
                st.send(k + 2 + u, so.at[r, h, 1, q], ro.at[r, h, 1, q], to1(-1))
        for h, index, to1, to2 in halves:
            k = 12 * r + 6 * h
            v = product(h, index, 1)
            sn[r, h, 0, :, 16:32] = v[:, 16:32].astype(BF16)
            kp[r, h, 0] = v[:, 0:16]
            for u, q in enumerate(two):
                st.send(
                    k + 4 + u, sn.at[r, h, 0, q, bot16], rn.at[r, h, 0, q, bot16], to1(1)
                )
            v = product(h, index, -1)
            sn[r, h, 1, :, 0:16] = v[:, 0:16].astype(BF16)
            kp[r, h, 1] = v[:, 16:32]
            for u, q in enumerate(two):
                st.send(
                    k + 4 + u, sn.at[r, h, 1, q, top16], rn.at[r, h, 1, q, top16], to1(-1)
                )
        for h, index, to1, to2 in halves:
            km[r, h] = product(h, index, 0)

    def relay(r):
        for u, q in enumerate(two):
            qq = slice(2 * u, 2 * u + 2)
            for h, index, to1, to2 in halves:
                k = 12 * r + 6 * h
                st.take(k + u, ro.at[r, h, 0, q], to1(1))
                sn[r, h, 0, qq, 0:16] = (
                    kp[r, h, 0, qq] + ro[r, h, 0, qq].astype(F32)
                ).astype(BF16)
                st.send(k + 4 + u, sn.at[r, h, 0, q, top16], rn.at[r, h, 0, q, top16], to1(1))
                st.take(k + 2 + u, ro.at[r, h, 1, q], to1(1))
                sn[r, h, 1, qq, 16:32] = (
                    kp[r, h, 1, qq] + ro[r, h, 1, qq].astype(F32)
                ).astype(BF16)
                st.send(k + 4 + u, sn.at[r, h, 1, q, bot16], rn.at[r, h, 1, q, bot16], to1(-1))

    def second(r):
        for u, q in enumerate(two):
            for h, index, to1, to2 in halves:
                k, k2 = 12 * r + 6 * h, 6 * r + 3 * h
                st.take(k + 4 + u, rn.at[r, h, :, q], to1(1))
                for i in (2 * u, 2 * u + 1):
                    v = km[r, h, i] + rn[r, h, 0, i].astype(F32) + rn[r, h, 1, i].astype(F32)
                    if i == 0:
                        so2[r, h] = v.reshape(2, 16, 1024).astype(BF16)
                        st2.send(k2 + 0, so2.at[r, h, 0], ro2.at[r, h, 0], to2(1))
                        st2.send(k2 + 1, so2.at[r, h, 1], ro2.at[r, h, 1], to2(-1))
                        continue
                    km[r, h, i] = v
                    if i == 1:
                        sn2[r, h, 0, 16:32] = v[16:32].astype(BF16)
                        st2.send(k2 + 2, sn2.at[r, h, 0, bot16], rn2.at[r, h, 0, bot16], to2(1))
                    elif i == 2:
                        sn2[r, h, 1, 0:16] = v[0:16].astype(BF16)
                        st2.send(k2 + 2, sn2.at[r, h, 1, top16], rn2.at[r, h, 1, top16], to2(-1))

    def relay2(r):
        for h, index, to1, to2 in halves:
            k2 = 6 * r + 3 * h
            st2.take(k2 + 0, ro2.at[r, h, 0], to1(1))
            sn2[r, h, 0, 0:16] = (km[r, h, 1, 0:16] + ro2[r, h, 0].astype(F32)).astype(BF16)
            st2.send(k2 + 2, sn2.at[r, h, 0, top16], rn2.at[r, h, 0, top16], to2(1))
            st2.take(k2 + 1, ro2.at[r, h, 1], to1(1))
            sn2[r, h, 1, 16:32] = (km[r, h, 2, 16:32] + ro2[r, h, 1].astype(F32)).astype(BF16)
            st2.send(k2 + 2, sn2.at[r, h, 1, bot16], rn2.at[r, h, 1, bot16], to2(-1))

    def total_rows(r):
        for h, index, to1, to2 in halves:
            k2 = 6 * r + 3 * h
            st2.take(k2 + 2, rn2.at[r, h], to1(1))
            for j in range(8):
                sub = slice(j * 128, j * 128 + 128)
                res[h * 8 + j] = (
                    km[r, h, 3, :, sub]
                    + rn2[r, h, 0, :, sub].astype(F32)
                    + rn2[r, h, 1, :, sub].astype(F32)
                )
            for j in range(h * 8, h * 8 + 8):
                for t in range(4):
                    rows16[j, t, pl.ds(r, 8, stride=2), :] = res[j, pl.ds(t, 8, stride=4), :]
            if r == 1:
                for j in range(h * 8, h * 8 + 8):
                    for t in range(4):
                        out_ref[t, :, j * 128 : j * 128 + 128] = rows16[j, t].astype(BF16)
                cols = pl.ds(h * 1024, 1024)
                store = pltpu.make_async_copy(
                    out_ref.at[:, :, cols], out_hbm.at[:, :, cols], ld.at[9 + h]
                )
                store.start()
                stores.append(store)

    def new_rows():
        for t in range(4):
            for h in range(4):
                cols = slice(h * 128, h * 128 + 128)
                nk[t, :, cols] = kvout[0, h, 2 * t : 2 * t + 2].astype(BF16)
                nv[t, :, cols] = kvout[1, h, 2 * t : 2 * t + 2].astype(BF16)
        for i, (source, target) in enumerate(((nk, nk_hbm), (nv, nv_hbm))):
            store = pltpu.make_async_copy(source, target, ld.at[7 + i])
            store.start()
            stores.append(store)

    stores = []

    gather(0, 0, 1, 2, 3)
    gather(1, 0, 1)
    gather(0, 4, 5)
    loads[2].wait()
    loads[3].wait()
    multiply(0, 0)
    gather(0, 6)
    gather(1, 2)
    ring1(0, 0)
    gather(0, 7)
    multiply(0, 1)
    gather(1, 3)
    ring2(0, 0)
    gather(1, 4)
    ring1(0, 1)
    gather(1, 5)
    multiply(1, 0)
    finish(0, 0)
    gather(1, 6)
    ring2(0, 1)
    gather(1, 7)
    multiply(1, 1)
    ring1(1, 0)
    finish(0, 1)
    ring1(1, 1)
    ring2(1, 0)
    ring2(1, 1)
    receive(0)
    loads[5].wait()
    loads[6].wait()
    attend(0, 0)
    finish(1, 0)
    finish(1, 1)
    attend(0, 1)
    spread_heads(0)
    receive(1)
    attend(1, 0)
    narrow1(0)
    attend(1, 1)
    spread_heads(1)
    new_rows()
    loads[4].wait()
    narrow2(0)
    narrow1(1)
    narrow3(0)
    products(0)
    narrow2(1)
    relay(0)
    narrow3(1)
    products(1)
    second(0)
    relay(1)
    relay2(0)
    second(1)
    total_rows(0)
    relay2(1)
    total_rows(1)
    for store in stores:
        store.wait()
    for group in (sqc, ag, ex, rs, aa, ao, gn, st, st2):
        group.drain()


def local(inputs, norm_gain, w_query, w_keyval, w_out, key_cache, value_cache, lengths, positions):
    dma = pltpu.SemaphoreType.DMA
    sm = pl.BlockSpec(memory_space=pltpu.SMEM)
    hbm = pl.BlockSpec(memory_space=pltpu.HBM)

    def b16(*shape):
        return pltpu.VMEM(shape, BF16)

    def f32(*shape):
        return pltpu.VMEM(shape, F32)

    return pl.pallas_call(
        layer_kernel,
        out_shape=(
            jax.ShapeDtypeStruct((4, 16, 2048), BF16),
            jax.ShapeDtypeStruct((4, 2, 512), BF16),
            jax.ShapeDtypeStruct((4, 2, 512), BF16),
        ),
        in_specs=[sm, sm] + [hbm] * 7,
        out_specs=(hbm, hbm, hbm),
        scratch_shapes=[
            b16(4, 16, 2048), b16(4, 2, 512), b16(4, 2, 512),
            b16(4, 16, 2048), b16(2048), b16(2048, 512), b16(64, 2048), b16(512, 2048),
            b16(2, 4096, 512), b16(2, 4096, 512),
            f32(16, 64, 128), f32(8, 128), f32(7, 8, 128), b16(2, 4, 2, 4, 16, 2048),
            f32(2, 2, 4, 8, 8, 576), f32(2, 4, 8, 8, 576), f32(2, 2, 2, 2, 8, 576),
            f32(2, 2, 8, 8, 576), b16(2, 8, 8, 576), b16(2, 16, 8, 576), f32(16, 8, 576),
            b16(2, 128, 256), b16(128, 512), b16(128, 512), f32(2, 4, 8, 128), f32(128, 4096),
            b16(2, 16, 8, 256), b16(2, 8, 16, 8, 256), b16(16, 32, 512),
            b16(2, 2, 2, 4, 16, 1024), b16(2, 2, 2, 4, 32, 1024),
            b16(2, 2, 2, 4, 16, 1024), b16(2, 2, 2, 4, 32, 1024),
            f32(2, 2, 2, 4, 16, 1024), f32(2, 2, 4, 32, 1024),
            b16(2, 2, 2, 16, 1024), b16(2, 2, 2, 32, 1024),
            b16(2, 2, 2, 16, 1024), b16(2, 2, 2, 32, 1024),
            f32(16, 32, 128), f32(16, 4, 16, 128),
            dma((11,)), dma, dma((1,)), dma, dma((60,)), dma, dma((4,)), dma, dma((12,)), dma,
            dma((2,)), dma, dma((2,)), dma, dma((6,)), dma, dma((24,)), dma, dma((12,)),
        ],
        compiler_params=pltpu.CompilerParams(
            collective_id=0, has_side_effects=True, vmem_limit_bytes=60 << 20
        ),
        name="layer",
    )(
        lengths, positions, inputs, norm_gain, w_query, w_keyval.T, w_out,
        key_cache, value_cache,
    )


def solution(mesh):
    return jax.shard_map(
        local,
        mesh=mesh,
        in_specs=(
            P(None, "wide", "narrow"),
            P("narrow"),
            P("narrow", "wide"),
            P("narrow", "wide"),
            P("wide", "narrow"),
            P(("wide", "narrow"), None, None),
            P(("wide", "narrow"), None, None),
            P(("wide", "narrow")),
            P(("wide", "narrow")),
        ),
        out_specs=(
            P(None, "wide", "narrow"),
            P(None, ("wide", "narrow"), None),
            P(None, ("wide", "narrow"), None),
        ),
        check_vma=False,
    )
```

```python
import jax
import jax.numpy as jnp
import numpy as np
from jax import lax
from jax.experimental import pallas as pl
from jax.experimental.pallas import tpu as pltpu
from jax.sharding import PartitionSpec as P

D = 16384
HQ = 64
KVH = 4
HD = 128
STEPS = 4
F32 = jnp.float32
BF16 = jnp.bfloat16
MESH = pl.DeviceIdType.MESH
NT = (((1,), (1,)), ((), ()))
CHUNK = 2048

SLOTS = (
    ((0, 0), (-1, 0), (1, 0), (2, 0)),
    ((-1, -1), (-1, 1), (1, -1), (1, 1)),
    ((0, -1), (0, 1), (2, -1), (2, 1)),
    ((0, 2), (-1, 2), (1, 2), (2, 2)),
)
WHERE = {(a % 4, b % 4): (g, s) for g, row in enumerate(SLOTS) for s, (a, b) in enumerate(row)}
OFFSETS = (2, 1, -1, 0)
FREQ = np.exp(
    -np.log(np.float32(500000.0)) * np.arange(64, dtype=np.float32) * np.float32(2.0) / np.float32(128)
)


def m4(v):
    return lax.rem(v + 8, 4)


def rcopy(src, dst, ssem, rsem, target):
    return pltpu.make_async_remote_copy(
        src_ref=src,
        dst_ref=dst,
        send_sem=ssem,
        recv_sem=rsem,
        device_id=target,
        device_id_type=MESH,
    )


class Copies:
    def __init__(self, ssem, rsem):
        self.ssem, self.rsem, self.sent = ssem, rsem, []

    def send(self, k, src, dst, target):
        c = rcopy(src, dst, self.ssem, self.rsem.at[k], target)
        c.start()
        self.sent.append(c)

    def take(self, k, dst, target):
        rcopy(dst, dst, self.ssem, self.rsem.at[k], target).wait_recv()

    def drain(self):
        for c in self.sent:
            c.wait_send()


def gather_half(cp, k0, buf, r, h, to1, to2):
    full, lo, hi = pl.ds(0, 2048), pl.ds(0, 1024), pl.ds(1024, 1024)

    def at(a, b, cols):
        g, s = WHERE[(a % 4, b % 4)]
        return buf.at[r, g, h, s, :, cols]

    def send1(k, a, b, cols, d):
        cp.send(k0 + k, at(a, b, cols), at(a - d, b, cols), to1(d))

    def send2(k, a, b, cols, d):
        cp.send(k0 + k, at(a, b, cols), at(a, b - d, cols), to2(d))

    def take(k, a, b, cols):
        cp.take(k0 + k, at(a, b, cols), to1(1))

    def spread(j, a):
        send2(3 + 3 * j, a, 0, full, 1)
        send2(4 + 3 * j, a, 0, full, -1)

    def onward(j, a):
        take(3 + 3 * j, a, -1, full)
        send2(5 + 3 * j, a, -1, lo, 1)
        take(4 + 3 * j, a, 1, full)
        send2(5 + 3 * j, a, 1, hi, -1)

    def last(j, a):
        take(5 + 3 * j, a, 2, full)

    def s0():
        send1(0, 0, 0, full, 1)
        send1(1, 0, 0, full, -1)

    def s1():
        spread(0, 0)

    def s2():
        take(0, -1, 0, full)
        send1(2, -1, 0, lo, 1)
        take(1, 1, 0, full)
        send1(2, 1, 0, hi, -1)
        spread(1, -1)
        spread(2, 1)

    def s3():
        onward(0, 0)

    def s4():
        take(2, 2, 0, full)
        spread(3, 2)

    def s5():
        onward(1, -1)
        onward(2, 1)

    def s6():
        last(0, 0)
        onward(3, 2)

    def s7():
        last(1, -1)
        last(2, 1)
        last(3, 2)

    return [s0, s1, s2, s3, s4, s5, s6, s7]


def zip_rows(a, b):
    low = lax.broadcasted_iota(jnp.int32, (1,) * (a.ndim - 2) + (8, a.shape[-1]), a.ndim - 2) < 4
    axis = a.ndim - 2
    return (
        jnp.where(low, a, pltpu.roll(b, 4, axis)),
        jnp.where(low, pltpu.roll(a, 4, axis), b),
    )


def layer_kernel(
    len_ref, pos_ref, x_hbm, gain_hbm, wq_hbm, wkv_hbm, wo_hbm, k_hbm, v_hbm,
    out_hbm, new_hbm,
    out_ref, new, xv, gain, wq, wkv, wo, kb, vb,
    xs, sq, sqr, buf, part, pair, ring_o, ring_n, qsend, qrecv, qx,
    qs, kf, vf, kvout, sc, att, g, gm,
    so, sn, ro, rn, kp, km, so2, sn2, ro2, rn2, res, rows16,
    ld, sq_s, sq_r, ag_s, ag_r, ex_s, ex_r, rs_s, rs_r, aa_s, aa_r,
    ao_s, ao_r, gn_s, gn_r, st_s, st_r, st2_s, st2_r,
):
    w = lax.axis_index("wide")
    n = lax.axis_index("narrow")
    z, x, y, c = w // 4, lax.rem(w, 4), n // 2, lax.rem(n, 2)

    def along_x(d):
        return (z * 4 + m4(x + d), n)

    def along_z(d):
        return (m4(z + d) * 4 + x, n)

    other = (w, y * 2 + (1 - c))
    up, down = (w, m4(y + 1) * 2 + c), (w, m4(y - 1) * 2 + c)
    up2, down2 = (w, m4(y + 1) * 2 + 1 - c), (w, m4(y - 1) * 2 + 1 - c)
    far, above, below = m4(y + 2), m4(y + 1), m4(y - 1)

    barrier = pltpu.get_barrier_semaphore()
    for i in range(1, 8):
        pl.semaphore_signal(
            barrier, inc=1, device_id=(w, lax.rem(n + i, 8)), device_id_type=MESH
        )
    for d in (1, -1):
        pl.semaphore_signal(barrier, inc=1, device_id=along_x(d), device_id_type=MESH)
        pl.semaphore_signal(barrier, inc=1, device_id=along_z(d), device_id_type=MESH)

    pairs = [(x_hbm, xv), (gain_hbm, gain), (wq_hbm, wq), (wkv_hbm, wkv), (wo_hbm, wo)]
    pairs += [(k_hbm, kb), (v_hbm, vb)]
    loads = [pltpu.make_async_copy(s, d, ld.at[i]) for i, (s, d) in enumerate(pairs)]
    for load in loads[:5]:
        load.start()
    qs[...] = jnp.zeros_like(qs)
    kf[...] = jnp.zeros_like(kf)
    vf[...] = jnp.zeros_like(vf)
    loads[0].wait()
    acc = jnp.zeros((64, 128), F32)
    for j in range(16):
        cols = slice(j * 128, j * 128 + 128)
        for t in range(4):
            xs[j, pl.ds(t, 16, stride=4), :] = xv[t, :, cols].astype(F32)
        acc = acc + xs[j] * xs[j]
    row = jnp.sum(acc, axis=-1, keepdims=True)
    diag = lax.broadcasted_iota(jnp.int32, (64, 128), 0) == lax.broadcasted_iota(
        jnp.int32, (64, 128), 1
    )
    flat = jnp.sum(jnp.where(diag, row, 0.0), axis=0, keepdims=True)
    sq[...] = jnp.broadcast_to(flat, (8, 128))
    pl.semaphore_wait(barrier, 11)

    sqc = Copies(sq_s, sq_r)
    for i in range(1, 8):
        sqc.send(0, sq, sqr.at[i - 1], (w, lax.rem(n + i, 8)))
    loads[5].start()
    loads[6].start()

    spot = lax.rem(lax.broadcasted_iota(jnp.int32, (8, 128), 1), 64)
    freq = jnp.zeros((8, 128), F32)
    for i in range(64):
        freq = jnp.where(spot == i, F32(FREQ[i]), freq)
    later = lax.rem(lax.broadcasted_iota(jnp.int32, (8, 128), 0), 4)
    left = lax.broadcasted_iota(jnp.int32, (8, 128), 1) < 64
    turns = []
    for r in range(2):
        angle = (later + pos_ref[r]).astype(F32) * freq
        sine = jnp.sin(angle)
        turns.append((jnp.cos(angle), jnp.where(left, -sine, sine)))

    sqc.take(0, sqr, other)
    total = sq[...]
    for i in range(7):
        total = total + sqr[i]
    column = jnp.sum(
        jnp.where(diag, jnp.broadcast_to(total[0:1], (64, 128)), 0.0), axis=-1, keepdims=True
    )
    inv = lax.rsqrt(column / D + 1e-05)
    loads[1].wait()
    for j in range(16):
        cols = slice(j * 128, j * 128 + 128)
        own = (xs[j] * inv * gain[cols].astype(F32).reshape(1, 128)).reshape(4, 2, 8, 128)
        for r, v in enumerate(zip_rows(own[:, 0], own[:, 1])):
            v = v.reshape(32, 128).astype(BF16)
            buf[r, 0, 0, 0, :, cols] = v[0:16]
            buf[r, 0, 1, 0, :, cols] = v[16:32]

    ag = Copies(ag_s, ag_r)
    ways = [
        [
            gather_half(ag, r * 30, buf, r, 0, along_x, along_z),
            gather_half(ag, r * 30 + 15, buf, r, 1, along_z, along_x),
        ]
        for r in range(2)
    ]

    def gather(r, *steps):
        for i in steps:
            ways[r][0][i]()
            ways[r][1][i]()

    ex, rs, aa = Copies(ex_s, ex_r), Copies(rs_s, rs_r), Copies(aa_s, aa_r)

    def multiply(r, m):
        lhs = buf[r, 2 * m : 2 * m + 2].reshape(256, 2048)
        q = jnp.dot(lhs, wq[...], preferred_element_type=F32)
        kv = lax.dot_general(lhs, wkv[...], NT, preferred_element_type=F32)
        for cols, v in ((slice(0, 512), q), (slice(512, 576), kv)):
            v = v.reshape(2, 2, 2, 2, 2, 8, v.shape[-1])
            for h in range(2):
                for yy in range(2):
                    a = v[:, h, :, 0, yy].reshape(4, 8, v.shape[-1])
                    b = v[:, h, :, 1, yy].reshape(4, 8, v.shape[-1])
                    for cc, tile in enumerate(zip_rows(a, b)):
                        part[r, cc, h * 2 + yy, 4 * m : 4 * m + 4, :, cols] = tile
        at = pl.ds(4 * m, 4)
        ex.send(2 * r + m, part.at[r, 1 - c, :, at], pair.at[r, :, at], other)

    def ring1(r, m):
        k = 3 * (2 * r + m)
        at, lo, hi = pl.ds(4 * m, 4), pl.ds(4 * m, 2), pl.ds(4 * m + 2, 2)
        ex.take(2 * r + m, pair.at[r, :, at], other)
        part[r, c, :, at] = part[r, c, :, at] + pair[r, :, at]
        rs.send(k + 0, part.at[r, c, far, lo], ring_o.at[r, 0, m], up)
        rs.send(k + 1, part.at[r, c, far, hi], ring_o.at[r, 1, m], down)
        rs.send(k + 2, part.at[r, c, above, hi], ring_n.at[r, 0, hi], up)
        rs.send(k + 2, part.at[r, c, below, lo], ring_n.at[r, 1, lo], down)

    def ring2(r, m):
        k = 3 * (2 * r + m)
        lo, hi = pl.ds(4 * m, 2), pl.ds(4 * m + 2, 2)
        rs.take(k + 0, ring_o.at[r, 0, m], up)
        part[r, c, above, lo] = part[r, c, above, lo] + ring_o[r, 0, m]
        rs.send(k + 2, part.at[r, c, above, lo], ring_n.at[r, 0, lo], up)
        rs.take(k + 1, ring_o.at[r, 1, m], up)
        part[r, c, below, hi] = part[r, c, below, hi] + ring_o[r, 1, m]
        rs.send(k + 2, part.at[r, c, below, hi], ring_n.at[r, 1, hi], down)

    def shift(a, b):
        return jnp.where(y < 2, b, a), jnp.where(y < 2, a, b)

    def finish(r, m):
        k = 3 * (2 * r + m)
        at = pl.ds(4 * m, 4)
        rs.take(k + 2, ring_n.at[r, :, at], up)
        qsend[r, at] = (part[r, c, y, at] + ring_n[r, 0, at] + ring_n[r, 1, at]).astype(BF16)
        for i in (2 * m, 2 * m + 1):
            for s, (a, b) in enumerate(SLOTS[i]):
                k = 4 * i + s
                if k == 0:
                    qrecv[r, 0] = qsend[r, 0]
                    continue
                dz, dx = shift(a, b)
                target = (m4(z + dz) * 4 + m4(x + dx), n)
                aa.send(r, qsend.at[r, k // 2], qrecv.at[r, k], target)

    def receive(r):
        aa.take(r, qrecv.at[r, pl.ds(1, 15)], other)
        for i in range(4):
            for s, (a, b) in enumerate(SLOTS[i]):
                k = 4 * i + s
                dz, dx = shift(a, b)
                tile = qrecv[r, k].astype(F32)
                if s % 2:
                    tile = pltpu.roll(tile, 4, 0)
                qx[m4(z - dz) * 4 + m4(x - dx)] = tile
        cos, sin = turns[r]

        def turn(v):
            return (v * cos + pltpu.roll(v, 64, v.ndim - 1) * sin).astype(BF16)

        low = lax.broadcasted_iota(jnp.int32, (1, 8, 128), 1) < 4
        for p in range(2):
            a = turn(qx[:, :, p * 256 : p * 256 + 128]).astype(F32)
            b = turn(qx[:, :, p * 256 + 128 : p * 256 + 256]).astype(F32)
            tile = jnp.where(low, a, pltpu.roll(b, 4, 1))
            for h in range(4):
                gi = h % 2
                qs[h // 2, gi * 64 + p * 32 : gi * 64 + p * 32 + 32,
                   gi * 128 : gi * 128 + 128] = (
                    tile[4 * h : 4 * h + 4].reshape(32, 128).astype(BF16)
                )
        for h in range(4):
            cols = slice(h * 128, h * 128 + 128)
            key = jnp.concatenate([qx[2 * h, :, 512:576], qx[2 * h + 1, :, 512:576]], -1)
            val = jnp.concatenate([qx[2 * h + 8, :, 512:576], qx[2 * h + 9, :, 512:576]], -1)
            key = turn(key)
            kf[0:8, cols] = key
            vf[0:8, cols] = val.astype(BF16)
            kvout[0, h, pl.ds(r, 4, stride=2), :] = key.astype(F32)[0:4]
            kvout[1, h, pl.ds(r, 4, stride=2), :] = val[0:4]

    factor = 1.0 / jnp.sqrt(F32(HD))

    def attend(r, gp):
        lane = lax.broadcasted_iota(jnp.int32, (128, 128), 1)
        step = lax.rem(lax.broadcasted_iota(jnp.int32, (128, 128), 0), 4)
        place = lax.broadcasted_iota(jnp.int32, (128, CHUNK), 1)
        q = qs[gp]
        cols = pl.ds(gp * 256, 256)
        length = len_ref[r]
        fs = lax.dot_general(q, kf[:, cols], NT, preferred_element_type=F32) * factor
        fs = jnp.where(lane <= step, fs, -jnp.inf)

        def score(j, top):
            at = pl.ds(pl.multiple_of(j * CHUNK, CHUNK), CHUNK)
            s = lax.dot_general(q, kb[r, at, cols], NT, preferred_element_type=F32) * factor
            s = jnp.where(place < length - j * CHUNK, s, -jnp.inf)
            sc[:, at] = s
            for u in range(CHUNK // 128):
                top = jnp.maximum(top, s[:, u * 128 : u * 128 + 128])
            return top

        top = lax.fori_loop(0, 4096 // CHUNK, score, fs)
        top = jnp.max(top, axis=-1, keepdims=True)
        fe = jnp.exp(fs - top)

        def expo(j, acc):
            at = pl.ds(pl.multiple_of(j * CHUNK, CHUNK), CHUNK)
            e = jnp.exp(sc[:, at] - top)
            sc[:, at] = e
            for u in range(CHUNK // 128):
                acc = acc + e[:, u * 128 : u * 128 + 128]
            return acc

        acc = lax.fori_loop(0, 4096 // CHUNK, expo, fe)
        scale = 1.0 / jnp.sum(acc, axis=-1, keepdims=True)

        def value(j, out):
            at = pl.ds(pl.multiple_of(j * CHUNK, CHUNK), CHUNK)
            p = (sc[:, at] * scale).astype(BF16)
            return out + jnp.dot(p, vb[r, at, cols], preferred_element_type=F32)

        out = jnp.dot((fe * scale).astype(BF16), vf[:, cols], preferred_element_type=F32)
        out = lax.fori_loop(0, 4096 // CHUNK, value, out)
        for gi in range(2):
            v = out[gi * 64 : gi * 64 + 64, gi * 128 : gi * 128 + 128].reshape(2, 4, 8, 128)
            h = 2 * gp + gi
            att[r, 4 * h : 4 * h + 4, :, 0:128] = v[0].astype(BF16)
            att[r, 4 * h : 4 * h + 4, :, 128:256] = v[1].astype(BF16)

    ao, gn = Copies(ao_s, ao_r), Copies(gn_s, gn_r)
    na, nb, nf = above * 2 + c, below * 2 + c, far * 2 + c
    lo8, hi8 = pl.ds(0, 8), pl.ds(8, 8)

    def spread_heads(r):
        for i in range(1, 16):
            peer = lax.rem(w + i, 16)
            ao.send(r, att.at[r, peer], g.at[r, n, w], (peer, n))
        g[r, n, w] = att[r, w]

    def narrow1(r):
        k = 3 * r
        ao.take(r, g.at[r, n, pl.ds(0, 15)], other)
        gn.send(k + 0, g.at[r, n], g.at[r, n], up)
        gn.send(k + 1, g.at[r, n], g.at[r, n], down)
        gn.send(k + 2, g.at[r, n], g.at[r, n], other)

    def narrow2(r):
        k = 3 * r
        gn.take(k + 0, g.at[r, nb], up)
        gn.send(k + 2, g.at[r, nb, lo8], g.at[r, nb, lo8], up)
        gn.send(k + 2, g.at[r, nb, lo8], g.at[r, nb, lo8], up2)
        gn.send(k + 2, g.at[r, nb], g.at[r, nb], other)
        gn.take(k + 1, g.at[r, na], up)
        gn.send(k + 2, g.at[r, na, hi8], g.at[r, na, hi8], down)
        gn.send(k + 2, g.at[r, na, hi8], g.at[r, na, hi8], down2)
        gn.send(k + 2, g.at[r, na], g.at[r, na], other)

    def narrow3(r):
        k = 3 * r
        gn.take(k + 2, g.at[r, pl.ds(0, 5)], up)

        def regroup(i, carry):
            v = g[r, :, i].astype(F32).reshape(4, 2, 8, 256)
            for hl, tile in enumerate(zip_rows(v[:, 0], v[:, 1])):
                tile = tile.reshape(32, 256).astype(BF16)
                for p in range(2):
                    at = p * 256 + hl * 128
                    gm[i, :, at : at + 128] = tile[:, p * 128 : p * 128 + 128]
            return carry

        lax.fori_loop(0, 16, regroup, 0)

    st, st2 = Copies(st_s, st_r), Copies(st2_s, st2_r)
    halves = (
        (0, lambda a, b: m4(z + b) * 4 + m4(x + a), along_x, along_z),
        (1, lambda a, b: m4(z + a) * 4 + m4(x + b), along_z, along_x),
    )
    top16, bot16 = pl.ds(0, 16), pl.ds(16, 16)
    two = (pl.ds(0, 2), pl.ds(2, 2))

    def product(h, index, a):
        lhs = jnp.concatenate([gm[index(a, b)] for b in OFFSETS], axis=0)
        cols = slice(h * 1024, h * 1024 + 1024)
        v = jnp.dot(lhs, wo[:, cols], preferred_element_type=F32)
        return v.reshape(4, 32, 1024)

    def products(r):
        for h, index, to1, to2 in halves:
            k = 12 * r + 6 * h
            v = product(h, index, 2)
            so[r, h, 0] = v[:, 0:16].astype(BF16)
            so[r, h, 1] = v[:, 16:32].astype(BF16)
            for u, q in enumerate(two):
                st.send(k + u, so.at[r, h, 0, q], ro.at[r, h, 0, q], to1(1))
                st.send(k + 2 + u, so.at[r, h, 1, q], ro.at[r, h, 1, q], to1(-1))
        for h, index, to1, to2 in halves:
            k = 12 * r + 6 * h
            v = product(h, index, 1)
            sn[r, h, 0, :, 16:32] = v[:, 16:32].astype(BF16)
            kp[r, h, 0] = v[:, 0:16]
            for u, q in enumerate(two):
                st.send(
                    k + 4 + u, sn.at[r, h, 0, q, bot16], rn.at[r, h, 0, q, bot16], to1(1)
                )
            v = product(h, index, -1)
            sn[r, h, 1, :, 0:16] = v[:, 0:16].astype(BF16)
            kp[r, h, 1] = v[:, 16:32]
            for u, q in enumerate(two):
                st.send(
                    k + 4 + u, sn.at[r, h, 1, q, top16], rn.at[r, h, 1, q, top16], to1(-1)
                )
        for h, index, to1, to2 in halves:
            km[r, h] = product(h, index, 0)

    def relay(r):
        for u, q in enumerate(two):
            qq = slice(2 * u, 2 * u + 2)
            for h, index, to1, to2 in halves:
                k = 12 * r + 6 * h
                st.take(k + u, ro.at[r, h, 0, q], to1(1))
                sn[r, h, 0, qq, 0:16] = (
                    kp[r, h, 0, qq] + ro[r, h, 0, qq].astype(F32)
                ).astype(BF16)
                st.send(k + 4 + u, sn.at[r, h, 0, q, top16], rn.at[r, h, 0, q, top16], to1(1))
                st.take(k + 2 + u, ro.at[r, h, 1, q], to1(1))
                sn[r, h, 1, qq, 16:32] = (
                    kp[r, h, 1, qq] + ro[r, h, 1, qq].astype(F32)
                ).astype(BF16)
                st.send(k + 4 + u, sn.at[r, h, 1, q, bot16], rn.at[r, h, 1, q, bot16], to1(-1))

    def second(r):
        for u, q in enumerate(two):
            for h, index, to1, to2 in halves:
                k, k2 = 12 * r + 6 * h, 6 * r + 3 * h
                st.take(k + 4 + u, rn.at[r, h, :, q], to1(1))
                for i in (2 * u, 2 * u + 1):
                    v = km[r, h, i] + rn[r, h, 0, i].astype(F32) + rn[r, h, 1, i].astype(F32)
                    if i == 0:
                        so2[r, h] = v.reshape(2, 16, 1024).astype(BF16)
                        st2.send(k2 + 0, so2.at[r, h, 0], ro2.at[r, h, 0], to2(1))
                        st2.send(k2 + 1, so2.at[r, h, 1], ro2.at[r, h, 1], to2(-1))
                        continue
                    km[r, h, i] = v
                    if i == 1:
                        sn2[r, h, 0, 16:32] = v[16:32].astype(BF16)
                        st2.send(k2 + 2, sn2.at[r, h, 0, bot16], rn2.at[r, h, 0, bot16], to2(1))
                    elif i == 2:
                        sn2[r, h, 1, 0:16] = v[0:16].astype(BF16)
                        st2.send(k2 + 2, sn2.at[r, h, 1, top16], rn2.at[r, h, 1, top16], to2(-1))

    def relay2(r):
        for h, index, to1, to2 in halves:
            k2 = 6 * r + 3 * h
            st2.take(k2 + 0, ro2.at[r, h, 0], to1(1))
            sn2[r, h, 0, 0:16] = (km[r, h, 1, 0:16] + ro2[r, h, 0].astype(F32)).astype(BF16)
            st2.send(k2 + 2, sn2.at[r, h, 0, top16], rn2.at[r, h, 0, top16], to2(1))
            st2.take(k2 + 1, ro2.at[r, h, 1], to1(1))
            sn2[r, h, 1, 16:32] = (km[r, h, 2, 16:32] + ro2[r, h, 1].astype(F32)).astype(BF16)
            st2.send(k2 + 2, sn2.at[r, h, 1, bot16], rn2.at[r, h, 1, bot16], to2(-1))

    def total_rows(r):
        for h, index, to1, to2 in halves:
            k2 = 6 * r + 3 * h
            st2.take(k2 + 2, rn2.at[r, h], to1(1))
            for j in range(8):
                sub = slice(j * 128, j * 128 + 128)
                res[h * 8 + j] = (
                    km[r, h, 3, :, sub]
                    + rn2[r, h, 0, :, sub].astype(F32)
                    + rn2[r, h, 1, :, sub].astype(F32)
                )
            for j in range(h * 8, h * 8 + 8):
                for t in range(4):
                    rows16[j, t, pl.ds(r, 8, stride=2), :] = res[j, pl.ds(t, 8, stride=4), :]
            if r == 1:
                for j in range(h * 8, h * 8 + 8):
                    for t in range(4):
                        out_ref[t, :, j * 128 : j * 128 + 128] = rows16[j, t].astype(BF16)
                cols = pl.ds(h * 1024, 1024)
                store = pltpu.make_async_copy(
                    out_ref.at[:, :, cols], out_hbm.at[:, :, cols], ld.at[8 + h]
                )
                store.start()
                stores.append(store)

    def new_rows():
        for t in range(4):
            for h in range(4):
                cols = slice(h * 128, h * 128 + 128)
                for i in range(2):
                    new[i, t, :, cols] = kvout[i, h, 2 * t : 2 * t + 2].astype(BF16)
        store = pltpu.make_async_copy(new, new_hbm, ld.at[7])
        store.start()
        stores.append(store)

    stores = []

    gather(0, 0, 1, 2, 3)
    gather(1, 0, 1)
    gather(0, 4, 5)
    loads[2].wait()
    loads[3].wait()
    multiply(0, 0)
    gather(0, 6)
    gather(1, 2)
    ring1(0, 0)
    gather(0, 7)
    multiply(0, 1)
    gather(1, 3)
    ring2(0, 0)
    gather(1, 4)
    ring1(0, 1)
    gather(1, 5)
    multiply(1, 0)
    finish(0, 0)
    gather(1, 6)
    ring2(0, 1)
    gather(1, 7)
    multiply(1, 1)
    ring1(1, 0)
    finish(0, 1)
    ring1(1, 1)
    ring2(1, 0)
    ring2(1, 1)
    receive(0)
    loads[5].wait()
    loads[6].wait()
    attend(0, 0)
    finish(1, 0)
    finish(1, 1)
    attend(0, 1)
    spread_heads(0)
    receive(1)
    attend(1, 0)
    narrow1(0)
    attend(1, 1)
    spread_heads(1)
    new_rows()
    loads[4].wait()
    narrow2(0)
    narrow1(1)
    narrow3(0)
    products(0)
    narrow2(1)
    relay(0)
    narrow3(1)
    products(1)
    second(0)
    relay(1)
    relay2(0)
    second(1)
    total_rows(0)
    relay2(1)
    total_rows(1)
    for store in stores:
        store.wait()
    for group in (sqc, ag, ex, rs, aa, ao, gn, st, st2):
        group.drain()


def local(inputs, norm_gain, w_query, w_keyval, w_out, key_cache, value_cache, lengths, positions):
    dma = pltpu.SemaphoreType.DMA
    sm = pl.BlockSpec(memory_space=pltpu.SMEM)
    hbm = pl.BlockSpec(memory_space=pltpu.HBM)

    def b16(*shape):
        return pltpu.VMEM(shape, BF16)

    def f32(*shape):
        return pltpu.VMEM(shape, F32)

    attended, new = pl.pallas_call(
        layer_kernel,
        out_shape=(
            jax.ShapeDtypeStruct((4, 16, 2048), BF16),
            jax.ShapeDtypeStruct((2, 4, 2, 512), BF16),
        ),
        in_specs=[sm, sm] + [hbm] * 7,
        out_specs=(hbm, hbm),
        scratch_shapes=[
            b16(4, 16, 2048), b16(2, 4, 2, 512),
            b16(4, 16, 2048), b16(2048), b16(2048, 512), b16(64, 2048), b16(512, 2048),
            b16(2, 4096, 512), b16(2, 4096, 512),
            f32(16, 64, 128), f32(8, 128), f32(7, 8, 128), b16(2, 4, 2, 4, 16, 2048),
            f32(2, 2, 4, 8, 8, 576), f32(2, 4, 8, 8, 576), f32(2, 2, 2, 2, 8, 576),
            f32(2, 2, 8, 8, 576), b16(2, 8, 8, 576), b16(2, 16, 8, 576), f32(16, 8, 576),
            b16(2, 128, 256), b16(128, 512), b16(128, 512), f32(2, 4, 8, 128), f32(128, 4096),
            b16(2, 16, 8, 256), b16(2, 8, 16, 8, 256), b16(16, 32, 512),
            b16(2, 2, 2, 4, 16, 1024), b16(2, 2, 2, 4, 32, 1024),
            b16(2, 2, 2, 4, 16, 1024), b16(2, 2, 2, 4, 32, 1024),
            f32(2, 2, 2, 4, 16, 1024), f32(2, 2, 4, 32, 1024),
            b16(2, 2, 2, 16, 1024), b16(2, 2, 2, 32, 1024),
            b16(2, 2, 2, 16, 1024), b16(2, 2, 2, 32, 1024),
            f32(16, 32, 128), f32(16, 4, 16, 128),
            dma((10,)), dma, dma((1,)), dma, dma((60,)), dma, dma((4,)), dma, dma((12,)), dma,
            dma((2,)), dma, dma((2,)), dma, dma((6,)), dma, dma((24,)), dma, dma((12,)),
        ],
        compiler_params=pltpu.CompilerParams(
            collective_id=0, has_side_effects=True, vmem_limit_bytes=60 << 20
        ),
        name="layer",
    )(
        lengths, positions, inputs, norm_gain, w_query, w_keyval.T, w_out,
        key_cache, value_cache,
    )
    return attended, new[0], new[1]


def solution(mesh):
    return jax.shard_map(
        local,
        mesh=mesh,
        in_specs=(
            P(None, "wide", "narrow"),
            P("narrow"),
            P("narrow", "wide"),
            P("narrow", "wide"),
            P("wide", "narrow"),
            P(("wide", "narrow"), None, None),
            P(("wide", "narrow"), None, None),
            P(("wide", "narrow")),
            P(("wide", "narrow")),
        ),
        out_specs=(
            P(None, "wide", "narrow"),
            P(None, ("wide", "narrow"), None),
            P(None, ("wide", "narrow"), None),
        ),
        check_vma=False,
    )
```
